512 devices in a mesh: seq: 64 (over z, x, y_lo), tp: 8 (over y_hi, core).
Axes of the slice: x: 4, y: 8 (y_hi: 4, y_lo: 2; y = y_hi * 2 + y_lo), z: 8, core: 2. Of those that a mesh axis runs over, the one named last changes fastest.
Arguments:
- tokens: bfloat16 [16384, 3200], P('seq'), may hold values from -8 to 8
- norm_gain: float32 [3200], replicated, may hold values from 0.5 to 1.5
- qkv_weight: bfloat16 [3200, 3, 2048], P('seq', None, 'tp'), may hold values from -1 to 1
- q_gain: float32 [2048], P('tp'), may hold values from 0.5 to 5, as said below
- k_gain: float32 [2048], P('tp'), may hold values from 0.5 to 5, as said below
- out_weight: bfloat16 [2048, 3200], P('tp', 'seq'), may hold values from -0.125 to 0.125
- layer_scale: float32 [3200], P('tp'), may hold values from 0.5 to 2
- segment_ids: int32 [16384], replicated, may hold values from 0 to 63, never falling along the last dimension, each value on 1 to 512 neighbouring positions
Outputs:
- mixed: bfloat16 [16384, 3200], P('seq', 'tp')
The draws below stay inside these ranges and needn't reach their ends.
Inputs may be any that keep to these rules, and one draw needn't show every extreme that they name: `segment_ids`: image numbers never fall along the row; each image has 1 to 512 patches, one exactly 512. `q_gain`: positive gains. `k_gain`: positive gains.
All inputs are finite; a program needn't handle non-finite values.
Results may differ from the reference program's by a relative error of at most 0.0078.
Values may be sent and summed in bfloat16 or wider, within the bound.
A program may use at most 64 MiB of HBM per device.

```python
import math
import jax
import jax.numpy as jnp
import numpy as np
from jax import lax

D = 3200
HEAD_DIM = 128
HEADS = 16
TOK_DEV = 256
TOKENS = 16384
IMAGES = 64
N_SEQ = 64


def draw_tokens(key, part):
    parts = jax.random.split(jax.random.fold_in(key, 11), 1)
    base = jax.random.normal(parts[0], (TOKENS, D), jnp.float32)
    return jnp.clip(base, -6.0, 6.0).astype(jnp.bfloat16)


def draw_qkv_weight(key, part):
    width = HEADS * HEAD_DIM
    parts = jax.random.split(jax.random.fold_in(key, 23), 1)
    base = jax.random.normal(parts[0], (D, 3, width), jnp.float32)
    head = (jnp.arange(width) // HEAD_DIM).astype(jnp.float32)
    growth = 3.0
    scale = jnp.power(growth, head / (HEADS - 1)) / math.sqrt(D)
    return jnp.clip(base * scale[None, None, :], -1.0, 1.0).astype(jnp.bfloat16)


def gain_draw(key, salt):
    upper = 2.0
    level = jax.random.uniform(jax.random.fold_in(key, salt), (HEADS * HEAD_DIM,), jnp.float32, math.log(0.5), math.log(upper))
    return jnp.exp(level)


def draw_q_gain(key, part):
    return gain_draw(key, 37)


def draw_k_gain(key, part):
    return gain_draw(key, 41)


def shard_levels(key, extent, cuts, low, high):
    loudness = 1.0
    for dim, blocks in cuts:
        steps = jax.random.uniform(jax.random.fold_in(jax.random.fold_in(key, 6), dim), (blocks,), jnp.float32, low / len(cuts), high / len(cuts))
        loudness = loudness * jnp.repeat(jnp.exp(steps), extent[dim] // blocks).reshape((-1,) + (1,) * (len(extent) - 1 - dim))
    return loudness


def profile(count, total, limit, slope):
    weights = [(1 << 20) // math.isqrt(rank ** slope) + 1 for rank in range(2, count + 1)]
    rest, given = total - limit - (count - 1), [1] * (count - 1)
    while rest > 0:
        candidates = [i for i in range(count - 1) if given[i] < limit]
        whole, remaining = sum([weights[i] for i in candidates]), rest
        for i in candidates:
            extra = min(limit - given[i], max(1, remaining * weights[i] // whole), rest)
            given[i] = given[i] + extra
            rest = rest - extra
    return np.array([limit] + given)


def ragged(key, amount, total, reach, skew):
    if amount == 2:
        one = jax.random.randint(key, (), max(1, total - reach), min(reach, total - 1) + 1)
        return jnp.stack([one, total - one])
    sizes = jnp.asarray(profile(amount, total, reach, skew), jnp.int32)
    twos = (amount - 1) // 2
    source_of, sink = sizes[1:1 + 2 * twos:2], sizes[2:2 + 2 * twos:2]
    room = jnp.minimum(source_of - 1, reach - sink)
    shifted = jax.random.randint(jax.random.fold_in(key, 1), (twos,), 0, 1 << 20) % (room + 1)
    sizes = sizes.at[1:1 + 2 * twos:2].set(source_of - shifted).at[2:2 + 2 * twos:2].set(sink + shifted)
    return sizes[jax.random.permutation(jax.random.fold_in(key, 2), amount)]


def bell_draw(key, dims, scale, reach, cuts=(), held_as=jnp.bfloat16):
    array = scale * jax.random.normal(key, dims, jnp.float32)
    if cuts:
        array = array * shard_levels(key, dims, cuts, -0.22, 0.18)
    return jnp.clip(array, -reach, reach).astype(held_as)


def setup_inputs(seed: int = 0) -> dict:
    splits = jax.random.split(jax.random.key(seed), 9)
    tokens = draw_tokens(jax.random.fold_in(splits[8], 71), 0)
    norm_gain = jnp.clip(jax.random.uniform(splits[1], (D,), jnp.float32, 0.5, 1.5), 0.5, 1.5)
    qkv_weight = draw_qkv_weight(jax.random.fold_in(splits[8], 71), 0)
    q_gain = draw_q_gain(jax.random.fold_in(splits[8], 71), 0)
    k_gain = draw_k_gain(jax.random.fold_in(splits[8], 71), 0)
    out_weight = bell_draw(splits[5], (HEADS * HEAD_DIM, D), (HEADS * HEAD_DIM) ** -0.5, 0.125, ((0, 8), (1, 64)))
    layer_scale = jnp.clip(jnp.exp(math.log(2.0) - 1.3862944 * jax.random.uniform(splits[6], (D,), jnp.float32) ** shard_levels(splits[6], (D,), ((0, 8),), -0.2, 0.2)), 0.5, 2.0)
    segment_ids = jnp.searchsorted(jnp.cumsum(ragged(splits[7], IMAGES, TOKENS, 2 * TOK_DEV, 2)), jnp.arange(TOKENS), side="right").astype(jnp.int32)
    return dict(tokens=tokens, norm_gain=norm_gain, qkv_weight=qkv_weight, q_gain=q_gain, k_gain=k_gain, out_weight=out_weight, layer_scale=layer_scale, segment_ids=segment_ids)


eps = 1e-06
floor_score = -1e+30

def attend(query, keys, values, query_seg, key_seg):
    count = query.shape[0]
    width = query.shape[1]
    heads = width // HEAD_DIM
    query_f = query.astype(jnp.float32).reshape(count, heads, HEAD_DIM)
    keys_f = keys.astype(jnp.float32).reshape(keys.shape[0], heads, HEAD_DIM)
    values_f = values.astype(jnp.float32).reshape(values.shape[0], heads, HEAD_DIM)
    scores = jnp.einsum('qhd,khd->hqk', query_f, keys_f) * HEAD_DIM ** (-0.5)
    mask = (query_seg[:, None] == key_seg[None, :])[None]
    scores = jnp.where(mask, scores, floor_score)
    peak = lax.optimization_barrier(jnp.max(scores, axis=-1, keepdims=True))
    weights = jnp.where(mask, jnp.exp(scores - peak), 0.0)
    total = lax.optimization_barrier(jnp.sum(weights, axis=-1))
    probs = weights.astype(jnp.bfloat16).astype(jnp.float32)
    context = jnp.einsum('hqk,khd->qhd', probs, values_f)
    context = context / jnp.transpose(total)[:, :, None]
    return context.reshape(count, width).astype(jnp.bfloat16)

def reference(tokens, norm_gain, qkv_weight, q_gain, k_gain, out_weight, layer_scale, segment_ids):
    source = tokens.astype(jnp.float32)
    normed = (source * lax.rsqrt(lax.optimization_barrier(jnp.mean(source * source, axis=-1, keepdims=True)) + eps) * norm_gain).astype(jnp.bfloat16)
    width = HEADS * HEAD_DIM
    flat = qkv_weight.reshape(D, 3 * width)
    joined = jnp.dot(normed, flat, preferred_element_type=jnp.float32).reshape(TOKENS, 3, width)
    query = joined[:, 0]
    keys = joined[:, 1]
    values = joined[:, 2]
    query_normed = (query * lax.rsqrt(lax.optimization_barrier(jnp.mean(query * query, axis=-1, keepdims=True)) + eps) * q_gain).astype(jnp.bfloat16)
    key_normed = (keys * lax.rsqrt(lax.optimization_barrier(jnp.mean(keys * keys, axis=-1, keepdims=True)) + eps) * k_gain).astype(jnp.bfloat16)
    values_low = values.astype(jnp.bfloat16)
    blank = jnp.zeros((2 * TOK_DEV, width), jnp.bfloat16)
    keys_pad = jnp.concatenate([blank, key_normed, blank], axis=0)
    values_pad = jnp.concatenate([blank, values_low, blank], axis=0)
    outside = jnp.full((2 * TOK_DEV,), -1, jnp.int32)
    seg_pad = jnp.concatenate([outside, segment_ids.astype(jnp.int32), outside], axis=0)

    def one_block(block):
        start = (block * TOK_DEV).astype(jnp.int32)
        query_block = lax.dynamic_slice_in_dim(query_normed, start, TOK_DEV, 0)
        query_seg = lax.dynamic_slice_in_dim(segment_ids.astype(jnp.int32), start, TOK_DEV, 0)
        key_block = lax.dynamic_slice_in_dim(keys_pad, start, 5 * TOK_DEV, 0)
        value_block = lax.dynamic_slice_in_dim(values_pad, start, 5 * TOK_DEV, 0)
        key_seg = lax.dynamic_slice_in_dim(seg_pad, start, 5 * TOK_DEV, 0)
        return attend(query_block, key_block, value_block, query_seg, key_seg)
    context = lax.map(one_block, jnp.arange(N_SEQ, dtype=jnp.int32)).reshape(TOKENS, width)
    projected = jnp.dot(context, out_weight, preferred_element_type=jnp.float32)
    return (source + layer_scale * projected).astype(jnp.bfloat16)
```

```python
import jax
import jax.numpy as jnp
from jax import lax
from jax.sharding import PartitionSpec as P

HEAD_DIM = 128


eps = 1e-06
floor_score = -1e30


def passed_along(x, axis, by):
    size = lax.axis_size(axis)
    pairs = [(i, i + by) for i in range(size) if 0 <= i + by < size]
    return lax.ppermute(x, axis, pairs)


def masked_scores(query, keys, query_seg, key_seg):
    scores = jnp.einsum(
        "qhd,khd->hqk", query, keys, preferred_element_type=jnp.float32
    ) * HEAD_DIM ** (-0.5)
    mask = (query_seg[:, None] == key_seg[None, :])[None]
    return (jnp.where(mask, scores, floor_score), mask)


def shards(tokens, norm_gain, qkv_weight, q_gain, k_gain, out_weight, layer_scale, segment_ids):
    count = tokens.shape[0]
    source = tokens.astype(jnp.float32)
    normed = (
        source * lax.rsqrt(jnp.mean(source * source, axis=-1, keepdims=True) + eps) * norm_gain
    ).astype(jnp.bfloat16)
    local_width = qkv_weight.shape[2]
    heads = local_width // HEAD_DIM
    stacked = jnp.concatenate([qkv_weight, jnp.transpose(out_weight)[:, None, :]], axis=1)
    gathered = lax.all_gather(stacked, "seq", axis=0, tiled=True)
    joined = jnp.einsum(
        "td,dch->tch",
        normed,
        gathered[:, :3],
        preferred_element_type=jnp.float32,
    )
    query = joined[:, 0]
    keys = joined[:, 1]
    values = joined[:, 2]
    query_sq, key_sq = lax.psum(
        (jnp.sum(query * query, axis=-1), jnp.sum(keys * keys, axis=-1)), "tp"
    )
    full_width = local_width * lax.axis_size("tp")
    query_normed = (query * lax.rsqrt(query_sq / full_width + eps)[:, None] * q_gain).astype(
        jnp.bfloat16
    )
    key_normed = (keys * lax.rsqrt(key_sq / full_width + eps)[:, None] * k_gain).astype(
        jnp.bfloat16
    )
    paired = jnp.stack([key_normed, values.astype(jnp.bfloat16)], axis=1)
    pieces = []
    for offset in (2, 1, 0, -1, -2):
        if offset == 0:
            pieces.append(paired)
        else:
            pieces.append(passed_along(paired, "seq", offset))
    widened = jnp.concatenate(pieces, axis=0)
    position = lax.axis_index("seq")
    outside = jnp.full((2 * count,), -1, jnp.int32)
    seg_pad = jnp.concatenate([outside, segment_ids, outside], axis=0)
    key_seg = lax.dynamic_slice_in_dim(seg_pad, position * count, 5 * count, 0)
    query_seg = lax.dynamic_slice_in_dim(segment_ids, position * count, count, 0)
    query_heads = query_normed.reshape(count, heads, HEAD_DIM)
    key_heads = widened[:, 0].reshape(5 * count, heads, HEAD_DIM)
    value_heads = widened[:, 1].reshape(5 * count, heads, HEAD_DIM)
    scores, mask = masked_scores(query_heads, key_heads, query_seg, key_seg)
    peak = jnp.max(scores, axis=-1, keepdims=True)
    weights = jnp.where(mask, jnp.exp(scores - peak), 0.0)
    total = jnp.sum(weights, axis=-1)
    probs = weights.astype(jnp.bfloat16)
    summed = jnp.einsum("hqk,khd->qhd", probs, value_heads, preferred_element_type=jnp.float32)
    context = (
        (summed / jnp.transpose(total)[:, :, None]).reshape(count, local_width).astype(jnp.bfloat16)
    )
    terms = jnp.einsum(
        "th,dh->td", context, gathered[:, 3], preferred_element_type=jnp.float32
    )
    projected = lax.psum_scatter(terms, "tp", scatter_dimension=1, tiled=True)
    share = layer_scale.shape[0]
    residual = lax.dynamic_slice_in_dim(source, lax.axis_index("tp") * share, share, 1)
    return (residual + layer_scale * projected).astype(jnp.bfloat16)


def solution(mesh):
    return jax.shard_map(
        shards,
        mesh=mesh,
        in_specs=(
            P("seq", None),
            P(),
            P("seq", None, "tp"),
            P("tp"),
            P("tp"),
            P("tp", "seq"),
            P("tp"),
            P(),
        ),
        out_specs=P("seq", "tp"),
        check_vma=False,
    )
```

```python
import functools

import jax
import jax.numpy as jnp
from jax import lax
from jax.sharding import PartitionSpec as P
from jax.experimental import pallas as pl
from jax.experimental.pallas import tpu as pltpu

HEAD_DIM = 128


eps = 1e-06
floor_score = -1e30


def passed_along(x, axis, by):
    size = lax.axis_size(axis)
    pairs = [(i, i + by) for i in range(size) if 0 <= i + by < size]
    return lax.ppermute(x, axis, pairs)


def gather_kernel(n, x_ref, out_ref, send_sem, recv_sem, local_sem):
    me = lax.axis_index("seq")
    tp = lax.axis_index("tp")
    mesh_id = pl.DeviceIdType.MESH
    barrier = pltpu.get_barrier_semaphore()

    def greet(k, carry):
        peer = lax.rem(me + k, n)
        pl.semaphore_signal(barrier, inc=1, device_id=(peer, tp), device_id_type=mesh_id)
        return carry

    lax.fori_loop(1, n, greet, 0)
    pl.semaphore_wait(barrier, n - 1)
    local = pltpu.make_async_copy(x_ref, out_ref.at[me], local_sem)
    local.start()

    def remote(k):
        peer = lax.rem(me + k, n)
        return pltpu.make_async_remote_copy(
            src_ref=x_ref,
            dst_ref=out_ref.at[me],
            send_sem=send_sem.at[k],
            recv_sem=recv_sem.at[k],
            device_id=(peer, tp),
            device_id_type=mesh_id,
        )

    def send(k, carry):
        remote(k).start()
        return carry

    def finish(k, carry):
        copy = remote(k)
        copy.wait_send()
        copy.wait_recv()
        return carry

    lax.fori_loop(1, n, send, 0)
    lax.fori_loop(1, n, finish, 0)
    local.wait()


def gather_seq(block):
    n = lax.axis_size("seq")
    return pl.pallas_call(
        functools.partial(gather_kernel, n),
        out_shape=jax.ShapeDtypeStruct((n,) + block.shape, block.dtype),
        in_specs=[pl.BlockSpec(memory_space=pl.ANY)],
        out_specs=pl.BlockSpec(memory_space=pl.ANY),
        scratch_shapes=[
            pltpu.SemaphoreType.DMA((n,)),
            pltpu.SemaphoreType.DMA((n,)),
            pltpu.SemaphoreType.DMA(()),
        ],
        compiler_params=pltpu.CompilerParams(collective_id=0, has_side_effects=True),
    )(block)


def masked_scores(query, keys, query_seg, key_seg):
    scores = jnp.einsum(
        "qhd,khd->hqk", query, keys, preferred_element_type=jnp.float32
    ) * HEAD_DIM ** (-0.5)
    mask = (query_seg[:, None] == key_seg[None, :])[None]
    return (jnp.where(mask, scores, floor_score), mask)


def shards(tokens, norm_gain, qkv_weight, q_gain, k_gain, out_weight, layer_scale, segment_ids):
    count = tokens.shape[0]
    source = tokens.astype(jnp.float32)
    normed = (
        source * lax.rsqrt(jnp.mean(source * source, axis=-1, keepdims=True) + eps) * norm_gain
    ).astype(jnp.bfloat16)
    local_width = qkv_weight.shape[2]
    heads = local_width // HEAD_DIM
    stacked = jnp.concatenate([qkv_weight, jnp.transpose(out_weight)[:, None, :]], axis=1)
    rows, kinds, width = stacked.shape
    gathered = gather_seq(stacked.reshape(rows, kinds * width)).reshape(-1, kinds, width)
    joined = jnp.einsum(
        "td,dch->tch",
        normed,
        gathered[:, :3],
        preferred_element_type=jnp.float32,
    )
    query = joined[:, 0]
    keys = joined[:, 1]
    values = joined[:, 2]
    query_sq, key_sq = lax.psum(
        (jnp.sum(query * query, axis=-1), jnp.sum(keys * keys, axis=-1)), "tp"
    )
    full_width = local_width * lax.axis_size("tp")
    query_normed = (query * lax.rsqrt(query_sq / full_width + eps)[:, None] * q_gain).astype(
        jnp.bfloat16
    )
    key_normed = (keys * lax.rsqrt(key_sq / full_width + eps)[:, None] * k_gain).astype(
        jnp.bfloat16
    )
    paired = jnp.stack([key_normed, values.astype(jnp.bfloat16)], axis=1)
    pieces = []
    for offset in (2, 1, 0, -1, -2):
        if offset == 0:
            pieces.append(paired)
        else:
            pieces.append(passed_along(paired, "seq", offset))
    widened = jnp.concatenate(pieces, axis=0)
    position = lax.axis_index("seq")
    outside = jnp.full((2 * count,), -1, jnp.int32)
    seg_pad = jnp.concatenate([outside, segment_ids, outside], axis=0)
    key_seg = lax.dynamic_slice_in_dim(seg_pad, position * count, 5 * count, 0)
    query_seg = lax.dynamic_slice_in_dim(segment_ids, position * count, count, 0)
    query_heads = query_normed.reshape(count, heads, HEAD_DIM)
    key_heads = widened[:, 0].reshape(5 * count, heads, HEAD_DIM)
    value_heads = widened[:, 1].reshape(5 * count, heads, HEAD_DIM)
    scores, mask = masked_scores(query_heads, key_heads, query_seg, key_seg)
    peak = jnp.max(scores, axis=-1, keepdims=True)
    weights = jnp.where(mask, jnp.exp(scores - peak), 0.0)
    total = jnp.sum(weights, axis=-1)
    probs = weights.astype(jnp.bfloat16)
    summed = jnp.einsum("hqk,khd->qhd", probs, value_heads, preferred_element_type=jnp.float32)
    context = (
        (summed / jnp.transpose(total)[:, :, None]).reshape(count, local_width).astype(jnp.bfloat16)
    )
    terms = jnp.einsum(
        "th,dh->td", context, gathered[:, 3], preferred_element_type=jnp.float32
    )
    projected = lax.psum_scatter(terms, "tp", scatter_dimension=1, tiled=True)
    share = layer_scale.shape[0]
    residual = lax.dynamic_slice_in_dim(source, lax.axis_index("tp") * share, share, 1)
    return (residual + layer_scale * projected).astype(jnp.bfloat16)


def solution(mesh):
    return jax.shard_map(
        shards,
        mesh=mesh,
        in_specs=(
            P("seq", None),
            P(),
            P("seq", None, "tp"),
            P("tp"),
            P("tp"),
            P("tp", "seq"),
            P("tp"),
            P(),
        ),
        out_specs=P("seq", "tp"),
        check_vma=False,
    )
```

```python
import functools

import jax
import jax.numpy as jnp
from jax import lax
from jax.sharding import PartitionSpec as P
from jax.experimental import pallas as pl
from jax.experimental.pallas import tpu as pltpu

HEAD_DIM = 128


eps = 1e-06
floor_score = -1e30


def passed_along(x, axis, by):
    size = lax.axis_size(axis)
    pairs = [(i, i + by) for i in range(size) if 0 <= i + by < size]
    return lax.ppermute(x, axis, pairs)


def gather_kernel(n, x_ref, out_ref, pair_sems, row_sems, ring_sems, local_sem):
    me = lax.axis_index("seq")
    tp = lax.axis_index("tp")
    mesh_id = pl.DeviceIdType.MESH
    pair, row = 2, 4
    slab = pair * row
    rings = n // slab
    low = me % pair
    across = (me // pair) % row
    ring = me // slab
    partner = me - low + (1 - low)
    row_peers = [ring * slab + ((across + k) % row) * pair + low for k in range(1, row)]
    ahead = ((ring + 1) % rings) * slab + me % slab
    behind = ((ring + rings - 1) % rings) * slab + me % slab

    barrier = pltpu.get_barrier_semaphore()
    for peer in [partner, ahead, behind] + row_peers:
        pl.semaphore_signal(barrier, inc=1, device_id=(peer, tp), device_id_type=mesh_id)
    pl.semaphore_wait(barrier, 3 + len(row_peers))

    local = pltpu.make_async_copy(x_ref, out_ref.at[me], local_sem)
    local.start()
    first = pltpu.make_async_remote_copy(
        src_ref=x_ref,
        dst_ref=out_ref.at[me],
        send_sem=pair_sems.at[0],
        recv_sem=pair_sems.at[1],
        device_id=(partner, tp),
        device_id_type=mesh_id,
    )
    first.start()
    local.wait()
    first.wait_send()
    first.wait_recv()

    base = me - low
    second = []
    for k, peer in enumerate(row_peers):
        copy = pltpu.make_async_remote_copy(
            src_ref=out_ref.at[pl.ds(base, pair)],
            dst_ref=out_ref.at[pl.ds(base, pair)],
            send_sem=row_sems.at[0, k],
            recv_sem=row_sems.at[1, k],
            device_id=(peer, tp),
            device_id_type=mesh_id,
        )
        copy.start()
        second.append(copy)
    for copy in second:
        copy.wait_send()
        copy.wait_recv()

    half = slab // 2

    def step(t, carry):
        forward = (ring - t + rings) % rings
        backward = (ring + t) % rings
        window_f = out_ref.at[pl.ds(forward * slab, half)]
        window_b = out_ref.at[pl.ds(backward * slab + half, half)]
        to_ahead = pltpu.make_async_remote_copy(
            src_ref=window_f,
            dst_ref=window_f,
            send_sem=ring_sems.at[0, 0, t],
            recv_sem=ring_sems.at[1, 0, t],
            device_id=(ahead, tp),
            device_id_type=mesh_id,
        )
        to_behind = pltpu.make_async_remote_copy(
            src_ref=window_b,
            dst_ref=window_b,
            send_sem=ring_sems.at[0, 1, t],
            recv_sem=ring_sems.at[1, 1, t],
            device_id=(behind, tp),
            device_id_type=mesh_id,
        )
        to_ahead.start()
        to_behind.start()
        to_ahead.wait_send()
        to_behind.wait_send()
        to_ahead.wait_recv()
        to_behind.wait_recv()
        return carry

    lax.fori_loop(0, rings - 1, step, 0)


def gather_seq(block):
    n = lax.axis_size("seq")
    return pl.pallas_call(
        functools.partial(gather_kernel, n),
        out_shape=jax.ShapeDtypeStruct((n,) + block.shape, block.dtype),
        in_specs=[pl.BlockSpec(memory_space=pl.ANY)],
        out_specs=pl.BlockSpec(memory_space=pl.ANY),
        scratch_shapes=[
            pltpu.SemaphoreType.DMA((2,)),
            pltpu.SemaphoreType.DMA((2, 3)),
            pltpu.SemaphoreType.DMA((2, 2, n // 8)),
            pltpu.SemaphoreType.DMA(()),
        ],
        compiler_params=pltpu.CompilerParams(collective_id=0, has_side_effects=True),
    )(block)


def masked_scores(query, keys, query_seg, key_seg):
    scores = jnp.einsum(
        "qhd,khd->hqk", query, keys, preferred_element_type=jnp.float32
    ) * HEAD_DIM ** (-0.5)
    mask = (query_seg[:, None] == key_seg[None, :])[None]
    return (jnp.where(mask, scores, floor_score), mask)


def shards(tokens, norm_gain, qkv_weight, q_gain, k_gain, out_weight, layer_scale, segment_ids):
    count = tokens.shape[0]
    source = tokens.astype(jnp.float32)
    normed = (
        source * lax.rsqrt(jnp.mean(source * source, axis=-1, keepdims=True) + eps) * norm_gain
    ).astype(jnp.bfloat16)
    local_width = qkv_weight.shape[2]
    heads = local_width // HEAD_DIM
    stacked = jnp.concatenate([qkv_weight, jnp.transpose(out_weight)[:, None, :]], axis=1)
    rows, kinds, width = stacked.shape
    gathered = gather_seq(stacked.reshape(rows, kinds * width)).reshape(-1, kinds, width)
    joined = jnp.einsum(
        "td,dch->tch",
        normed,
        gathered[:, :3],
        preferred_element_type=jnp.float32,
    )
    query = joined[:, 0]
    keys = joined[:, 1]
    values = joined[:, 2]
    query_sq, key_sq = lax.psum(
        (jnp.sum(query * query, axis=-1), jnp.sum(keys * keys, axis=-1)), "tp"
    )
    full_width = local_width * lax.axis_size("tp")
    query_normed = (query * lax.rsqrt(query_sq / full_width + eps)[:, None] * q_gain).astype(
        jnp.bfloat16
    )
    key_normed = (keys * lax.rsqrt(key_sq / full_width + eps)[:, None] * k_gain).astype(
        jnp.bfloat16
    )
    paired = jnp.stack([key_normed, values.astype(jnp.bfloat16)], axis=1)
    pieces = []
    for offset in (2, 1, 0, -1, -2):
        if offset == 0:
            pieces.append(paired)
        else:
            pieces.append(passed_along(paired, "seq", offset))
    widened = jnp.concatenate(pieces, axis=0)
    position = lax.axis_index("seq")
    outside = jnp.full((2 * count,), -1, jnp.int32)
    seg_pad = jnp.concatenate([outside, segment_ids, outside], axis=0)
    key_seg = lax.dynamic_slice_in_dim(seg_pad, position * count, 5 * count, 0)
    query_seg = lax.dynamic_slice_in_dim(segment_ids, position * count, count, 0)
    query_heads = query_normed.reshape(count, heads, HEAD_DIM)
    key_heads = widened[:, 0].reshape(5 * count, heads, HEAD_DIM)
    value_heads = widened[:, 1].reshape(5 * count, heads, HEAD_DIM)
    scores, mask = masked_scores(query_heads, key_heads, query_seg, key_seg)
    peak = jnp.max(scores, axis=-1, keepdims=True)
    weights = jnp.where(mask, jnp.exp(scores - peak), 0.0)
    total = jnp.sum(weights, axis=-1)
    probs = weights.astype(jnp.bfloat16)
    summed = jnp.einsum("hqk,khd->qhd", probs, value_heads, preferred_element_type=jnp.float32)
    context = (
        (summed / jnp.transpose(total)[:, :, None]).reshape(count, local_width).astype(jnp.bfloat16)
    )
    terms = jnp.einsum(
        "th,dh->td", context, gathered[:, 3], preferred_element_type=jnp.float32
    )
    projected = lax.psum_scatter(terms, "tp", scatter_dimension=1, tiled=True)
    share = layer_scale.shape[0]
    residual = lax.dynamic_slice_in_dim(source, lax.axis_index("tp") * share, share, 1)
    return (residual + layer_scale * projected).astype(jnp.bfloat16)


def solution(mesh):
    return jax.shard_map(
        shards,
        mesh=mesh,
        in_specs=(
            P("seq", None),
            P(),
            P("seq", None, "tp"),
            P("tp"),
            P("tp"),
            P("tp", "seq"),
            P("tp"),
            P(),
        ),
        out_specs=P("seq", "tp"),
        check_vma=False,
    )
```

```python
import functools

import jax
import jax.numpy as jnp
from jax import lax
from jax.sharding import PartitionSpec as P
from jax.experimental import pallas as pl
from jax.experimental.pallas import tpu as pltpu

HEAD_DIM = 128


eps = 1e-06
floor_score = -1e30


def passed_along(x, axis, by):
    size = lax.axis_size(axis)
    pairs = [(i, i + by) for i in range(size) if 0 <= i + by < size]
    return lax.ppermute(x, axis, pairs)


def gather_kernel(n, x_ref, out_ref, pair_sems, row_sems, ring_sems, local_sem):
    me = lax.axis_index("seq")
    tp = lax.axis_index("tp")
    mesh_id = pl.DeviceIdType.MESH
    pair, row = 2, 4
    slab = pair * row
    rings = n // slab
    low = me % pair
    across = (me // pair) % row
    ring = me // slab
    partner = me - low + (1 - low)
    row_peers = [ring * slab + ((across + k) % row) * pair + low for k in range(1, row)]
    ahead = ((ring + 1) % rings) * slab + me % slab
    behind = ((ring + rings - 1) % rings) * slab + me % slab

    barrier = pltpu.get_barrier_semaphore()
    for peer in [partner, ahead, behind] + row_peers:
        pl.semaphore_signal(barrier, inc=1, device_id=(peer, tp), device_id_type=mesh_id)
    pl.semaphore_wait(barrier, 3 + len(row_peers))

    local = pltpu.make_async_copy(x_ref, out_ref.at[me], local_sem)
    local.start()
    first = pltpu.make_async_remote_copy(
        src_ref=x_ref,
        dst_ref=out_ref.at[me],
        send_sem=pair_sems.at[0],
        recv_sem=pair_sems.at[1],
        device_id=(partner, tp),
        device_id_type=mesh_id,
    )
    first.start()
    local.wait()
    first.wait_send()
    first.wait_recv()

    base = me - low
    second = []
    for k, peer in enumerate(row_peers):
        copy = pltpu.make_async_remote_copy(
            src_ref=out_ref.at[pl.ds(base, pair)],
            dst_ref=out_ref.at[pl.ds(base, pair)],
            send_sem=row_sems.at[0, k],
            recv_sem=row_sems.at[1, k],
            device_id=(peer, tp),
            device_id_type=mesh_id,
        )
        copy.start()
        second.append(copy)
    for copy in second:
        copy.wait_send()
        copy.wait_recv()

    half = slab // 2

    def step(t, carry):
        forward = (ring - t + rings) % rings
        backward = (ring + t) % rings
        window_f = out_ref.at[pl.ds(forward * slab, half)]
        window_b = out_ref.at[pl.ds(backward * slab + half, half)]
        to_ahead = pltpu.make_async_remote_copy(
            src_ref=window_f,
            dst_ref=window_f,
            send_sem=ring_sems.at[0, 0, t],
            recv_sem=ring_sems.at[1, 0, t],
            device_id=(ahead, tp),
            device_id_type=mesh_id,
        )
        to_behind = pltpu.make_async_remote_copy(
            src_ref=window_b,
            dst_ref=window_b,
            send_sem=ring_sems.at[0, 1, t],
            recv_sem=ring_sems.at[1, 1, t],
            device_id=(behind, tp),
            device_id_type=mesh_id,
        )
        to_ahead.start()
        to_behind.start()
        to_ahead.wait_send()
        to_behind.wait_send()
        to_ahead.wait_recv()
        to_behind.wait_recv()
        return carry

    lax.fori_loop(0, rings - 1, step, 0)


def gather_seq(block):
    n = lax.axis_size("seq")
    return pl.pallas_call(
        functools.partial(gather_kernel, n),
        out_shape=jax.ShapeDtypeStruct((n,) + block.shape, block.dtype),
        in_specs=[pl.BlockSpec(memory_space=pl.ANY)],
        out_specs=pl.BlockSpec(memory_space=pl.ANY),
        scratch_shapes=[
            pltpu.SemaphoreType.DMA((2,)),
            pltpu.SemaphoreType.DMA((2, 3)),
            pltpu.SemaphoreType.DMA((2, 2, n // 8)),
            pltpu.SemaphoreType.DMA(()),
        ],
        compiler_params=pltpu.CompilerParams(collective_id=0, has_side_effects=True),
    )(block)


def masked_scores(query, keys, query_seg, key_seg):
    scores = jnp.einsum(
        "qhd,khd->hqk", query, keys, preferred_element_type=jnp.float32
    ) * HEAD_DIM ** (-0.5)
    mask = (query_seg[:, None] == key_seg[None, :])[None]
    return (jnp.where(mask, scores, floor_score), mask)


def shards(tokens, norm_gain, qkv_weight, q_gain, k_gain, out_weight, layer_scale, segment_ids):
    count = tokens.shape[0]
    source = tokens.astype(jnp.float32)
    normed = (
        source * lax.rsqrt(jnp.mean(source * source, axis=-1, keepdims=True) + eps) * norm_gain
    ).astype(jnp.bfloat16)
    local_width = qkv_weight.shape[2]
    heads = local_width // HEAD_DIM
    stacked = jnp.concatenate([qkv_weight, jnp.transpose(out_weight)[:, None, :]], axis=1)
    rows, kinds, width = stacked.shape
    gathered = gather_seq(stacked.reshape(rows, kinds * width)).reshape(-1, kinds, width)
    joined = jnp.einsum(
        "td,dch->tch",
        normed,
        gathered[:, :3],
        preferred_element_type=jnp.float32,
    )
    query = joined[:, 0]
    keys = joined[:, 1]
    values = joined[:, 2]
    query_sq, key_sq = lax.psum(
        (jnp.sum(query * query, axis=-1), jnp.sum(keys * keys, axis=-1)), "tp"
    )
    full_width = local_width * lax.axis_size("tp")
    query_normed = (query * lax.rsqrt(query_sq / full_width + eps)[:, None] * q_gain).astype(
        jnp.bfloat16
    )
    key_normed = (keys * lax.rsqrt(key_sq / full_width + eps)[:, None] * k_gain).astype(
        jnp.bfloat16
    )
    paired = jnp.stack([key_normed, values.astype(jnp.bfloat16)], axis=1)
    pieces = []
    for offset in (2, 1, 0, -1, -2):
        if offset == 0:
            pieces.append(paired)
        else:
            pieces.append(passed_along(paired, "seq", offset))
    widened = jnp.concatenate(pieces, axis=0)
    position = lax.axis_index("seq")
    outside = jnp.full((2 * count,), -1, jnp.int32)
    seg_pad = jnp.concatenate([outside, segment_ids, outside], axis=0)
    key_seg = lax.dynamic_slice_in_dim(seg_pad, position * count, 5 * count, 0)
    query_seg = lax.dynamic_slice_in_dim(segment_ids, position * count, count, 0)
    query_heads = query_normed.reshape(count, heads, HEAD_DIM)
    key_heads = widened[:, 0].reshape(5 * count, heads, HEAD_DIM)
    value_heads = widened[:, 1].reshape(5 * count, heads, HEAD_DIM)
    scores, mask = masked_scores(query_heads, key_heads, query_seg, key_seg)
    peak = jnp.max(scores, axis=-1, keepdims=True)
    weights = jnp.where(mask, jnp.exp(scores - peak), 0.0)
    total = jnp.sum(weights, axis=-1)
    probs = weights.astype(jnp.bfloat16)
    summed = jnp.einsum("hqk,khd->qhd", probs, value_heads, preferred_element_type=jnp.float32)
    context = (
        (summed / jnp.transpose(total)[:, :, None]).reshape(count, local_width).astype(jnp.bfloat16)
    )
    blank = jnp.zeros_like(context)
    widened_context = jnp.stack([blank, blank, blank, context], axis=1)
    terms = jnp.einsum(
        "tkh,dkh->td", widened_context, gathered, preferred_element_type=jnp.float32
    )
    projected = lax.psum_scatter(
        terms.astype(jnp.bfloat16), "tp", scatter_dimension=1, tiled=True
    ).astype(jnp.float32)
    share = layer_scale.shape[0]
    residual = lax.dynamic_slice_in_dim(source, lax.axis_index("tp") * share, share, 1)
    return (residual + layer_scale * projected).astype(jnp.bfloat16)


def solution(mesh):
    return jax.shard_map(
        shards,
        mesh=mesh,
        in_specs=(
            P("seq", None),
            P(),
            P("seq", None, "tp"),
            P("tp"),
            P("tp"),
            P("tp", "seq"),
            P("tp"),
            P(),
        ),
        out_specs=P("seq", "tp"),
        check_vma=False,
    )
```

```python
import functools

import jax
import jax.numpy as jnp
from jax import lax
from jax.sharding import PartitionSpec as P
from jax.experimental import pallas as pl
from jax.experimental.pallas import tpu as pltpu

HEAD_DIM = 128


eps = 1e-06
floor_score = -1e30


def passed_along(x, axis, by):
    size = lax.axis_size(axis)
    pairs = [(i, i + by) for i in range(size) if 0 <= i + by < size]
    return lax.ppermute(x, axis, pairs)


def gather_kernel(n, x_ref, out_ref, pair_sems, row_sems, ring_sems, local_sem):
    me = lax.axis_index("seq")
    tp = lax.axis_index("tp")
    mesh_id = pl.DeviceIdType.MESH
    pair, row = 2, 4
    slab = pair * row
    rings = n // slab
    low = me % pair
    across = (me // pair) % row
    ring = me // slab
    partner = me - low + (1 - low)
    row_peers = [ring * slab + ((across + k) % row) * pair + low for k in range(1, row)]
    ahead = ((ring + 1) % rings) * slab + me % slab
    behind = ((ring + rings - 1) % rings) * slab + me % slab

    barrier = pltpu.get_barrier_semaphore()
    for peer in [partner, ahead, behind] + row_peers:
        pl.semaphore_signal(barrier, inc=1, device_id=(peer, tp), device_id_type=mesh_id)
    pl.semaphore_wait(barrier, 3 + len(row_peers))

    local = pltpu.make_async_copy(x_ref, out_ref.at[me], local_sem)
    local.start()
    first = pltpu.make_async_remote_copy(
        src_ref=x_ref,
        dst_ref=out_ref.at[me],
        send_sem=pair_sems.at[0],
        recv_sem=pair_sems.at[1],
        device_id=(partner, tp),
        device_id_type=mesh_id,
    )
    first.start()
    local.wait()
    first.wait_send()
    first.wait_recv()

    base = me - low
    second = []
    for k, peer in enumerate(row_peers):
        copy = pltpu.make_async_remote_copy(
            src_ref=out_ref.at[pl.ds(base, pair)],
            dst_ref=out_ref.at[pl.ds(base, pair)],
            send_sem=row_sems.at[0, k],
            recv_sem=row_sems.at[1, k],
            device_id=(peer, tp),
            device_id_type=mesh_id,
        )
        copy.start()
        second.append(copy)
    for copy in second:
        copy.wait_send()
        copy.wait_recv()

    half = slab // 2

    def step(t, carry):
        forward = (ring - t + rings) % rings
        backward = (ring + t) % rings
        window_f = out_ref.at[pl.ds(forward * slab, half)]
        window_b = out_ref.at[pl.ds(backward * slab + half, half)]
        to_ahead = pltpu.make_async_remote_copy(
            src_ref=window_f,
            dst_ref=window_f,
            send_sem=ring_sems.at[0, 0, t],
            recv_sem=ring_sems.at[1, 0, t],
            device_id=(ahead, tp),
            device_id_type=mesh_id,
        )
        to_behind = pltpu.make_async_remote_copy(
            src_ref=window_b,
            dst_ref=window_b,
            send_sem=ring_sems.at[0, 1, t],
            recv_sem=ring_sems.at[1, 1, t],
            device_id=(behind, tp),
            device_id_type=mesh_id,
        )
        to_ahead.start()
        to_behind.start()
        to_ahead.wait_send()
        to_behind.wait_send()
        to_ahead.wait_recv()
        to_behind.wait_recv()
        return carry

    lax.fori_loop(0, rings - 1, step, 0)


def gather_seq(block):
    n = lax.axis_size("seq")
    return pl.pallas_call(
        functools.partial(gather_kernel, n),
        out_shape=jax.ShapeDtypeStruct((n,) + block.shape, block.dtype),
        in_specs=[pl.BlockSpec(memory_space=pl.ANY)],
        out_specs=pl.BlockSpec(memory_space=pl.ANY),
        scratch_shapes=[
            pltpu.SemaphoreType.DMA((2,)),
            pltpu.SemaphoreType.DMA((2, 3)),
            pltpu.SemaphoreType.DMA((2, 2, n // 8)),
            pltpu.SemaphoreType.DMA(()),
        ],
        compiler_params=pltpu.CompilerParams(collective_id=0, has_side_effects=True),
    )(block)


def masked_scores(query, keys, query_seg, key_seg):
    scores = jnp.einsum(
        "qhd,khd->hqk", query, keys, preferred_element_type=jnp.float32
    ) * HEAD_DIM ** (-0.5)
    mask = (query_seg[:, None] == key_seg[None, :])[None]
    return (jnp.where(mask, scores, floor_score), mask)


def shards(tokens, norm_gain, qkv_weight, q_gain, k_gain, out_weight, layer_scale, segment_ids):
    count = tokens.shape[0]
    source = tokens.astype(jnp.float32)
    normed = (
        source * lax.rsqrt(jnp.mean(source * source, axis=-1, keepdims=True) + eps) * norm_gain
    ).astype(jnp.bfloat16)
    local_width = qkv_weight.shape[2]
    heads = local_width // HEAD_DIM
    stacked = jnp.concatenate([qkv_weight, jnp.transpose(out_weight)[:, None, :]], axis=1)
    rows, kinds, width = stacked.shape
    gathered = gather_seq(stacked).reshape(-1, kinds, width)
    joined = jnp.einsum(
        "td,dch->tch",
        normed,
        gathered[:, :3],
        preferred_element_type=jnp.float32,
    )
    query = joined[:, 0]
    keys = joined[:, 1]
    values = joined[:, 2]
    query_sq, key_sq = lax.psum(
        (jnp.sum(query * query, axis=-1), jnp.sum(keys * keys, axis=-1)), "tp"
    )
    full_width = local_width * lax.axis_size("tp")
    query_normed = (query * lax.rsqrt(query_sq / full_width + eps)[:, None] * q_gain).astype(
        jnp.bfloat16
    )
    key_normed = (keys * lax.rsqrt(key_sq / full_width + eps)[:, None] * k_gain).astype(
        jnp.bfloat16
    )
    paired = jnp.stack([key_normed, values.astype(jnp.bfloat16)], axis=1)
    pieces = []
    for offset in (2, 1, 0, -1, -2):
        if offset == 0:
            pieces.append(paired)
        else:
            pieces.append(passed_along(paired, "seq", offset))
    widened = jnp.concatenate(pieces, axis=0)
    position = lax.axis_index("seq")
    outside = jnp.full((2 * count,), -1, jnp.int32)
    seg_pad = jnp.concatenate([outside, segment_ids, outside], axis=0)
    key_seg = lax.dynamic_slice_in_dim(seg_pad, position * count, 5 * count, 0)
    query_seg = lax.dynamic_slice_in_dim(segment_ids, position * count, count, 0)
    query_heads = query_normed.reshape(count, heads, HEAD_DIM)
    key_heads = widened[:, 0].reshape(5 * count, heads, HEAD_DIM)
    value_heads = widened[:, 1].reshape(5 * count, heads, HEAD_DIM)
    scores, mask = masked_scores(query_heads, key_heads, query_seg, key_seg)
    peak = jnp.max(scores, axis=-1, keepdims=True)
    weights = jnp.where(mask, jnp.exp(scores - peak), 0.0)
    total = jnp.sum(weights, axis=-1)
    probs = weights.astype(jnp.bfloat16)
    summed = jnp.einsum("hqk,khd->qhd", probs, value_heads, preferred_element_type=jnp.float32)
    context = (
        (summed / jnp.transpose(total)[:, :, None]).reshape(count, local_width).astype(jnp.bfloat16)
    )
    blank = jnp.zeros_like(context)
    widened_context = jnp.stack([blank, blank, blank, context], axis=1)
    terms = jnp.einsum(
        "tkh,dkh->td", widened_context, gathered, preferred_element_type=jnp.float32
    )
    projected = lax.psum_scatter(
        terms.astype(jnp.bfloat16), "tp", scatter_dimension=1, tiled=True
    ).astype(jnp.float32)
    share = layer_scale.shape[0]
    residual = lax.dynamic_slice_in_dim(source, lax.axis_index("tp") * share, share, 1)
    return (residual + layer_scale * projected).astype(jnp.bfloat16)


def solution(mesh):
    return jax.shard_map(
        shards,
        mesh=mesh,
        in_specs=(
            P("seq", None),
            P(),
            P("seq", None, "tp"),
            P("tp"),
            P("tp"),
            P("tp", "seq"),
            P("tp"),
            P(),
        ),
        out_specs=P("seq", "tp"),
        check_vma=False,
    )
```

```python
import functools

import jax
import jax.numpy as jnp
from jax import lax
from jax.sharding import PartitionSpec as P
from jax.experimental import pallas as pl
from jax.experimental.pallas import tpu as pltpu

HEAD_DIM = 128


eps = 1e-06
floor_score = -1e30


def passed_along(x, axis, by):
    size = lax.axis_size(axis)
    pairs = [(i, i + by) for i in range(size) if 0 <= i + by < size]
    return lax.ppermute(x, axis, pairs)


def gather_kernel(n, x_ref, out_ref, pair_sems, row_sems, ring_sems, local_sem):
    me = lax.axis_index("seq")
    tp = lax.axis_index("tp")
    mesh_id = pl.DeviceIdType.MESH
    pair, row = 2, 4
    slab = pair * row
    rings = n // slab
    low = me % pair
    across = (me // pair) % row
    ring = me // slab
    partner = me - low + (1 - low)
    row_peers = [ring * slab + ((across + k) % row) * pair + low for k in range(1, row)]
    ahead = ((ring + 1) % rings) * slab + me % slab
    behind = ((ring + rings - 1) % rings) * slab + me % slab

    barrier = pltpu.get_barrier_semaphore()
    for peer in [partner, ahead, behind] + row_peers:
        pl.semaphore_signal(barrier, inc=1, device_id=(peer, tp), device_id_type=mesh_id)
    pl.semaphore_wait(barrier, 3 + len(row_peers))

    local = pltpu.make_async_copy(x_ref, out_ref.at[me], local_sem)
    local.start()
    first = pltpu.make_async_remote_copy(
        src_ref=x_ref,
        dst_ref=out_ref.at[me],
        send_sem=pair_sems.at[0],
        recv_sem=pair_sems.at[1],
        device_id=(partner, tp),
        device_id_type=mesh_id,
    )
    first.start()
    local.wait()
    first.wait_send()
    first.wait_recv()

    base = me - low
    second = []
    for k, peer in enumerate(row_peers):
        copy = pltpu.make_async_remote_copy(
            src_ref=out_ref.at[pl.ds(base, pair)],
            dst_ref=out_ref.at[pl.ds(base, pair)],
            send_sem=row_sems.at[0, k],
            recv_sem=row_sems.at[1, k],
            device_id=(peer, tp),
            device_id_type=mesh_id,
        )
        copy.start()
        second.append(copy)
    for copy in second:
        copy.wait_send()
        copy.wait_recv()

    half = slab // 2

    def step(t, carry):
        forward = (ring - t + rings) % rings
        backward = (ring + t) % rings
        window_f = out_ref.at[pl.ds(forward * slab, half)]
        window_b = out_ref.at[pl.ds(backward * slab + half, half)]
        to_ahead = pltpu.make_async_remote_copy(
            src_ref=window_f,
            dst_ref=window_f,
            send_sem=ring_sems.at[0, 0, t],
            recv_sem=ring_sems.at[1, 0, t],
            device_id=(ahead, tp),
            device_id_type=mesh_id,
        )
        to_behind = pltpu.make_async_remote_copy(
            src_ref=window_b,
            dst_ref=window_b,
            send_sem=ring_sems.at[0, 1, t],
            recv_sem=ring_sems.at[1, 1, t],
            device_id=(behind, tp),
            device_id_type=mesh_id,
        )
        to_ahead.start()
        to_behind.start()
        to_ahead.wait_send()
        to_behind.wait_send()
        to_ahead.wait_recv()
        to_behind.wait_recv()
        return carry

    lax.fori_loop(0, rings - 1, step, 0)


def gather_seq(block):
    n = lax.axis_size("seq")
    return pl.pallas_call(
        functools.partial(gather_kernel, n),
        out_shape=jax.ShapeDtypeStruct((n,) + block.shape, block.dtype),
        in_specs=[pl.BlockSpec(memory_space=pl.ANY)],
        out_specs=pl.BlockSpec(memory_space=pl.ANY),
        scratch_shapes=[
            pltpu.SemaphoreType.DMA((2,)),
            pltpu.SemaphoreType.DMA((2, 3)),
            pltpu.SemaphoreType.DMA((2, 2, n // 8)),
            pltpu.SemaphoreType.DMA(()),
        ],
        compiler_params=pltpu.CompilerParams(collective_id=0, has_side_effects=True),
    )(block)


def scatter_kernel(chips, x_ref, out_ref, send_sem, recv_sem, local_sem):
    seq = lax.axis_index("seq")
    tp = lax.axis_index("tp")
    mesh_id = pl.DeviceIdType.MESH
    core = tp % 2
    mine = tp // 2
    owners = [(mine + k) % chips for k in range(1, chips)]

    barrier = pltpu.get_barrier_semaphore()
    for owner in owners:
        pl.semaphore_signal(
            barrier, inc=1, device_id=(seq, owner * 2 + core), device_id_type=mesh_id
        )
    pl.semaphore_wait(barrier, chips - 1)

    local = pltpu.make_async_copy(x_ref.at[mine], out_ref.at[mine], local_sem)
    local.start()
    copies = []
    for k, owner in enumerate(owners):
        copy = pltpu.make_async_remote_copy(
            src_ref=x_ref.at[owner],
            dst_ref=out_ref.at[mine],
            send_sem=send_sem.at[k],
            recv_sem=recv_sem.at[k],
            device_id=(seq, owner * 2 + core),
            device_id_type=mesh_id,
        )
        copy.start()
        copies.append(copy)
    for copy in copies:
        copy.wait_send()
        copy.wait_recv()
    local.wait()


def scatter_chips(block):
    chips = block.shape[0]
    return pl.pallas_call(
        functools.partial(scatter_kernel, chips),
        out_shape=jax.ShapeDtypeStruct(block.shape, block.dtype),
        in_specs=[pl.BlockSpec(memory_space=pl.ANY)],
        out_specs=pl.BlockSpec(memory_space=pl.ANY),
        scratch_shapes=[
            pltpu.SemaphoreType.DMA((chips,)),
            pltpu.SemaphoreType.DMA((chips,)),
            pltpu.SemaphoreType.DMA(()),
        ],
        compiler_params=pltpu.CompilerParams(collective_id=1, has_side_effects=True),
    )(block)


def masked_scores(query, keys, query_seg, key_seg):
    scores = jnp.einsum(
        "qhd,khd->hqk", query, keys, preferred_element_type=jnp.float32
    ) * HEAD_DIM ** (-0.5)
    mask = (query_seg[:, None] == key_seg[None, :])[None]
    return (jnp.where(mask, scores, floor_score), mask)


def shards(tokens, norm_gain, qkv_weight, q_gain, k_gain, out_weight, layer_scale, segment_ids):
    count = tokens.shape[0]
    source = tokens.astype(jnp.float32)
    normed = (
        source * lax.rsqrt(jnp.mean(source * source, axis=-1, keepdims=True) + eps) * norm_gain
    ).astype(jnp.bfloat16)
    local_width = qkv_weight.shape[2]
    heads = local_width // HEAD_DIM
    stacked = jnp.concatenate([qkv_weight, jnp.transpose(out_weight)[:, None, :]], axis=1)
    rows, kinds, width = stacked.shape
    gathered = gather_seq(stacked).reshape(-1, kinds, width)
    joined = jnp.einsum(
        "td,dch->tch",
        normed,
        gathered[:, :3],
        preferred_element_type=jnp.float32,
    )
    query = joined[:, 0]
    keys = joined[:, 1]
    values = joined[:, 2]
    query_sq, key_sq = lax.psum(
        (jnp.sum(query * query, axis=-1), jnp.sum(keys * keys, axis=-1)), "tp"
    )
    full_width = local_width * lax.axis_size("tp")
    query_normed = (query * lax.rsqrt(query_sq / full_width + eps)[:, None] * q_gain).astype(
        jnp.bfloat16
    )
    key_normed = (keys * lax.rsqrt(key_sq / full_width + eps)[:, None] * k_gain).astype(
        jnp.bfloat16
    )
    paired = jnp.stack([key_normed, values.astype(jnp.bfloat16)], axis=1)
    pieces = []
    for offset in (2, 1, 0, -1, -2):
        if offset == 0:
            pieces.append(paired)
        else:
            pieces.append(passed_along(paired, "seq", offset))
    widened = jnp.concatenate(pieces, axis=0)
    position = lax.axis_index("seq")
    outside = jnp.full((2 * count,), -1, jnp.int32)
    seg_pad = jnp.concatenate([outside, segment_ids, outside], axis=0)
    key_seg = lax.dynamic_slice_in_dim(seg_pad, position * count, 5 * count, 0)
    query_seg = lax.dynamic_slice_in_dim(segment_ids, position * count, count, 0)
    query_heads = query_normed.reshape(count, heads, HEAD_DIM)
    key_heads = widened[:, 0].reshape(5 * count, heads, HEAD_DIM)
    value_heads = widened[:, 1].reshape(5 * count, heads, HEAD_DIM)
    scores, mask = masked_scores(query_heads, key_heads, query_seg, key_seg)
    peak = jnp.max(scores, axis=-1, keepdims=True)
    weights = jnp.where(mask, jnp.exp(scores - peak), 0.0)
    total = jnp.sum(weights, axis=-1)
    probs = weights.astype(jnp.bfloat16)
    summed = jnp.einsum("hqk,khd->qhd", probs, value_heads, preferred_element_type=jnp.float32)
    context = (
        (summed / jnp.transpose(total)[:, :, None]).reshape(count, local_width).astype(jnp.bfloat16)
    )
    blank = jnp.zeros_like(context)
    widened_context = jnp.stack([blank, blank, blank, context], axis=1)
    parts = lax.axis_size("tp")
    chips = parts // 2
    core = lax.axis_index("tp") % 2
    by_owner = gathered.reshape(chips, 2, -1, *gathered.shape[1:])
    terms = jnp.einsum(
        "tkh,ycdkh->cytd", widened_context, by_owner, preferred_element_type=jnp.float32
    )
    outgoing = lax.dynamic_index_in_dim(terms, 1 - core, 0, keepdims=False)
    kept = lax.dynamic_index_in_dim(terms, core, 0, keepdims=False)
    incoming = lax.ppermute(outgoing, "tp", [(i, i ^ 1) for i in range(parts)])
    chip_sums = (kept + incoming).astype(jnp.bfloat16)
    projected = jnp.sum(scatter_chips(chip_sums).astype(jnp.float32), axis=0)
    share = layer_scale.shape[0]
    residual = lax.dynamic_slice_in_dim(source, lax.axis_index("tp") * share, share, 1)
    return (residual + layer_scale * projected).astype(jnp.bfloat16)


def solution(mesh):
    return jax.shard_map(
        shards,
        mesh=mesh,
        in_specs=(
            P("seq", None),
            P(),
            P("seq", None, "tp"),
            P("tp"),
            P("tp"),
            P("tp", "seq"),
            P("tp"),
            P(),
        ),
        out_specs=P("seq", "tp"),
        check_vma=False,
    )
```

```python
import functools

import jax
import jax.numpy as jnp
from jax import lax
from jax.sharding import PartitionSpec as P
from jax.experimental import pallas as pl
from jax.experimental.pallas import tpu as pltpu

HEAD_DIM = 128


eps = 1e-06
floor_score = -1e30


def passed_along(x, axis, by):
    size = lax.axis_size(axis)
    pairs = [(i, i + by) for i in range(size) if 0 <= i + by < size]
    return lax.ppermute(x, axis, pairs)


def gather_kernel(n, x_ref, out_ref, pair_sems, row_sems, ring_sems, local_sem):
    me = lax.axis_index("seq")
    tp = lax.axis_index("tp")
    mesh_id = pl.DeviceIdType.MESH
    pair, row = 2, 4
    slab = pair * row
    rings = n // slab
    low = me % pair
    across = (me // pair) % row
    ring = me // slab
    partner = me - low + (1 - low)
    row_peers = [ring * slab + ((across + k) % row) * pair + low for k in range(1, row)]
    ahead = ((ring + 1) % rings) * slab + me % slab
    behind = ((ring + rings - 1) % rings) * slab + me % slab

    barrier = pltpu.get_barrier_semaphore()
    for peer in [partner, ahead, behind] + row_peers:
        pl.semaphore_signal(barrier, inc=1, device_id=(peer, tp), device_id_type=mesh_id)
    pl.semaphore_wait(barrier, 3 + len(row_peers))

    local = pltpu.make_async_copy(x_ref, out_ref.at[me], local_sem)
    local.start()
    first = pltpu.make_async_remote_copy(
        src_ref=x_ref,
        dst_ref=out_ref.at[me],
        send_sem=pair_sems.at[0],
        recv_sem=pair_sems.at[1],
        device_id=(partner, tp),
        device_id_type=mesh_id,
    )
    first.start()
    local.wait()
    first.wait_send()
    first.wait_recv()

    base = me - low
    second = []
    for k, peer in enumerate(row_peers):
        copy = pltpu.make_async_remote_copy(
            src_ref=out_ref.at[pl.ds(base, pair)],
            dst_ref=out_ref.at[pl.ds(base, pair)],
            send_sem=row_sems.at[0, k],
            recv_sem=row_sems.at[1, k],
            device_id=(peer, tp),
            device_id_type=mesh_id,
        )
        copy.start()
        second.append(copy)
    for copy in second:
        copy.wait_send()
        copy.wait_recv()

    half = slab // 2

    def step(t, carry):
        forward = (ring - t + rings) % rings
        backward = (ring + t) % rings
        window_f = out_ref.at[pl.ds(forward * slab, half)]
        window_b = out_ref.at[pl.ds(backward * slab + half, half)]
        to_ahead = pltpu.make_async_remote_copy(
            src_ref=window_f,
            dst_ref=window_f,
            send_sem=ring_sems.at[0, 0, t],
            recv_sem=ring_sems.at[1, 0, t],
            device_id=(ahead, tp),
            device_id_type=mesh_id,
        )
        to_behind = pltpu.make_async_remote_copy(
            src_ref=window_b,
            dst_ref=window_b,
            send_sem=ring_sems.at[0, 1, t],
            recv_sem=ring_sems.at[1, 1, t],
            device_id=(behind, tp),
            device_id_type=mesh_id,
        )
        to_ahead.start()
        to_behind.start()
        to_ahead.wait_send()
        to_behind.wait_send()
        to_ahead.wait_recv()
        to_behind.wait_recv()
        return carry

    lax.fori_loop(0, rings - 1, step, 0)


def gather_seq(block):
    n = lax.axis_size("seq")
    return pl.pallas_call(
        functools.partial(gather_kernel, n),
        out_shape=jax.ShapeDtypeStruct((n,) + block.shape, block.dtype),
        in_specs=[pl.BlockSpec(memory_space=pl.ANY)],
        out_specs=pl.BlockSpec(memory_space=pl.ANY),
        scratch_shapes=[
            pltpu.SemaphoreType.DMA((2,)),
            pltpu.SemaphoreType.DMA((2, 3)),
            pltpu.SemaphoreType.DMA((2, 2, n // 8)),
            pltpu.SemaphoreType.DMA(()),
        ],
        compiler_params=pltpu.CompilerParams(collective_id=0, has_side_effects=True),
    )(block)


def scatter_kernel(chips, x_ref, out_ref, send_sem, recv_sem, local_sem):
    seq = lax.axis_index("seq")
    tp = lax.axis_index("tp")
    mesh_id = pl.DeviceIdType.MESH
    core = tp % 2
    mine = tp // 2
    owners = [(mine + k) % chips for k in range(1, chips)]

    barrier = pltpu.get_barrier_semaphore()
    for owner in owners:
        pl.semaphore_signal(
            barrier, inc=1, device_id=(seq, owner * 2 + core), device_id_type=mesh_id
        )
    pl.semaphore_wait(barrier, chips - 1)

    local = pltpu.make_async_copy(x_ref.at[mine], out_ref.at[mine], local_sem)
    local.start()
    copies = []
    for k, owner in enumerate(owners):
        copy = pltpu.make_async_remote_copy(
            src_ref=x_ref.at[owner],
            dst_ref=out_ref.at[mine],
            send_sem=send_sem.at[k],
            recv_sem=recv_sem.at[k],
            device_id=(seq, owner * 2 + core),
            device_id_type=mesh_id,
        )
        copy.start()
        copies.append(copy)
    for copy in copies:
        copy.wait_send()
        copy.wait_recv()
    local.wait()


def scatter_chips(block):
    chips = block.shape[0]
    return pl.pallas_call(
        functools.partial(scatter_kernel, chips),
        out_shape=jax.ShapeDtypeStruct(block.shape, block.dtype),
        in_specs=[pl.BlockSpec(memory_space=pl.ANY)],
        out_specs=pl.BlockSpec(memory_space=pl.ANY),
        scratch_shapes=[
            pltpu.SemaphoreType.DMA((chips,)),
            pltpu.SemaphoreType.DMA((chips,)),
            pltpu.SemaphoreType.DMA(()),
        ],
        compiler_params=pltpu.CompilerParams(collective_id=1, has_side_effects=True),
    )(block)


def exchange_kernel(axis, offsets, x_ref, out_ref, send_sem, recv_sem, local_sem):
    size = lax.axis_size(axis)
    me = lax.axis_index(axis)
    seq = lax.axis_index("seq")
    tp = lax.axis_index("tp")
    mesh_id = pl.DeviceIdType.MESH

    def device(position):
        return (position, tp) if axis == "seq" else (seq, position)

    def slot(entry):
        return me if entry is None else entry

    peers = [lax.rem(me + offset + size, size) for offset, _ in offsets]
    barrier = pltpu.get_barrier_semaphore()
    for peer in peers:
        pl.semaphore_signal(barrier, inc=1, device_id=device(peer), device_id_type=mesh_id)
    pl.semaphore_wait(barrier, len(peers))

    own = offsets_own_slot(offsets, me)
    local = pltpu.make_async_copy(x_ref, out_ref.at[own], local_sem)
    local.start()
    copies = []
    for k, ((_, entry), peer) in enumerate(zip(offsets, peers)):
        copy = pltpu.make_async_remote_copy(
            src_ref=x_ref,
            dst_ref=out_ref.at[slot(entry)],
            send_sem=send_sem.at[k],
            recv_sem=recv_sem.at[k],
            device_id=device(peer),
            device_id_type=mesh_id,
        )
        copy.start()
        copies.append(copy)
    for copy in copies:
        copy.wait_send()
        copy.wait_recv()
    local.wait()


def offsets_own_slot(offsets, me):
    slots = [entry for _, entry in offsets]
    if None in slots:
        return me
    return len(offsets) // 2


def exchange(block, axis, offsets, slots, collective_id):
    count = len(offsets)
    return pl.pallas_call(
        functools.partial(exchange_kernel, axis, offsets),
        out_shape=jax.ShapeDtypeStruct((slots,) + block.shape, block.dtype),
        in_specs=[pl.BlockSpec(memory_space=pl.ANY)],
        out_specs=pl.BlockSpec(memory_space=pl.ANY),
        scratch_shapes=[
            pltpu.SemaphoreType.DMA((count,)),
            pltpu.SemaphoreType.DMA((count,)),
            pltpu.SemaphoreType.DMA(()),
        ],
        compiler_params=pltpu.CompilerParams(
            collective_id=collective_id, has_side_effects=True
        ),
    )(block)


def masked_scores(query, keys, query_seg, key_seg):
    scores = jnp.einsum(
        "qhd,khd->hqk", query, keys, preferred_element_type=jnp.float32
    ) * HEAD_DIM ** (-0.5)
    mask = (query_seg[:, None] == key_seg[None, :])[None]
    return (jnp.where(mask, scores, floor_score), mask)


def shards(tokens, norm_gain, qkv_weight, q_gain, k_gain, out_weight, layer_scale, segment_ids):
    count = tokens.shape[0]
    source = tokens.astype(jnp.float32)
    normed = (
        source * lax.rsqrt(jnp.mean(source * source, axis=-1, keepdims=True) + eps) * norm_gain
    ).astype(jnp.bfloat16)
    local_width = qkv_weight.shape[2]
    heads = local_width // HEAD_DIM
    stacked = jnp.concatenate([qkv_weight, jnp.transpose(out_weight)[:, None, :]], axis=1)
    rows, kinds, width = stacked.shape
    gathered = gather_seq(stacked).reshape(-1, kinds, width)
    joined = jnp.einsum(
        "td,dch->tch",
        normed,
        gathered[:, :3],
        preferred_element_type=jnp.float32,
    )
    query = joined[:, 0]
    keys = joined[:, 1]
    values = joined[:, 2]
    parts = lax.axis_size("tp")
    squares = jnp.stack([jnp.sum(query * query, axis=-1), jnp.sum(keys * keys, axis=-1)])
    everyone = [(k, None) for k in range(1, parts)]
    query_sq, key_sq = jnp.sum(exchange(squares, "tp", everyone, parts, 2), axis=0)
    full_width = local_width * lax.axis_size("tp")
    query_normed = (query * lax.rsqrt(query_sq / full_width + eps)[:, None] * q_gain).astype(
        jnp.bfloat16
    )
    key_normed = (keys * lax.rsqrt(key_sq / full_width + eps)[:, None] * k_gain).astype(
        jnp.bfloat16
    )
    paired = jnp.stack([key_normed, values.astype(jnp.bfloat16)], axis=1)
    halo = [(2, 0), (1, 1), (-1, 3), (-2, 4)]
    widened = exchange(paired, "seq", halo, 5, 3).reshape(5 * count, *paired.shape[1:])
    position = lax.axis_index("seq")
    outside = jnp.full((2 * count,), -1, jnp.int32)
    seg_pad = jnp.concatenate([outside, segment_ids, outside], axis=0)
    key_seg = lax.dynamic_slice_in_dim(seg_pad, position * count, 5 * count, 0)
    query_seg = lax.dynamic_slice_in_dim(segment_ids, position * count, count, 0)
    query_heads = query_normed.reshape(count, heads, HEAD_DIM)
    key_heads = widened[:, 0].reshape(5 * count, heads, HEAD_DIM)
    value_heads = widened[:, 1].reshape(5 * count, heads, HEAD_DIM)
    scores, mask = masked_scores(query_heads, key_heads, query_seg, key_seg)
    peak = jnp.max(scores, axis=-1, keepdims=True)
    weights = jnp.where(mask, jnp.exp(scores - peak), 0.0)
    total = jnp.sum(weights, axis=-1)
    probs = weights.astype(jnp.bfloat16)
    summed = jnp.einsum("hqk,khd->qhd", probs, value_heads, preferred_element_type=jnp.float32)
    context = (
        (summed / jnp.transpose(total)[:, :, None]).reshape(count, local_width).astype(jnp.bfloat16)
    )
    blank = jnp.zeros_like(context)
    widened_context = jnp.stack([blank, blank, blank, context], axis=1)
    chips = parts // 2
    core = lax.axis_index("tp") % 2
    by_owner = gathered.reshape(chips, 2, -1, *gathered.shape[1:])
    terms = jnp.einsum(
        "tkh,ycdkh->cytd", widened_context, by_owner, preferred_element_type=jnp.float32
    )
    outgoing = lax.dynamic_index_in_dim(terms, 1 - core, 0, keepdims=False)
    kept = lax.dynamic_index_in_dim(terms, core, 0, keepdims=False)
    incoming = lax.ppermute(outgoing, "tp", [(i, i ^ 1) for i in range(parts)])
    chip_sums = (kept + incoming).astype(jnp.bfloat16)
    projected = jnp.sum(scatter_chips(chip_sums).astype(jnp.float32), axis=0)
    share = layer_scale.shape[0]
    residual = lax.dynamic_slice_in_dim(source, lax.axis_index("tp") * share, share, 1)
    return (residual + layer_scale * projected).astype(jnp.bfloat16)


def solution(mesh):
    return jax.shard_map(
        shards,
        mesh=mesh,
        in_specs=(
            P("seq", None),
            P(),
            P("seq", None, "tp"),
            P("tp"),
            P("tp"),
            P("tp", "seq"),
            P("tp"),
            P(),
        ),
        out_specs=P("seq", "tp"),
        check_vma=False,
    )
```

```python
import functools

import jax
import jax.numpy as jnp
from jax import lax
from jax.sharding import PartitionSpec as P
from jax.experimental import pallas as pl
from jax.experimental.pallas import tpu as pltpu

HEAD_DIM = 128


eps = 1e-06
floor_score = -1e30


def passed_along(x, axis, by):
    size = lax.axis_size(axis)
    pairs = [(i, i + by) for i in range(size) if 0 <= i + by < size]
    return lax.ppermute(x, axis, pairs)


def gather_kernel(x_ref, out_ref, pair_sems, row_sems, lane_sems, ring_sems, cross_sems, local_sem):
    rings, slab = out_ref.shape[0], out_ref.shape[1]
    pair = 2
    row = slab // pair
    lanes = out_ref.shape[-1] // 2
    first_lanes, second_lanes = pl.ds(0, lanes), pl.ds(lanes, lanes)
    me = lax.axis_index("seq")
    tp = lax.axis_index("tp")
    mesh_id = pl.DeviceIdType.MESH
    ring = me // slab
    spot = me % slab
    low = spot % pair
    across = spot // pair
    base = spot - low

    def device(r, s):
        return (r * slab + s, tp)

    ahead = (ring + 1) % rings
    behind = (ring + rings - 1) % rings
    partner = base + 1 - low
    row_spots = [((across + k) % row) * pair + low for k in range(1, row)]
    right = ((across + 1) % row) * pair + low
    left = ((across + row - 1) % row) * pair + low

    barrier = pltpu.get_barrier_semaphore()
    targets = [device(ring, partner), device(ahead, spot), device(behind, spot)]
    targets += [device(ring, s) for s in row_spots]
    for target in targets:
        pl.semaphore_signal(barrier, inc=1, device_id=target, device_id_type=mesh_id)
    pl.semaphore_wait(barrier, len(targets))

    def remote(window, target, sems, index):
        return pltpu.make_async_remote_copy(
            src_ref=window,
            dst_ref=window,
            send_sem=sems.at[(0,) + index],
            recv_sem=sems.at[(1,) + index],
            device_id=target,
            device_id_type=mesh_id,
        )

    def finish(copies):
        for copy in copies:
            copy.wait_send()
            copy.wait_recv()

    local = pltpu.make_async_copy(x_ref, out_ref.at[ring, spot], local_sem)
    local.start()
    swap = pltpu.make_async_remote_copy(
        src_ref=x_ref,
        dst_ref=out_ref.at[ring, spot],
        send_sem=pair_sems.at[0],
        recv_sem=pair_sems.at[1],
        device_id=device(ring, partner),
        device_id_type=mesh_id,
    )
    swap.start()
    local.wait()
    finish([swap])

    pair_a = out_ref.at[ring, pl.ds(base, pair), :, :, first_lanes]
    rows_a = [remote(pair_a, device(ring, s), row_sems, (k,)) for k, s in enumerate(row_spots)]
    for copy in rows_a:
        copy.start()
    for t in range(rings - 1):
        cw = out_ref.at[(ring - t + rings) % rings, base, :, :, second_lanes]
        ccw = out_ref.at[(ring + t) % rings, base + 1, :, :, second_lanes]
        step = [
            remote(cw, device(ahead, spot), lane_sems, (0, t)),
            remote(ccw, device(behind, spot), lane_sems, (1, t)),
        ]
        for copy in step:
            copy.start()
        finish(step)
    finish(rows_a)

    half = slab // 2
    mid = rings // 2
    cross = [
        remote(out_ref.at[:, pl.ds(base, pair), :, :, second_lanes], device(ring, right), cross_sems, (0, 0)),
        remote(out_ref.at[:, pl.ds(base, pair), :, :, second_lanes], device(ring, left), cross_sems, (1, 0)),
    ]
    for copy in cross:
        copy.start()
    onward = None
    for t in range(rings - 1):
        cw = out_ref.at[(ring - t + rings) % rings, pl.ds(0, half), :, :, first_lanes]
        ccw = out_ref.at[(ring + t) % rings, pl.ds(half, half), :, :, first_lanes]
        step = [
            remote(cw, device(ahead, spot), ring_sems, (0, t)),
            remote(ccw, device(behind, spot), ring_sems, (1, t)),
        ]
        for copy in step:
            copy.start()
        finish(step)
        if t == 2:
            finish(cross)
            from_left = ((across + row - 1) % row) * pair
            from_right = ((across + 1) % row) * pair
            onward = [
                remote(
                    out_ref.at[pl.ds(0, mid), pl.ds(from_left, pair), :, :, second_lanes],
                    device(ring, right),
                    cross_sems,
                    (0, 1),
                ),
                remote(
                    out_ref.at[pl.ds(mid, mid), pl.ds(from_right, pair), :, :, second_lanes],
                    device(ring, left),
                    cross_sems,
                    (1, 1),
                ),
            ]
            for copy in onward:
                copy.start()
    finish(onward)


def gather_seq(block, rings, slab):
    return pl.pallas_call(
        gather_kernel,
        out_shape=jax.ShapeDtypeStruct((rings, slab) + block.shape, block.dtype),
        in_specs=[pl.BlockSpec(memory_space=pl.ANY)],
        out_specs=pl.BlockSpec(memory_space=pl.ANY),
        scratch_shapes=[
            pltpu.SemaphoreType.DMA((2,)),
            pltpu.SemaphoreType.DMA((2, slab // 2 - 1)),
            pltpu.SemaphoreType.DMA((2, 2, rings - 1)),
            pltpu.SemaphoreType.DMA((2, 2, rings - 1)),
            pltpu.SemaphoreType.DMA((2, 2, 2)),
            pltpu.SemaphoreType.DMA(()),
        ],
        compiler_params=pltpu.CompilerParams(collective_id=0, has_side_effects=True),
    )(block)


def scatter_kernel(chips, x_ref, out_ref, send_sem, recv_sem, local_sem):
    seq = lax.axis_index("seq")
    tp = lax.axis_index("tp")
    mesh_id = pl.DeviceIdType.MESH
    core = tp % 2
    mine = tp // 2
    owners = [(mine + k) % chips for k in range(1, chips)]

    barrier = pltpu.get_barrier_semaphore()
    for owner in owners:
        pl.semaphore_signal(
            barrier, inc=1, device_id=(seq, owner * 2 + core), device_id_type=mesh_id
        )
    pl.semaphore_wait(barrier, chips - 1)

    local = pltpu.make_async_copy(x_ref.at[mine], out_ref.at[mine], local_sem)
    local.start()
    copies = []
    for k, owner in enumerate(owners):
        copy = pltpu.make_async_remote_copy(
            src_ref=x_ref.at[owner],
            dst_ref=out_ref.at[mine],
            send_sem=send_sem.at[k],
            recv_sem=recv_sem.at[k],
            device_id=(seq, owner * 2 + core),
            device_id_type=mesh_id,
        )
        copy.start()
        copies.append(copy)
    for copy in copies:
        copy.wait_send()
        copy.wait_recv()
    local.wait()


def scatter_chips(block):
    chips = block.shape[0]
    return pl.pallas_call(
        functools.partial(scatter_kernel, chips),
        out_shape=jax.ShapeDtypeStruct(block.shape, block.dtype),
        in_specs=[pl.BlockSpec(memory_space=pl.ANY)],
        out_specs=pl.BlockSpec(memory_space=pl.ANY),
        scratch_shapes=[
            pltpu.SemaphoreType.DMA((chips,)),
            pltpu.SemaphoreType.DMA((chips,)),
            pltpu.SemaphoreType.DMA(()),
        ],
        compiler_params=pltpu.CompilerParams(collective_id=1, has_side_effects=True),
    )(block)


def masked_scores(query, keys, query_seg, key_seg):
    scores = jnp.einsum(
        "qhd,khd->hqk", query, keys, preferred_element_type=jnp.float32
    ) * HEAD_DIM ** (-0.5)
    mask = (query_seg[:, None] == key_seg[None, :])[None]
    return (jnp.where(mask, scores, floor_score), mask)


def shards(tokens, norm_gain, qkv_weight, q_gain, k_gain, out_weight, layer_scale, segment_ids):
    count = tokens.shape[0]
    source = tokens.astype(jnp.float32)
    normed = (
        source * lax.rsqrt(jnp.mean(source * source, axis=-1, keepdims=True) + eps) * norm_gain
    ).astype(jnp.bfloat16)
    local_width = qkv_weight.shape[2]
    heads = local_width // HEAD_DIM
    stacked = jnp.concatenate([qkv_weight, jnp.transpose(out_weight)[:, None, :]], axis=1)
    rows, kinds, width = stacked.shape
    slab = 8
    gathered = gather_seq(stacked, lax.axis_size("seq") // slab, slab).reshape(-1, kinds, width)
    joined = jnp.einsum(
        "td,dch->tch",
        normed,
        gathered[:, :3],
        preferred_element_type=jnp.float32,
    )
    query = joined[:, 0]
    keys = joined[:, 1]
    values = joined[:, 2]
    query_sq, key_sq = lax.psum(
        (jnp.sum(query * query, axis=-1), jnp.sum(keys * keys, axis=-1)), "tp"
    )
    full_width = local_width * lax.axis_size("tp")
    query_normed = (query * lax.rsqrt(query_sq / full_width + eps)[:, None] * q_gain).astype(
        jnp.bfloat16
    )
    key_normed = (keys * lax.rsqrt(key_sq / full_width + eps)[:, None] * k_gain).astype(
        jnp.bfloat16
    )
    paired = jnp.stack([key_normed, values.astype(jnp.bfloat16)], axis=1)
    pieces = []
    for offset in (2, 1, 0, -1, -2):
        if offset == 0:
            pieces.append(paired)
        else:
            pieces.append(passed_along(paired, "seq", offset))
    widened = jnp.concatenate(pieces, axis=0)
    position = lax.axis_index("seq")
    outside = jnp.full((2 * count,), -1, jnp.int32)
    seg_pad = jnp.concatenate([outside, segment_ids, outside], axis=0)
    key_seg = lax.dynamic_slice_in_dim(seg_pad, position * count, 5 * count, 0)
    query_seg = lax.dynamic_slice_in_dim(segment_ids, position * count, count, 0)
    query_heads = query_normed.reshape(count, heads, HEAD_DIM)
    key_heads = widened[:, 0].reshape(5 * count, heads, HEAD_DIM)
    value_heads = widened[:, 1].reshape(5 * count, heads, HEAD_DIM)
    scores, mask = masked_scores(query_heads, key_heads, query_seg, key_seg)
    peak = jnp.max(scores, axis=-1, keepdims=True)
    weights = jnp.where(mask, jnp.exp(scores - peak), 0.0)
    total = jnp.sum(weights, axis=-1)
    probs = weights.astype(jnp.bfloat16)
    summed = jnp.einsum("hqk,khd->qhd", probs, value_heads, preferred_element_type=jnp.float32)
    context = (
        (summed / jnp.transpose(total)[:, :, None]).reshape(count, local_width).astype(jnp.bfloat16)
    )
    blank = jnp.zeros_like(context)
    widened_context = jnp.stack([blank, blank, blank, context], axis=1)
    parts = lax.axis_size("tp")
    chips = parts // 2
    core = lax.axis_index("tp") % 2
    by_owner = gathered.reshape(chips, 2, -1, *gathered.shape[1:])
    terms = jnp.einsum(
        "tkh,ycdkh->cytd", widened_context, by_owner, preferred_element_type=jnp.float32
    )
    outgoing = lax.dynamic_index_in_dim(terms, 1 - core, 0, keepdims=False)
    kept = lax.dynamic_index_in_dim(terms, core, 0, keepdims=False)
    incoming = lax.ppermute(outgoing, "tp", [(i, i ^ 1) for i in range(parts)])
    chip_sums = (kept + incoming).astype(jnp.bfloat16)
    projected = jnp.sum(scatter_chips(chip_sums).astype(jnp.float32), axis=0)
    share = layer_scale.shape[0]
    residual = lax.dynamic_slice_in_dim(source, lax.axis_index("tp") * share, share, 1)
    return (residual + layer_scale * projected).astype(jnp.bfloat16)


def solution(mesh):
    return jax.shard_map(
        shards,
        mesh=mesh,
        in_specs=(
            P("seq", None),
            P(),
            P("seq", None, "tp"),
            P("tp"),
            P("tp"),
            P("tp", "seq"),
            P("tp"),
            P(),
        ),
        out_specs=P("seq", "tp"),
        check_vma=False,
    )
```

```python
import functools

import jax
import jax.numpy as jnp
from jax import lax
from jax.sharding import PartitionSpec as P
from jax.experimental import pallas as pl
from jax.experimental.pallas import tpu as pltpu

HEAD_DIM = 128


eps = 1e-06
floor_score = -1e30


def passed_along(x, axis, by):
    size = lax.axis_size(axis)
    pairs = [(i, i + by) for i in range(size) if 0 <= i + by < size]
    return lax.ppermute(x, axis, pairs)


def gather_kernel(x_ref, out_ref, pair_sems, row_sems, lane_sems, ring_sems, cross_sems, local_sem):
    rings, slab = out_ref.shape[0], out_ref.shape[1]
    pair = 2
    row = slab // pair
    lanes = out_ref.shape[-1] // 2
    first_lanes, second_lanes = pl.ds(0, lanes), pl.ds(lanes, lanes)
    me = lax.axis_index("seq")
    tp = lax.axis_index("tp")
    mesh_id = pl.DeviceIdType.MESH
    ring = me // slab
    spot = me % slab
    low = spot % pair
    across = spot // pair
    base = spot - low

    def device(r, s):
        return (r * slab + s, tp)

    ahead = (ring + 1) % rings
    behind = (ring + rings - 1) % rings
    partner = base + 1 - low
    row_spots = [((across + k) % row) * pair + low for k in range(1, row)]
    right = ((across + 1) % row) * pair + low
    left = ((across + row - 1) % row) * pair + low

    barrier = pltpu.get_barrier_semaphore()
    targets = [device(ring, partner), device(ahead, spot), device(behind, spot)]
    targets += [device(ring, s) for s in row_spots]
    for target in targets:
        pl.semaphore_signal(barrier, inc=1, device_id=target, device_id_type=mesh_id)
    pl.semaphore_wait(barrier, len(targets))

    def remote(window, target, sems, index):
        return pltpu.make_async_remote_copy(
            src_ref=window,
            dst_ref=window,
            send_sem=sems.at[(0,) + index],
            recv_sem=sems.at[(1,) + index],
            device_id=target,
            device_id_type=mesh_id,
        )

    def finish(copies):
        for copy in copies:
            copy.wait_send()
            copy.wait_recv()

    local = pltpu.make_async_copy(x_ref, out_ref.at[ring, spot], local_sem)
    local.start()
    swap = pltpu.make_async_remote_copy(
        src_ref=x_ref,
        dst_ref=out_ref.at[ring, spot],
        send_sem=pair_sems.at[0],
        recv_sem=pair_sems.at[1],
        device_id=device(ring, partner),
        device_id_type=mesh_id,
    )
    swap.start()
    local.wait()
    finish([swap])

    pair_a = out_ref.at[ring, pl.ds(base, pair), :, :, first_lanes]
    rows_a = [remote(pair_a, device(ring, s), row_sems, (k,)) for k, s in enumerate(row_spots)]
    for copy in rows_a:
        copy.start()
    for t in range(rings - 1):
        cw = out_ref.at[(ring - t + rings) % rings, base, :, :, second_lanes]
        ccw = out_ref.at[(ring + t) % rings, base + 1, :, :, second_lanes]
        step = [
            remote(cw, device(ahead, spot), lane_sems, (0, t)),
            remote(ccw, device(behind, spot), lane_sems, (1, t)),
        ]
        for copy in step:
            copy.start()
        finish(step)
    finish(rows_a)

    half = slab // 2
    mid = rings // 2
    cross = [
        remote(out_ref.at[:, pl.ds(base, pair), :, :, second_lanes], device(ring, right), cross_sems, (0, 0)),
        remote(out_ref.at[:, pl.ds(base, pair), :, :, second_lanes], device(ring, left), cross_sems, (1, 0)),
    ]
    for copy in cross:
        copy.start()
    onward = None
    for t in range(rings - 1):
        cw = out_ref.at[(ring - t + rings) % rings, pl.ds(0, half), :, :, first_lanes]
        ccw = out_ref.at[(ring + t) % rings, pl.ds(half, half), :, :, first_lanes]
        step = [
            remote(cw, device(ahead, spot), ring_sems, (0, t)),
            remote(ccw, device(behind, spot), ring_sems, (1, t)),
        ]
        for copy in step:
            copy.start()
        finish(step)
        if t == 2:
            finish(cross)
            from_left = ((across + row - 1) % row) * pair
            from_right = ((across + 1) % row) * pair
            onward = [
                remote(
                    out_ref.at[pl.ds(0, mid), pl.ds(from_left, pair), :, :, second_lanes],
                    device(ring, right),
                    cross_sems,
                    (0, 1),
                ),
                remote(
                    out_ref.at[pl.ds(mid, mid), pl.ds(from_right, pair), :, :, second_lanes],
                    device(ring, left),
                    cross_sems,
                    (1, 1),
                ),
            ]
            for copy in onward:
                copy.start()
    finish(onward)


def gather_seq(block, rings, slab):
    return pl.pallas_call(
        gather_kernel,
        out_shape=jax.ShapeDtypeStruct((rings, slab) + block.shape, block.dtype),
        in_specs=[pl.BlockSpec(memory_space=pl.ANY)],
        out_specs=pl.BlockSpec(memory_space=pl.ANY),
        scratch_shapes=[
            pltpu.SemaphoreType.DMA((2,)),
            pltpu.SemaphoreType.DMA((2, slab // 2 - 1)),
            pltpu.SemaphoreType.DMA((2, 2, rings - 1)),
            pltpu.SemaphoreType.DMA((2, 2, rings - 1)),
            pltpu.SemaphoreType.DMA((2, 2, 2)),
            pltpu.SemaphoreType.DMA(()),
        ],
        compiler_params=pltpu.CompilerParams(collective_id=0, has_side_effects=True),
    )(block)


def scatter_kernel(terms_ref, out_ref, mine, incoming, sums, send_sem, recv_sem, local_sems):
    chips = out_ref.shape[0]
    seq = lax.axis_index("seq")
    tp = lax.axis_index("tp")
    mesh_id = pl.DeviceIdType.MESH
    core = tp % 2
    here = tp // 2
    owners = [(here + k) % chips for k in range(1, chips)]
    targets = [(seq, tp + 1 - 2 * core)] + [(seq, owner * 2 + core) for owner in owners]

    barrier = pltpu.get_barrier_semaphore()
    for target in targets:
        pl.semaphore_signal(barrier, inc=1, device_id=target, device_id_type=mesh_id)
    pl.semaphore_wait(barrier, len(targets))

    keep = pltpu.make_async_copy(terms_ref.at[core], mine, local_sems.at[0])
    keep.start()
    swap = pltpu.make_async_remote_copy(
        src_ref=terms_ref.at[1 - core],
        dst_ref=incoming,
        send_sem=send_sem.at[0],
        recv_sem=recv_sem.at[0],
        device_id=targets[0],
        device_id_type=mesh_id,
    )
    swap.start()
    keep.wait()
    swap.wait_send()
    swap.wait_recv()
    sums[...] = (mine[...] + incoming[...]).astype(sums.dtype)

    local = pltpu.make_async_copy(sums.at[here], out_ref.at[here], local_sems.at[1])
    local.start()
    copies = []
    for k, owner in enumerate(owners):
        copy = pltpu.make_async_remote_copy(
            src_ref=sums.at[owner],
            dst_ref=out_ref.at[here],
            send_sem=send_sem.at[k + 1],
            recv_sem=recv_sem.at[k + 1],
            device_id=targets[k + 1],
            device_id_type=mesh_id,
        )
        copy.start()
        copies.append(copy)
    for copy in copies:
        copy.wait_send()
        copy.wait_recv()
    local.wait()


def scatter_chips(terms):
    block = terms.shape[1:]
    chips = block[0]
    return pl.pallas_call(
        scatter_kernel,
        out_shape=jax.ShapeDtypeStruct(block, jnp.bfloat16),
        in_specs=[pl.BlockSpec(memory_space=pl.ANY)],
        out_specs=pl.BlockSpec(memory_space=pl.ANY),
        scratch_shapes=[
            pltpu.VMEM(block, jnp.float32),
            pltpu.VMEM(block, jnp.float32),
            pltpu.VMEM(block, jnp.bfloat16),
            pltpu.SemaphoreType.DMA((chips,)),
            pltpu.SemaphoreType.DMA((chips,)),
            pltpu.SemaphoreType.DMA((2,)),
        ],
        compiler_params=pltpu.CompilerParams(collective_id=1, has_side_effects=True),
    )(terms)


def masked_scores(query, keys, query_seg, key_seg):
    scores = jnp.einsum(
        "qhd,khd->hqk", query, keys, preferred_element_type=jnp.float32
    ) * HEAD_DIM ** (-0.5)
    mask = (query_seg[:, None] == key_seg[None, :])[None]
    return (jnp.where(mask, scores, floor_score), mask)


def shards(tokens, norm_gain, qkv_weight, q_gain, k_gain, out_weight, layer_scale, segment_ids):
    count = tokens.shape[0]
    source = tokens.astype(jnp.float32)
    normed = (
        source * lax.rsqrt(jnp.mean(source * source, axis=-1, keepdims=True) + eps) * norm_gain
    ).astype(jnp.bfloat16)
    local_width = qkv_weight.shape[2]
    heads = local_width // HEAD_DIM
    stacked = jnp.concatenate([qkv_weight, jnp.transpose(out_weight)[:, None, :]], axis=1)
    rows, kinds, width = stacked.shape
    slab = 8
    gathered = gather_seq(stacked, lax.axis_size("seq") // slab, slab).reshape(-1, kinds, width)
    joined = jnp.einsum(
        "td,dch->tch",
        normed,
        gathered[:, :3],
        preferred_element_type=jnp.float32,
    )
    query = joined[:, 0]
    keys = joined[:, 1]
    values = joined[:, 2]
    query_sq, key_sq = lax.psum(
        (jnp.sum(query * query, axis=-1), jnp.sum(keys * keys, axis=-1)), "tp"
    )
    full_width = local_width * lax.axis_size("tp")
    query_normed = (query * lax.rsqrt(query_sq / full_width + eps)[:, None] * q_gain).astype(
        jnp.bfloat16
    )
    key_normed = (keys * lax.rsqrt(key_sq / full_width + eps)[:, None] * k_gain).astype(
        jnp.bfloat16
    )
    paired = jnp.stack([key_normed, values.astype(jnp.bfloat16)], axis=1)
    pieces = []
    for offset in (2, 1, 0, -1, -2):
        if offset == 0:
            pieces.append(paired)
        else:
            pieces.append(passed_along(paired, "seq", offset))
    widened = jnp.concatenate(pieces, axis=0)
    position = lax.axis_index("seq")
    outside = jnp.full((2 * count,), -1, jnp.int32)
    seg_pad = jnp.concatenate([outside, segment_ids, outside], axis=0)
    key_seg = lax.dynamic_slice_in_dim(seg_pad, position * count, 5 * count, 0)
    query_seg = lax.dynamic_slice_in_dim(segment_ids, position * count, count, 0)
    query_heads = query_normed.reshape(count, heads, HEAD_DIM)
    key_heads = widened[:, 0].reshape(5 * count, heads, HEAD_DIM)
    value_heads = widened[:, 1].reshape(5 * count, heads, HEAD_DIM)
    scores, mask = masked_scores(query_heads, key_heads, query_seg, key_seg)
    peak = jnp.max(scores, axis=-1, keepdims=True)
    weights = jnp.where(mask, jnp.exp(scores - peak), 0.0)
    total = jnp.sum(weights, axis=-1)
    probs = weights.astype(jnp.bfloat16)
    summed = jnp.einsum("hqk,khd->qhd", probs, value_heads, preferred_element_type=jnp.float32)
    context = (
        (summed / jnp.transpose(total)[:, :, None]).reshape(count, local_width).astype(jnp.bfloat16)
    )
    blank = jnp.zeros_like(context)
    widened_context = jnp.stack([blank, blank, blank, context], axis=1)
    parts = lax.axis_size("tp")
    chips = parts // 2
    by_owner = gathered.reshape(chips, 2, -1, *gathered.shape[1:])
    terms = jnp.einsum(
        "tkh,ycdkh->cytd", widened_context, by_owner, preferred_element_type=jnp.float32
    )
    projected = jnp.sum(scatter_chips(terms).astype(jnp.float32), axis=0)
    share = layer_scale.shape[0]
    residual = lax.dynamic_slice_in_dim(source, lax.axis_index("tp") * share, share, 1)
    return (residual + layer_scale * projected).astype(jnp.bfloat16)


def solution(mesh):
    return jax.shard_map(
        shards,
        mesh=mesh,
        in_specs=(
            P("seq", None),
            P(),
            P("seq", None, "tp"),
            P("tp"),
            P("tp"),
            P("tp", "seq"),
            P("tp"),
            P(),
        ),
        out_specs=P("seq", "tp"),
        check_vma=False,
    )
```

```python
import functools

import jax
import jax.numpy as jnp
from jax import lax
from jax.sharding import PartitionSpec as P
from jax.experimental import pallas as pl
from jax.experimental.pallas import tpu as pltpu

HEAD_DIM = 128


eps = 1e-06
floor_score = -1e30


def passed_along(x, axis, by):
    size = lax.axis_size(axis)
    pairs = [(i, i + by) for i in range(size) if 0 <= i + by < size]
    return lax.ppermute(x, axis, pairs)


def gather_kernel(x_ref, out_ref, pair_sems, row_sems, lane_sems, ring_sems, cross_sems, local_sem):
    rings, slab = out_ref.shape[0], out_ref.shape[1]
    pair = 2
    row = slab // pair
    lanes = out_ref.shape[-1] // 2
    first_lanes, second_lanes = pl.ds(0, lanes), pl.ds(lanes, lanes)
    me = lax.axis_index("seq")
    tp = lax.axis_index("tp")
    mesh_id = pl.DeviceIdType.MESH
    ring = me // slab
    spot = me % slab
    low = spot % pair
    across = spot // pair
    base = spot - low

    def device(r, s):
        return (r * slab + s, tp)

    ahead = (ring + 1) % rings
    behind = (ring + rings - 1) % rings
    partner = base + 1 - low
    row_spots = [((across + k) % row) * pair + low for k in range(1, row)]
    right = ((across + 1) % row) * pair + low
    left = ((across + row - 1) % row) * pair + low

    barrier = pltpu.get_barrier_semaphore()
    targets = [device(ring, partner), device(ahead, spot), device(behind, spot)]
    targets += [device(ring, s) for s in row_spots]
    for target in targets:
        pl.semaphore_signal(barrier, inc=1, device_id=target, device_id_type=mesh_id)
    pl.semaphore_wait(barrier, len(targets))

    def remote(window, target, sems, index):
        return pltpu.make_async_remote_copy(
            src_ref=window,
            dst_ref=window,
            send_sem=sems.at[(0,) + index],
            recv_sem=sems.at[(1,) + index],
            device_id=target,
            device_id_type=mesh_id,
        )

    def finish(copies):
        for copy in copies:
            copy.wait_send()
            copy.wait_recv()

    local = pltpu.make_async_copy(x_ref, out_ref.at[ring, spot], local_sem)
    local.start()
    swap = pltpu.make_async_remote_copy(
        src_ref=x_ref,
        dst_ref=out_ref.at[ring, spot],
        send_sem=pair_sems.at[0],
        recv_sem=pair_sems.at[1],
        device_id=device(ring, partner),
        device_id_type=mesh_id,
    )
    swap.start()
    local.wait()
    finish([swap])

    pair_a = out_ref.at[ring, pl.ds(base, pair), :, :, first_lanes]
    rows_a = [remote(pair_a, device(ring, s), row_sems, (k,)) for k, s in enumerate(row_spots)]
    for copy in rows_a:
        copy.start()
    for t in range(rings - 1):
        cw = out_ref.at[(ring - t + rings) % rings, base, :, :, second_lanes]
        ccw = out_ref.at[(ring + t) % rings, base + 1, :, :, second_lanes]
        step = [
            remote(cw, device(ahead, spot), lane_sems, (0, t)),
            remote(ccw, device(behind, spot), lane_sems, (1, t)),
        ]
        for copy in step:
            copy.start()
        finish(step)
    finish(rows_a)

    half = slab // 2
    mid = rings // 2
    cross = [
        remote(out_ref.at[:, pl.ds(base, pair), :, :, second_lanes], device(ring, right), cross_sems, (0, 0)),
        remote(out_ref.at[:, pl.ds(base, pair), :, :, second_lanes], device(ring, left), cross_sems, (1, 0)),
    ]
    for copy in cross:
        copy.start()
    onward = None
    for t in range(rings - 1):
        cw = out_ref.at[(ring - t + rings) % rings, pl.ds(0, half), :, :, first_lanes]
        ccw = out_ref.at[(ring + t) % rings, pl.ds(half, half), :, :, first_lanes]
        step = [
            remote(cw, device(ahead, spot), ring_sems, (0, t)),
            remote(ccw, device(behind, spot), ring_sems, (1, t)),
        ]
        for copy in step:
            copy.start()
        finish(step)
        if t == 2:
            finish(cross)
            from_left = ((across + row - 1) % row) * pair
            from_right = ((across + 1) % row) * pair
            onward = [
                remote(
                    out_ref.at[pl.ds(0, mid), pl.ds(from_left, pair), :, :, second_lanes],
                    device(ring, right),
                    cross_sems,
                    (0, 1),
                ),
                remote(
                    out_ref.at[pl.ds(mid, mid), pl.ds(from_right, pair), :, :, second_lanes],
                    device(ring, left),
                    cross_sems,
                    (1, 1),
                ),
            ]
            for copy in onward:
                copy.start()
    finish(onward)


def gather_seq(block, rings, slab):
    return pl.pallas_call(
        gather_kernel,
        out_shape=jax.ShapeDtypeStruct((rings, slab) + block.shape, block.dtype),
        in_specs=[pl.BlockSpec(memory_space=pl.ANY)],
        out_specs=pl.BlockSpec(memory_space=pl.ANY),
        scratch_shapes=[
            pltpu.SemaphoreType.DMA((2,)),
            pltpu.SemaphoreType.DMA((2, slab // 2 - 1)),
            pltpu.SemaphoreType.DMA((2, 2, rings - 1)),
            pltpu.SemaphoreType.DMA((2, 2, rings - 1)),
            pltpu.SemaphoreType.DMA((2, 2, 2)),
            pltpu.SemaphoreType.DMA(()),
        ],
        compiler_params=pltpu.CompilerParams(collective_id=0, has_side_effects=True),
    )(block)


def scatter_kernel(terms_ref, out_ref, mine, incoming, sums, send_sem, recv_sem, local_sems):
    chips = out_ref.shape[0]
    seq = lax.axis_index("seq")
    tp = lax.axis_index("tp")
    mesh_id = pl.DeviceIdType.MESH
    core = tp % 2
    here = tp // 2
    owners = [(here + k) % chips for k in range(1, chips)]
    targets = [(seq, tp + 1 - 2 * core)] + [(seq, owner * 2 + core) for owner in owners]

    barrier = pltpu.get_barrier_semaphore()
    for target in targets:
        pl.semaphore_signal(barrier, inc=1, device_id=target, device_id_type=mesh_id)
    pl.semaphore_wait(barrier, len(targets))

    keep = pltpu.make_async_copy(terms_ref.at[core], mine, local_sems.at[0])
    keep.start()
    swap = pltpu.make_async_remote_copy(
        src_ref=terms_ref.at[1 - core],
        dst_ref=incoming,
        send_sem=send_sem.at[0],
        recv_sem=recv_sem.at[0],
        device_id=targets[0],
        device_id_type=mesh_id,
    )
    swap.start()
    keep.wait()
    swap.wait_send()
    swap.wait_recv()
    sums[...] = (mine[...] + incoming[...]).astype(sums.dtype)

    local = pltpu.make_async_copy(sums.at[here], out_ref.at[here], local_sems.at[1])
    local.start()
    copies = []
    for k, owner in enumerate(owners):
        copy = pltpu.make_async_remote_copy(
            src_ref=sums.at[owner],
            dst_ref=out_ref.at[here],
            send_sem=send_sem.at[k + 1],
            recv_sem=recv_sem.at[k + 1],
            device_id=targets[k + 1],
            device_id_type=mesh_id,
        )
        copy.start()
        copies.append(copy)
    for copy in copies:
        copy.wait_send()
        copy.wait_recv()
    local.wait()


def scatter_chips(terms):
    block = terms.shape[1:]
    chips = block[0]
    return pl.pallas_call(
        scatter_kernel,
        out_shape=jax.ShapeDtypeStruct(block, jnp.bfloat16),
        in_specs=[pl.BlockSpec(memory_space=pl.ANY)],
        out_specs=pl.BlockSpec(memory_space=pl.ANY),
        scratch_shapes=[
            pltpu.VMEM(block, jnp.float32),
            pltpu.VMEM(block, jnp.float32),
            pltpu.VMEM(block, jnp.bfloat16),
            pltpu.SemaphoreType.DMA((chips,)),
            pltpu.SemaphoreType.DMA((chips,)),
            pltpu.SemaphoreType.DMA((2,)),
        ],
        compiler_params=pltpu.CompilerParams(collective_id=1, has_side_effects=True),
    )(terms)


def exchange_kernel(axis, offsets, x_ref, out_ref, send_sem, recv_sem, local_sem):
    size = lax.axis_size(axis)
    me = lax.axis_index(axis)
    seq = lax.axis_index("seq")
    tp = lax.axis_index("tp")
    mesh_id = pl.DeviceIdType.MESH

    def device(position):
        return (position, tp) if axis == "seq" else (seq, position)

    def slot(entry):
        return me if entry is None else entry

    peers = [lax.rem(me + offset + size, size) for offset, _ in offsets]
    barrier = pltpu.get_barrier_semaphore()
    for peer in peers:
        pl.semaphore_signal(barrier, inc=1, device_id=device(peer), device_id_type=mesh_id)
    pl.semaphore_wait(barrier, len(peers))

    own = offsets_own_slot(offsets, me)
    local = pltpu.make_async_copy(x_ref, out_ref.at[own], local_sem)
    local.start()
    copies = []
    for k, ((_, entry), peer) in enumerate(zip(offsets, peers)):
        copy = pltpu.make_async_remote_copy(
            src_ref=x_ref,
            dst_ref=out_ref.at[slot(entry)],
            send_sem=send_sem.at[k],
            recv_sem=recv_sem.at[k],
            device_id=device(peer),
            device_id_type=mesh_id,
        )
        copy.start()
        copies.append(copy)
    for copy in copies:
        copy.wait_send()
        copy.wait_recv()
    local.wait()


def offsets_own_slot(offsets, me):
    slots = [entry for _, entry in offsets]
    if None in slots:
        return me
    return len(offsets) // 2


def exchange(block, axis, offsets, slots, collective_id):
    count = len(offsets)
    return pl.pallas_call(
        functools.partial(exchange_kernel, axis, offsets),
        out_shape=jax.ShapeDtypeStruct((slots,) + block.shape, block.dtype),
        in_specs=[pl.BlockSpec(memory_space=pl.ANY)],
        out_specs=pl.BlockSpec(memory_space=pl.ANY),
        scratch_shapes=[
            pltpu.SemaphoreType.DMA((count,)),
            pltpu.SemaphoreType.DMA((count,)),
            pltpu.SemaphoreType.DMA(()),
        ],
        compiler_params=pltpu.CompilerParams(
            collective_id=collective_id, has_side_effects=True
        ),
    )(block)


def masked_scores(query, keys, query_seg, key_seg):
    scores = jnp.einsum(
        "qhd,khd->hqk", query, keys, preferred_element_type=jnp.float32
    ) * HEAD_DIM ** (-0.5)
    mask = (query_seg[:, None] == key_seg[None, :])[None]
    return (jnp.where(mask, scores, floor_score), mask)


def shards(tokens, norm_gain, qkv_weight, q_gain, k_gain, out_weight, layer_scale, segment_ids):
    count = tokens.shape[0]
    source = tokens.astype(jnp.float32)
    normed = (
        source * lax.rsqrt(jnp.mean(source * source, axis=-1, keepdims=True) + eps) * norm_gain
    ).astype(jnp.bfloat16)
    local_width = qkv_weight.shape[2]
    heads = local_width // HEAD_DIM
    stacked = jnp.concatenate([qkv_weight, jnp.transpose(out_weight)[:, None, :]], axis=1)
    rows, kinds, width = stacked.shape
    slab = 8
    gathered = gather_seq(stacked, lax.axis_size("seq") // slab, slab).reshape(-1, kinds, width)
    joined = jnp.einsum(
        "td,dch->tch",
        normed,
        gathered[:, :3],
        preferred_element_type=jnp.float32,
    )
    query = joined[:, 0]
    keys = joined[:, 1]
    values = joined[:, 2]
    parts = lax.axis_size("tp")
    squares = jnp.stack([jnp.sum(query * query, axis=-1), jnp.sum(keys * keys, axis=-1)])
    everyone = [(k, None) for k in range(1, parts)]
    query_sq, key_sq = jnp.sum(exchange(squares, "tp", everyone, parts, 2), axis=0)
    full_width = local_width * lax.axis_size("tp")
    query_normed = (query * lax.rsqrt(query_sq / full_width + eps)[:, None] * q_gain).astype(
        jnp.bfloat16
    )
    key_normed = (keys * lax.rsqrt(key_sq / full_width + eps)[:, None] * k_gain).astype(
        jnp.bfloat16
    )
    paired = jnp.stack([key_normed, values.astype(jnp.bfloat16)], axis=1)
    pieces = []
    for offset in (2, 1, 0, -1, -2):
        if offset == 0:
            pieces.append(paired)
        else:
            pieces.append(passed_along(paired, "seq", offset))
    widened = jnp.concatenate(pieces, axis=0)
    position = lax.axis_index("seq")
    outside = jnp.full((2 * count,), -1, jnp.int32)
    seg_pad = jnp.concatenate([outside, segment_ids, outside], axis=0)
    key_seg = lax.dynamic_slice_in_dim(seg_pad, position * count, 5 * count, 0)
    query_seg = lax.dynamic_slice_in_dim(segment_ids, position * count, count, 0)
    query_heads = query_normed.reshape(count, heads, HEAD_DIM)
    key_heads = widened[:, 0].reshape(5 * count, heads, HEAD_DIM)
    value_heads = widened[:, 1].reshape(5 * count, heads, HEAD_DIM)
    scores, mask = masked_scores(query_heads, key_heads, query_seg, key_seg)
    peak = jnp.max(scores, axis=-1, keepdims=True)
    weights = jnp.where(mask, jnp.exp(scores - peak), 0.0)
    total = jnp.sum(weights, axis=-1)
    probs = weights.astype(jnp.bfloat16)
    summed = jnp.einsum("hqk,khd->qhd", probs, value_heads, preferred_element_type=jnp.float32)
    context = (
        (summed / jnp.transpose(total)[:, :, None]).reshape(count, local_width).astype(jnp.bfloat16)
    )
    blank = jnp.zeros_like(context)
    widened_context = jnp.stack([blank, blank, blank, context], axis=1)
    chips = parts // 2
    by_owner = gathered.reshape(chips, 2, -1, *gathered.shape[1:])
    terms = jnp.einsum(
        "tkh,ycdkh->cytd", widened_context, by_owner, preferred_element_type=jnp.float32
    )
    projected = jnp.sum(scatter_chips(terms).astype(jnp.float32), axis=0)
    share = layer_scale.shape[0]
    residual = lax.dynamic_slice_in_dim(source, lax.axis_index("tp") * share, share, 1)
    return (residual + layer_scale * projected).astype(jnp.bfloat16)


def solution(mesh):
    return jax.shard_map(
        shards,
        mesh=mesh,
        in_specs=(
            P("seq", None),
            P(),
            P("seq", None, "tp"),
            P("tp"),
            P("tp"),
            P("tp", "seq"),
            P("tp"),
            P(),
        ),
        out_specs=P("seq", "tp"),
        check_vma=False,
    )
```

```python
import functools

import jax
import jax.numpy as jnp
from jax import lax
from jax.sharding import PartitionSpec as P
from jax.experimental import pallas as pl
from jax.experimental.pallas import tpu as pltpu

HEAD_DIM = 128


eps = 1e-06
floor_score = -1e30


def passed_along(x, axis, by):
    size = lax.axis_size(axis)
    pairs = [(i, i + by) for i in range(size) if 0 <= i + by < size]
    return lax.ppermute(x, axis, pairs)


def gather_kernel(x_ref, out_ref, pair_sems, row_sems, lane_sems, ring_sems, cross_sems, local_sem):
    rings, slab = out_ref.shape[0], out_ref.shape[1]
    pair = 2
    row = slab // pair
    lanes = out_ref.shape[-1] // 2
    first_lanes, second_lanes = pl.ds(0, lanes), pl.ds(lanes, lanes)
    me = lax.axis_index("seq")
    tp = lax.axis_index("tp")
    mesh_id = pl.DeviceIdType.MESH
    ring = me // slab
    spot = me % slab
    low = spot % pair
    across = spot // pair
    base = spot - low

    def device(r, s):
        return (r * slab + s, tp)

    ahead = (ring + 1) % rings
    behind = (ring + rings - 1) % rings
    partner = base + 1 - low
    row_spots = [((across + k) % row) * pair + low for k in range(1, row)]
    right = ((across + 1) % row) * pair + low
    left = ((across + row - 1) % row) * pair + low

    barrier = pltpu.get_barrier_semaphore()
    targets = [device(ring, partner), device(ahead, spot), device(behind, spot)]
    targets += [device(ring, s) for s in row_spots]
    for target in targets:
        pl.semaphore_signal(barrier, inc=1, device_id=target, device_id_type=mesh_id)
    pl.semaphore_wait(barrier, len(targets))

    def remote(window, target, sems, index):
        return pltpu.make_async_remote_copy(
            src_ref=window,
            dst_ref=window,
            send_sem=sems.at[(0,) + index],
            recv_sem=sems.at[(1,) + index],
            device_id=target,
            device_id_type=mesh_id,
        )

    def finish(copies):
        for copy in copies:
            copy.wait_send()
            copy.wait_recv()

    local = pltpu.make_async_copy(x_ref, out_ref.at[ring, spot], local_sem)
    local.start()
    swap = pltpu.make_async_remote_copy(
        src_ref=x_ref,
        dst_ref=out_ref.at[ring, spot],
        send_sem=pair_sems.at[0],
        recv_sem=pair_sems.at[1],
        device_id=device(ring, partner),
        device_id_type=mesh_id,
    )
    swap.start()
    local.wait()
    finish([swap])

    pair_a = out_ref.at[ring, pl.ds(base, pair), :, :, first_lanes]
    rows_a = [remote(pair_a, device(ring, s), row_sems, (k,)) for k, s in enumerate(row_spots)]
    for copy in rows_a:
        copy.start()
    for t in range(rings // 2):
        last = t == rings // 2 - 1
        cw_spots = pl.ds(base, 1 if last else pair)
        ccw_spots = pl.ds(base + 1 if last else base, 1 if last else pair)
        cw = out_ref.at[(ring - t + rings) % rings, cw_spots, :, :, second_lanes]
        ccw = out_ref.at[(ring + t) % rings, ccw_spots, :, :, second_lanes]
        step = [
            remote(cw, device(ahead, spot), lane_sems, (0, t)),
            remote(ccw, device(behind, spot), lane_sems, (1, t)),
        ]
        for copy in step:
            copy.start()
        finish(step)
    finish(rows_a)

    half = slab // 2
    mid = rings // 2
    cross = [
        remote(out_ref.at[:, pl.ds(base, pair), :, :, second_lanes], device(ring, right), cross_sems, (0, 0)),
        remote(out_ref.at[:, pl.ds(base, pair), :, :, second_lanes], device(ring, left), cross_sems, (1, 0)),
    ]
    for copy in cross:
        copy.start()
    onward = None
    for t in range(rings // 2):
        last = t == rings // 2 - 1
        cw_spots = pl.ds(0, half if last else slab)
        ccw_spots = pl.ds(half if last else 0, half if last else slab)
        cw = out_ref.at[(ring - t + rings) % rings, cw_spots, :, :, first_lanes]
        ccw = out_ref.at[(ring + t) % rings, ccw_spots, :, :, first_lanes]
        step = [
            remote(cw, device(ahead, spot), ring_sems, (0, t)),
            remote(ccw, device(behind, spot), ring_sems, (1, t)),
        ]
        for copy in step:
            copy.start()
        finish(step)
        if t == 1:
            finish(cross)
            from_left = ((across + row - 1) % row) * pair
            from_right = ((across + 1) % row) * pair
            onward = [
                remote(
                    out_ref.at[pl.ds(0, mid), pl.ds(from_left, pair), :, :, second_lanes],
                    device(ring, right),
                    cross_sems,
                    (0, 1),
                ),
                remote(
                    out_ref.at[pl.ds(mid, mid), pl.ds(from_right, pair), :, :, second_lanes],
                    device(ring, left),
                    cross_sems,
                    (1, 1),
                ),
            ]
            for copy in onward:
                copy.start()
    finish(onward)


def gather_seq(block, rings, slab):
    return pl.pallas_call(
        gather_kernel,
        out_shape=jax.ShapeDtypeStruct((rings, slab) + block.shape, block.dtype),
        in_specs=[pl.BlockSpec(memory_space=pl.ANY)],
        out_specs=pl.BlockSpec(memory_space=pl.ANY),
        scratch_shapes=[
            pltpu.SemaphoreType.DMA((2,)),
            pltpu.SemaphoreType.DMA((2, slab // 2 - 1)),
            pltpu.SemaphoreType.DMA((2, 2, rings // 2)),
            pltpu.SemaphoreType.DMA((2, 2, rings // 2)),
            pltpu.SemaphoreType.DMA((2, 2, 2)),
            pltpu.SemaphoreType.DMA(()),
        ],
        compiler_params=pltpu.CompilerParams(collective_id=0, has_side_effects=True),
    )(block)


def scatter_kernel(terms_ref, out_ref, mine, incoming, sums, send_sem, recv_sem, local_sems):
    chips = out_ref.shape[0]
    seq = lax.axis_index("seq")
    tp = lax.axis_index("tp")
    mesh_id = pl.DeviceIdType.MESH
    core = tp % 2
    here = tp // 2
    owners = [(here + k) % chips for k in range(1, chips)]
    targets = [(seq, tp + 1 - 2 * core)] + [(seq, owner * 2 + core) for owner in owners]

    barrier = pltpu.get_barrier_semaphore()
    for target in targets:
        pl.semaphore_signal(barrier, inc=1, device_id=target, device_id_type=mesh_id)
    pl.semaphore_wait(barrier, len(targets))

    keep = pltpu.make_async_copy(terms_ref.at[core], mine, local_sems.at[0])
    keep.start()
    swap = pltpu.make_async_remote_copy(
        src_ref=terms_ref.at[1 - core],
        dst_ref=incoming,
        send_sem=send_sem.at[0],
        recv_sem=recv_sem.at[0],
        device_id=targets[0],
        device_id_type=mesh_id,
    )
    swap.start()
    keep.wait()
    swap.wait_send()
    swap.wait_recv()
    sums[...] = (mine[...] + incoming[...]).astype(sums.dtype)

    local = pltpu.make_async_copy(sums.at[here], out_ref.at[here], local_sems.at[1])
    local.start()
    copies = []
    for k, owner in enumerate(owners):
        copy = pltpu.make_async_remote_copy(
            src_ref=sums.at[owner],
            dst_ref=out_ref.at[here],
            send_sem=send_sem.at[k + 1],
            recv_sem=recv_sem.at[k + 1],
            device_id=targets[k + 1],
            device_id_type=mesh_id,
        )
        copy.start()
        copies.append(copy)
    for copy in copies:
        copy.wait_send()
        copy.wait_recv()
    local.wait()


def scatter_chips(terms):
    block = terms.shape[1:]
    chips = block[0]
    return pl.pallas_call(
        scatter_kernel,
        out_shape=jax.ShapeDtypeStruct(block, jnp.bfloat16),
        in_specs=[pl.BlockSpec(memory_space=pl.ANY)],
        out_specs=pl.BlockSpec(memory_space=pl.ANY),
        scratch_shapes=[
            pltpu.VMEM(block, jnp.float32),
            pltpu.VMEM(block, jnp.float32),
            pltpu.VMEM(block, jnp.bfloat16),
            pltpu.SemaphoreType.DMA((chips,)),
            pltpu.SemaphoreType.DMA((chips,)),
            pltpu.SemaphoreType.DMA((2,)),
        ],
        compiler_params=pltpu.CompilerParams(collective_id=1, has_side_effects=True),
    )(terms)


def exchange_kernel(axis, offsets, x_ref, out_ref, send_sem, recv_sem, local_sem):
    size = lax.axis_size(axis)
    me = lax.axis_index(axis)
    seq = lax.axis_index("seq")
    tp = lax.axis_index("tp")
    mesh_id = pl.DeviceIdType.MESH

    def device(position):
        return (position, tp) if axis == "seq" else (seq, position)

    def slot(entry):
        return me if entry is None else entry

    peers = [lax.rem(me + offset + size, size) for offset, _ in offsets]
    barrier = pltpu.get_barrier_semaphore()
    for peer in peers:
        pl.semaphore_signal(barrier, inc=1, device_id=device(peer), device_id_type=mesh_id)
    pl.semaphore_wait(barrier, len(peers))

    own = offsets_own_slot(offsets, me)
    local = pltpu.make_async_copy(x_ref, out_ref.at[own], local_sem)
    local.start()
    copies = []
    for k, ((_, entry), peer) in enumerate(zip(offsets, peers)):
        copy = pltpu.make_async_remote_copy(
            src_ref=x_ref,
            dst_ref=out_ref.at[slot(entry)],
            send_sem=send_sem.at[k],
            recv_sem=recv_sem.at[k],
            device_id=device(peer),
            device_id_type=mesh_id,
        )
        copy.start()
        copies.append(copy)
    for copy in copies:
        copy.wait_send()
        copy.wait_recv()
    local.wait()


def offsets_own_slot(offsets, me):
    slots = [entry for _, entry in offsets]
    if None in slots:
        return me
    return len(offsets) // 2


def exchange(block, axis, offsets, slots, collective_id):
    count = len(offsets)
    return pl.pallas_call(
        functools.partial(exchange_kernel, axis, offsets),
        out_shape=jax.ShapeDtypeStruct((slots,) + block.shape, block.dtype),
        in_specs=[pl.BlockSpec(memory_space=pl.ANY)],
        out_specs=pl.BlockSpec(memory_space=pl.ANY),
        scratch_shapes=[
            pltpu.SemaphoreType.DMA((count,)),
            pltpu.SemaphoreType.DMA((count,)),
            pltpu.SemaphoreType.DMA(()),
        ],
        compiler_params=pltpu.CompilerParams(
            collective_id=collective_id, has_side_effects=True
        ),
    )(block)


def masked_scores(query, keys, query_seg, key_seg):
    scores = jnp.einsum(
        "qhd,khd->hqk", query, keys, preferred_element_type=jnp.float32
    ) * HEAD_DIM ** (-0.5)
    mask = (query_seg[:, None] == key_seg[None, :])[None]
    return (jnp.where(mask, scores, floor_score), mask)


def shards(tokens, norm_gain, qkv_weight, q_gain, k_gain, out_weight, layer_scale, segment_ids):
    count = tokens.shape[0]
    source = tokens.astype(jnp.float32)
    normed = (
        source * lax.rsqrt(jnp.mean(source * source, axis=-1, keepdims=True) + eps) * norm_gain
    ).astype(jnp.bfloat16)
    local_width = qkv_weight.shape[2]
    heads = local_width // HEAD_DIM
    stacked = jnp.concatenate([qkv_weight, jnp.transpose(out_weight)[:, None, :]], axis=1)
    rows, kinds, width = stacked.shape
    slab = 8
    gathered = gather_seq(stacked, lax.axis_size("seq") // slab, slab).reshape(-1, kinds, width)
    joined = jnp.einsum(
        "td,dch->tch",
        normed,
        gathered[:, :3],
        preferred_element_type=jnp.float32,
    )
    query = joined[:, 0]
    keys = joined[:, 1]
    values = joined[:, 2]
    parts = lax.axis_size("tp")
    squares = jnp.stack([jnp.sum(query * query, axis=-1), jnp.sum(keys * keys, axis=-1)])
    everyone = [(k, None) for k in range(1, parts)]
    query_sq, key_sq = jnp.sum(exchange(squares, "tp", everyone, parts, 2), axis=0)
    full_width = local_width * lax.axis_size("tp")
    query_normed = (query * lax.rsqrt(query_sq / full_width + eps)[:, None] * q_gain).astype(
        jnp.bfloat16
    )
    key_normed = (keys * lax.rsqrt(key_sq / full_width + eps)[:, None] * k_gain).astype(
        jnp.bfloat16
    )
    paired = jnp.stack([key_normed, values.astype(jnp.bfloat16)], axis=1)
    pieces = []
    for offset in (2, 1, 0, -1, -2):
        if offset == 0:
            pieces.append(paired)
        else:
            pieces.append(passed_along(paired, "seq", offset))
    widened = jnp.concatenate(pieces, axis=0)
    position = lax.axis_index("seq")
    outside = jnp.full((2 * count,), -1, jnp.int32)
    seg_pad = jnp.concatenate([outside, segment_ids, outside], axis=0)
    key_seg = lax.dynamic_slice_in_dim(seg_pad, position * count, 5 * count, 0)
    query_seg = lax.dynamic_slice_in_dim(segment_ids, position * count, count, 0)
    query_heads = query_normed.reshape(count, heads, HEAD_DIM)
    key_heads = widened[:, 0].reshape(5 * count, heads, HEAD_DIM)
    value_heads = widened[:, 1].reshape(5 * count, heads, HEAD_DIM)
    scores, mask = masked_scores(query_heads, key_heads, query_seg, key_seg)
    peak = jnp.max(scores, axis=-1, keepdims=True)
    weights = jnp.where(mask, jnp.exp(scores - peak), 0.0)
    total = jnp.sum(weights, axis=-1)
    probs = weights.astype(jnp.bfloat16)
    summed = jnp.einsum("hqk,khd->qhd", probs, value_heads, preferred_element_type=jnp.float32)
    context = (
        (summed / jnp.transpose(total)[:, :, None]).reshape(count, local_width).astype(jnp.bfloat16)
    )
    blank = jnp.zeros_like(context)
    widened_context = jnp.stack([blank, blank, blank, context], axis=1)
    chips = parts // 2
    by_owner = gathered.reshape(chips, 2, -1, *gathered.shape[1:])
    terms = jnp.einsum(
        "tkh,ycdkh->cytd", widened_context, by_owner, preferred_element_type=jnp.float32
    )
    projected = jnp.sum(scatter_chips(terms).astype(jnp.float32), axis=0)
    share = layer_scale.shape[0]
    residual = lax.dynamic_slice_in_dim(source, lax.axis_index("tp") * share, share, 1)
    return (residual + layer_scale * projected).astype(jnp.bfloat16)


def solution(mesh):
    return jax.shard_map(
        shards,
        mesh=mesh,
        in_specs=(
            P("seq", None),
            P(),
            P("seq", None, "tp"),
            P("tp"),
            P("tp"),
            P("tp", "seq"),
            P("tp"),
            P(),
        ),
        out_specs=P("seq", "tp"),
        check_vma=False,
    )
```

```python
import functools

import jax
import jax.numpy as jnp
from jax import lax
from jax.sharding import PartitionSpec as P
from jax.experimental import pallas as pl
from jax.experimental.pallas import tpu as pltpu

HEAD_DIM = 128


eps = 1e-06
floor_score = -1e30


def passed_along(x, axis, by):
    size = lax.axis_size(axis)
    pairs = [(i, i + by) for i in range(size) if 0 <= i + by < size]
    return lax.ppermute(x, axis, pairs)


def gather_kernel(x_ref, out_ref, pair_sems, row_sems, lane_sems, ring_sems, cross_sems, local_sem):
    rings, slab = out_ref.shape[0], out_ref.shape[1]
    pair = 2
    row = slab // pair
    lanes = out_ref.shape[-1] // 2
    first_lanes, second_lanes = pl.ds(0, lanes), pl.ds(lanes, lanes)
    me = lax.axis_index("seq")
    tp = lax.axis_index("tp")
    mesh_id = pl.DeviceIdType.MESH
    ring = me // slab
    spot = me % slab
    low = spot % pair
    across = spot // pair
    base = spot - low

    def device(r, s):
        return (r * slab + s, tp)

    ahead = (ring + 1) % rings
    behind = (ring + rings - 1) % rings
    partner = base + 1 - low
    row_spots = [((across + k) % row) * pair + low for k in range(1, row)]
    right = ((across + 1) % row) * pair + low
    left = ((across + row - 1) % row) * pair + low

    barrier = pltpu.get_barrier_semaphore()
    targets = [device(ring, partner), device(ahead, spot), device(behind, spot)]
    targets += [device(ring, s) for s in row_spots]
    for target in targets:
        pl.semaphore_signal(barrier, inc=1, device_id=target, device_id_type=mesh_id)
    pl.semaphore_wait(barrier, len(targets))

    def remote(window, target, sems, index):
        return pltpu.make_async_remote_copy(
            src_ref=window,
            dst_ref=window,
            send_sem=sems.at[(0,) + index],
            recv_sem=sems.at[(1,) + index],
            device_id=target,
            device_id_type=mesh_id,
        )

    def finish(copies):
        for copy in copies:
            copy.wait_send()
            copy.wait_recv()

    local = pltpu.make_async_copy(x_ref, out_ref.at[ring, spot], local_sem)
    local.start()
    swap = pltpu.make_async_remote_copy(
        src_ref=x_ref,
        dst_ref=out_ref.at[ring, spot],
        send_sem=pair_sems.at[0],
        recv_sem=pair_sems.at[1],
        device_id=device(ring, partner),
        device_id_type=mesh_id,
    )
    swap.start()
    local.wait()
    finish([swap])

    pair_a = out_ref.at[ring, pl.ds(base, pair), :, :, first_lanes]
    rows_a = [remote(pair_a, device(ring, s), row_sems, (k,)) for k, s in enumerate(row_spots)]
    for copy in rows_a:
        copy.start()
    for t in range(rings // 2):
        last = t == rings // 2 - 1
        cw_spots = pl.ds(base, 1 if last else pair)
        ccw_spots = pl.ds(base + 1 if last else base, 1 if last else pair)
        cw = out_ref.at[(ring - t + rings) % rings, cw_spots, :, :, second_lanes]
        ccw = out_ref.at[(ring + t) % rings, ccw_spots, :, :, second_lanes]
        step = [
            remote(cw, device(ahead, spot), lane_sems, (0, t)),
            remote(ccw, device(behind, spot), lane_sems, (1, t)),
        ]
        for copy in step:
            copy.start()
        finish(step)
    finish(rows_a)

    half = slab // 2
    mid = rings // 2
    cross = [
        remote(out_ref.at[:, pl.ds(base, pair), :, :, second_lanes], device(ring, right), cross_sems, (0, 0)),
        remote(out_ref.at[:, pl.ds(base, pair), :, :, second_lanes], device(ring, left), cross_sems, (1, 0)),
    ]
    for copy in cross:
        copy.start()
    onward = None
    for t in range(rings // 2):
        last = t == rings // 2 - 1
        cw_spots = pl.ds(0, half if last else slab)
        ccw_spots = pl.ds(half if last else 0, half if last else slab)
        cw = out_ref.at[(ring - t + rings) % rings, cw_spots, :, :, first_lanes]
        ccw = out_ref.at[(ring + t) % rings, ccw_spots, :, :, first_lanes]
        step = [
            remote(cw, device(ahead, spot), ring_sems, (0, t)),
            remote(ccw, device(behind, spot), ring_sems, (1, t)),
        ]
        for copy in step:
            copy.start()
        finish(step)
        if t == 1:
            finish(cross)
            from_left = ((across + row - 1) % row) * pair
            from_right = ((across + 1) % row) * pair
            onward = [
                remote(
                    out_ref.at[pl.ds(0, mid), pl.ds(from_left, pair), :, :, second_lanes],
                    device(ring, right),
                    cross_sems,
                    (0, 1),
                ),
                remote(
                    out_ref.at[pl.ds(mid, mid), pl.ds(from_right, pair), :, :, second_lanes],
                    device(ring, left),
                    cross_sems,
                    (1, 1),
                ),
            ]
            for copy in onward:
                copy.start()
    finish(onward)


def gather_seq(block, rings, slab):
    return pl.pallas_call(
        gather_kernel,
        out_shape=jax.ShapeDtypeStruct((rings, slab) + block.shape, block.dtype),
        in_specs=[pl.BlockSpec(memory_space=pl.ANY)],
        out_specs=pl.BlockSpec(memory_space=pl.ANY),
        scratch_shapes=[
            pltpu.SemaphoreType.DMA((2,)),
            pltpu.SemaphoreType.DMA((2, slab // 2 - 1)),
            pltpu.SemaphoreType.DMA((2, 2, rings // 2)),
            pltpu.SemaphoreType.DMA((2, 2, rings // 2)),
            pltpu.SemaphoreType.DMA((2, 2, 2)),
            pltpu.SemaphoreType.DMA(()),
        ],
        compiler_params=pltpu.CompilerParams(collective_id=0, has_side_effects=True),
    )(block)


def scatter_kernel(terms_ref, out_ref, mine, incoming, sums, transit, send_sem, recv_sem, local_sems):
    chips = out_ref.shape[0]
    rows = out_ref.shape[1] // 2
    seq = lax.axis_index("seq")
    tp = lax.axis_index("tp")
    mesh_id = pl.DeviceIdType.MESH
    core = tp % 2
    here = tp // 2
    up = (here + 1) % chips
    far = (here + 2) % chips
    down = (here + chips - 1) % chips

    def device(chip):
        return (seq, chip * 2 + core)

    targets = [(seq, tp + 1 - 2 * core), device(up), device(far), device(down)]
    barrier = pltpu.get_barrier_semaphore()
    for target in targets:
        pl.semaphore_signal(barrier, inc=1, device_id=target, device_id_type=mesh_id)
    pl.semaphore_wait(barrier, len(targets))

    def remote(src, dst, target, k):
        return pltpu.make_async_remote_copy(
            src_ref=src,
            dst_ref=dst,
            send_sem=send_sem.at[k],
            recv_sem=recv_sem.at[k],
            device_id=target,
            device_id_type=mesh_id,
        )

    keep = pltpu.make_async_copy(terms_ref.at[core], mine, local_sems.at[0])
    keep.start()
    swap = remote(terms_ref.at[1 - core], incoming, targets[0], 0)
    swap.start()
    keep.wait()
    swap.wait_send()
    swap.wait_recv()
    sums[...] = (mine[...] + incoming[...]).astype(sums.dtype)

    top, bottom = pl.ds(0, rows), pl.ds(rows, rows)
    local = pltpu.make_async_copy(sums.at[here], out_ref.at[here], local_sems.at[1])
    local.start()
    direct = remote(sums.at[far, top], out_ref.at[here, top], device(far), 1)
    to_up = remote(sums.at[up], out_ref.at[here], device(up), 2)
    to_down = remote(sums.at[down], out_ref.at[here], device(down), 3)
    hand = remote(sums.at[far, bottom], transit, device(down), 4)
    copies = [direct, to_up, to_down, hand]
    for copy in copies:
        copy.start()
    hand.wait_recv()
    onward = remote(transit, out_ref.at[up, bottom], device(down), 5)
    onward.start()
    hand.wait_send()
    for copy in [direct, to_up, to_down]:
        copy.wait_send()
        copy.wait_recv()
    onward.wait_send()
    onward.wait_recv()
    local.wait()


def scatter_chips(terms):
    block = terms.shape[1:]
    chips = block[0]
    return pl.pallas_call(
        scatter_kernel,
        out_shape=jax.ShapeDtypeStruct(block, jnp.bfloat16),
        in_specs=[pl.BlockSpec(memory_space=pl.ANY)],
        out_specs=pl.BlockSpec(memory_space=pl.ANY),
        scratch_shapes=[
            pltpu.VMEM(block, jnp.float32),
            pltpu.VMEM(block, jnp.float32),
            pltpu.VMEM(block, jnp.bfloat16),
            pltpu.VMEM((block[1] // 2,) + block[2:], jnp.bfloat16),
            pltpu.SemaphoreType.DMA((6,)),
            pltpu.SemaphoreType.DMA((6,)),
            pltpu.SemaphoreType.DMA((2,)),
        ],
        compiler_params=pltpu.CompilerParams(collective_id=1, has_side_effects=True),
    )(terms)


def exchange_kernel(axis, offsets, x_ref, out_ref, send_sem, recv_sem, local_sem):
    size = lax.axis_size(axis)
    me = lax.axis_index(axis)
    seq = lax.axis_index("seq")
    tp = lax.axis_index("tp")
    mesh_id = pl.DeviceIdType.MESH

    def device(position):
        return (position, tp) if axis == "seq" else (seq, position)

    def slot(entry):
        return me if entry is None else entry

    peers = [lax.rem(me + offset + size, size) for offset, _ in offsets]
    barrier = pltpu.get_barrier_semaphore()
    for peer in peers:
        pl.semaphore_signal(barrier, inc=1, device_id=device(peer), device_id_type=mesh_id)
    pl.semaphore_wait(barrier, len(peers))

    own = offsets_own_slot(offsets, me)
    local = pltpu.make_async_copy(x_ref, out_ref.at[own], local_sem)
    local.start()
    copies = []
    for k, ((_, entry), peer) in enumerate(zip(offsets, peers)):
        copy = pltpu.make_async_remote_copy(
            src_ref=x_ref,
            dst_ref=out_ref.at[slot(entry)],
            send_sem=send_sem.at[k],
            recv_sem=recv_sem.at[k],
            device_id=device(peer),
            device_id_type=mesh_id,
        )
        copy.start()
        copies.append(copy)
    for copy in copies:
        copy.wait_send()
        copy.wait_recv()
    local.wait()


def offsets_own_slot(offsets, me):
    slots = [entry for _, entry in offsets]
    if None in slots:
        return me
    return len(offsets) // 2


def exchange(block, axis, offsets, slots, collective_id):
    count = len(offsets)
    return pl.pallas_call(
        functools.partial(exchange_kernel, axis, offsets),
        out_shape=jax.ShapeDtypeStruct((slots,) + block.shape, block.dtype),
        in_specs=[pl.BlockSpec(memory_space=pl.ANY)],
        out_specs=pl.BlockSpec(memory_space=pl.ANY),
        scratch_shapes=[
            pltpu.SemaphoreType.DMA((count,)),
            pltpu.SemaphoreType.DMA((count,)),
            pltpu.SemaphoreType.DMA(()),
        ],
        compiler_params=pltpu.CompilerParams(
            collective_id=collective_id, has_side_effects=True
        ),
    )(block)


def masked_scores(query, keys, query_seg, key_seg):
    scores = jnp.einsum(
        "qhd,khd->hqk", query, keys, preferred_element_type=jnp.float32
    ) * HEAD_DIM ** (-0.5)
    mask = (query_seg[:, None] == key_seg[None, :])[None]
    return (jnp.where(mask, scores, floor_score), mask)


def shards(tokens, norm_gain, qkv_weight, q_gain, k_gain, out_weight, layer_scale, segment_ids):
    count = tokens.shape[0]
    source = tokens.astype(jnp.float32)
    normed = (
        source * lax.rsqrt(jnp.mean(source * source, axis=-1, keepdims=True) + eps) * norm_gain
    ).astype(jnp.bfloat16)
    local_width = qkv_weight.shape[2]
    heads = local_width // HEAD_DIM
    stacked = jnp.concatenate([qkv_weight, jnp.transpose(out_weight)[:, None, :]], axis=1)
    rows, kinds, width = stacked.shape
    slab = 8
    gathered = gather_seq(stacked, lax.axis_size("seq") // slab, slab).reshape(-1, kinds, width)
    joined = jnp.einsum(
        "td,dch->tch",
        normed,
        gathered[:, :3],
        preferred_element_type=jnp.float32,
    )
    query = joined[:, 0]
    keys = joined[:, 1]
    values = joined[:, 2]
    parts = lax.axis_size("tp")
    squares = jnp.stack([jnp.sum(query * query, axis=-1), jnp.sum(keys * keys, axis=-1)])
    everyone = [(k, None) for k in range(1, parts)]
    query_sq, key_sq = jnp.sum(exchange(squares, "tp", everyone, parts, 2), axis=0)
    full_width = local_width * lax.axis_size("tp")
    query_normed = (query * lax.rsqrt(query_sq / full_width + eps)[:, None] * q_gain).astype(
        jnp.bfloat16
    )
    key_normed = (keys * lax.rsqrt(key_sq / full_width + eps)[:, None] * k_gain).astype(
        jnp.bfloat16
    )
    paired = jnp.stack([key_normed, values.astype(jnp.bfloat16)], axis=1)
    pieces = []
    for offset in (2, 1, 0, -1, -2):
        if offset == 0:
            pieces.append(paired)
        else:
            pieces.append(passed_along(paired, "seq", offset))
    widened = jnp.concatenate(pieces, axis=0)
    position = lax.axis_index("seq")
    outside = jnp.full((2 * count,), -1, jnp.int32)
    seg_pad = jnp.concatenate([outside, segment_ids, outside], axis=0)
    key_seg = lax.dynamic_slice_in_dim(seg_pad, position * count, 5 * count, 0)
    query_seg = lax.dynamic_slice_in_dim(segment_ids, position * count, count, 0)
    query_heads = query_normed.reshape(count, heads, HEAD_DIM)
    key_heads = widened[:, 0].reshape(5 * count, heads, HEAD_DIM)
    value_heads = widened[:, 1].reshape(5 * count, heads, HEAD_DIM)
    scores, mask = masked_scores(query_heads, key_heads, query_seg, key_seg)
    peak = jnp.max(scores, axis=-1, keepdims=True)
    weights = jnp.where(mask, jnp.exp(scores - peak), 0.0)
    total = jnp.sum(weights, axis=-1)
    probs = weights.astype(jnp.bfloat16)
    summed = jnp.einsum("hqk,khd->qhd", probs, value_heads, preferred_element_type=jnp.float32)
    context = (
        (summed / jnp.transpose(total)[:, :, None]).reshape(count, local_width).astype(jnp.bfloat16)
    )
    blank = jnp.zeros_like(context)
    widened_context = jnp.stack([blank, blank, blank, context], axis=1)
    chips = parts // 2
    by_owner = gathered.reshape(chips, 2, -1, *gathered.shape[1:])
    terms = jnp.einsum(
        "tkh,ycdkh->cytd", widened_context, by_owner, preferred_element_type=jnp.float32
    )
    projected = jnp.sum(scatter_chips(terms).astype(jnp.float32), axis=0)
    share = layer_scale.shape[0]
    residual = lax.dynamic_slice_in_dim(source, lax.axis_index("tp") * share, share, 1)
    return (residual + layer_scale * projected).astype(jnp.bfloat16)


def solution(mesh):
    return jax.shard_map(
        shards,
        mesh=mesh,
        in_specs=(
            P("seq", None),
            P(),
            P("seq", None, "tp"),
            P("tp"),
            P("tp"),
            P("tp", "seq"),
            P("tp"),
            P(),
        ),
        out_specs=P("seq", "tp"),
        check_vma=False,
    )
```

```python
import functools

import jax
import jax.numpy as jnp
from jax import lax
from jax.sharding import PartitionSpec as P
from jax.experimental import pallas as pl
from jax.experimental.pallas import tpu as pltpu

HEAD_DIM = 128


eps = 1e-06
floor_score = -1e30


def passed_along(x, axis, by):
    size = lax.axis_size(axis)
    pairs = [(i, i + by) for i in range(size) if 0 <= i + by < size]
    return lax.ppermute(x, axis, pairs)


def gather_kernel(x_ref, out_ref, pair_sems, row_sems, lane_sems, ring_sems, cross_sems, local_sem):
    rings, slab = out_ref.shape[0], out_ref.shape[1]
    pair = 2
    row = slab // pair
    lanes = out_ref.shape[-1] // 2
    first_lanes, second_lanes = pl.ds(0, lanes), pl.ds(lanes, lanes)
    me = lax.axis_index("seq")
    tp = lax.axis_index("tp")
    mesh_id = pl.DeviceIdType.MESH
    ring = me // slab
    spot = me % slab
    low = spot % pair
    across = spot // pair
    base = spot - low

    def device(r, s):
        return (r * slab + s, tp)

    ahead = (ring + 1) % rings
    behind = (ring + rings - 1) % rings
    partner = base + 1 - low
    row_spots = [((across + k) % row) * pair + low for k in range(1, row)]
    right = ((across + 1) % row) * pair + low
    left = ((across + row - 1) % row) * pair + low

    barrier = pltpu.get_barrier_semaphore()
    targets = [device(ring, partner), device(ahead, spot), device(behind, spot)]
    targets += [device(ring, s) for s in row_spots]
    for target in targets:
        pl.semaphore_signal(barrier, inc=1, device_id=target, device_id_type=mesh_id)
    pl.semaphore_wait(barrier, len(targets))

    def remote(window, target, sems, index):
        return pltpu.make_async_remote_copy(
            src_ref=window,
            dst_ref=window,
            send_sem=sems.at[(0,) + index],
            recv_sem=sems.at[(1,) + index],
            device_id=target,
            device_id_type=mesh_id,
        )

    def finish(copies):
        for copy in copies:
            copy.wait_send()
            copy.wait_recv()

    local = pltpu.make_async_copy(x_ref, out_ref.at[ring, spot], local_sem)
    local.start()
    swap = pltpu.make_async_remote_copy(
        src_ref=x_ref,
        dst_ref=out_ref.at[ring, spot],
        send_sem=pair_sems.at[0],
        recv_sem=pair_sems.at[1],
        device_id=device(ring, partner),
        device_id_type=mesh_id,
    )
    swap.start()
    local.wait()
    finish([swap])

    pair_a = out_ref.at[ring, pl.ds(base, pair), :, :, first_lanes]
    rows_a = [remote(pair_a, device(ring, s), row_sems, (k,)) for k, s in enumerate(row_spots)]
    for copy in rows_a:
        copy.start()
    for t in range(rings // 2):
        last = t == rings // 2 - 1
        cw_spots = pl.ds(base, 1 if last else pair)
        ccw_spots = pl.ds(base + 1 if last else base, 1 if last else pair)
        cw = out_ref.at[(ring - t + rings) % rings, cw_spots, :, :, second_lanes]
        ccw = out_ref.at[(ring + t) % rings, ccw_spots, :, :, second_lanes]
        step = [
            remote(cw, device(ahead, spot), lane_sems, (0, t)),
            remote(ccw, device(behind, spot), lane_sems, (1, t)),
        ]
        for copy in step:
            copy.start()
        finish(step)
    finish(rows_a)

    half = slab // 2
    mid = rings // 2
    cross = [
        remote(out_ref.at[:, pl.ds(base, pair), :, :, second_lanes], device(ring, right), cross_sems, (0, 0)),
        remote(out_ref.at[:, pl.ds(base, pair), :, :, second_lanes], device(ring, left), cross_sems, (1, 0)),
    ]
    for copy in cross:
        copy.start()
    onward = None
    for t in range(rings // 2):
        last = t == rings // 2 - 1
        cw_spots = pl.ds(0, half if last else slab)
        ccw_spots = pl.ds(half if last else 0, half if last else slab)
        cw = out_ref.at[(ring - t + rings) % rings, cw_spots, :, :, first_lanes]
        ccw = out_ref.at[(ring + t) % rings, ccw_spots, :, :, first_lanes]
        step = [
            remote(cw, device(ahead, spot), ring_sems, (0, t)),
            remote(ccw, device(behind, spot), ring_sems, (1, t)),
        ]
        for copy in step:
            copy.start()
        finish(step)
        if t == 1:
            finish(cross)
            from_left = ((across + row - 1) % row) * pair
            from_right = ((across + 1) % row) * pair
            onward = [
                remote(
                    out_ref.at[pl.ds(0, mid), pl.ds(from_left, pair), :, :, second_lanes],
                    device(ring, right),
                    cross_sems,
                    (0, 1),
                ),
                remote(
                    out_ref.at[pl.ds(mid, mid), pl.ds(from_right, pair), :, :, second_lanes],
                    device(ring, left),
                    cross_sems,
                    (1, 1),
                ),
            ]
            for copy in onward:
                copy.start()
    finish(onward)


def gather_seq(block, rings, slab):
    return pl.pallas_call(
        gather_kernel,
        out_shape=jax.ShapeDtypeStruct((rings, slab) + block.shape, block.dtype),
        in_specs=[pl.BlockSpec(memory_space=pl.ANY)],
        out_specs=pl.BlockSpec(memory_space=pl.ANY),
        scratch_shapes=[
            pltpu.SemaphoreType.DMA((2,)),
            pltpu.SemaphoreType.DMA((2, slab // 2 - 1)),
            pltpu.SemaphoreType.DMA((2, 2, rings // 2)),
            pltpu.SemaphoreType.DMA((2, 2, rings // 2)),
            pltpu.SemaphoreType.DMA((2, 2, 2)),
            pltpu.SemaphoreType.DMA(()),
        ],
        compiler_params=pltpu.CompilerParams(collective_id=0, has_side_effects=True),
    )(block)


def scatter_kernel(terms_ref, out_ref, mine, incoming, sums, send_sem, recv_sem, local_sems):
    chips = out_ref.shape[0]
    seq = lax.axis_index("seq")
    tp = lax.axis_index("tp")
    mesh_id = pl.DeviceIdType.MESH
    core = tp % 2
    here = tp // 2
    owners = [(here + k) % chips for k in range(1, chips)]
    targets = [(seq, tp + 1 - 2 * core)] + [(seq, owner * 2 + core) for owner in owners]

    barrier = pltpu.get_barrier_semaphore()
    for target in targets:
        pl.semaphore_signal(barrier, inc=1, device_id=target, device_id_type=mesh_id)
    pl.semaphore_wait(barrier, len(targets))

    keep = pltpu.make_async_copy(terms_ref.at[core], mine, local_sems.at[0])
    keep.start()
    swap = pltpu.make_async_remote_copy(
        src_ref=terms_ref.at[1 - core],
        dst_ref=incoming,
        send_sem=send_sem.at[0],
        recv_sem=recv_sem.at[0],
        device_id=targets[0],
        device_id_type=mesh_id,
    )
    swap.start()
    keep.wait()
    swap.wait_send()
    swap.wait_recv()
    total = mine[...].astype(jnp.float32) + incoming[...].astype(jnp.float32)
    sums[...] = total.astype(sums.dtype)

    local = pltpu.make_async_copy(sums.at[here], out_ref.at[here], local_sems.at[1])
    local.start()
    copies = []
    for k, owner in enumerate(owners):
        copy = pltpu.make_async_remote_copy(
            src_ref=sums.at[owner],
            dst_ref=out_ref.at[here],
            send_sem=send_sem.at[k + 1],
            recv_sem=recv_sem.at[k + 1],
            device_id=targets[k + 1],
            device_id_type=mesh_id,
        )
        copy.start()
        copies.append(copy)
    for copy in copies:
        copy.wait_send()
        copy.wait_recv()
    local.wait()


def scatter_chips(terms):
    block = terms.shape[1:]
    chips = block[0]
    return pl.pallas_call(
        scatter_kernel,
        out_shape=jax.ShapeDtypeStruct(block, jnp.bfloat16),
        in_specs=[pl.BlockSpec(memory_space=pl.ANY)],
        out_specs=pl.BlockSpec(memory_space=pl.ANY),
        scratch_shapes=[
            pltpu.VMEM(block, terms.dtype),
            pltpu.VMEM(block, terms.dtype),
            pltpu.VMEM(block, jnp.bfloat16),
            pltpu.SemaphoreType.DMA((chips,)),
            pltpu.SemaphoreType.DMA((chips,)),
            pltpu.SemaphoreType.DMA((2,)),
        ],
        compiler_params=pltpu.CompilerParams(collective_id=1, has_side_effects=True),
    )(terms)


def exchange_kernel(axis, offsets, x_ref, out_ref, send_sem, recv_sem, local_sem):
    size = lax.axis_size(axis)
    me = lax.axis_index(axis)
    seq = lax.axis_index("seq")
    tp = lax.axis_index("tp")
    mesh_id = pl.DeviceIdType.MESH

    def device(position):
        return (position, tp) if axis == "seq" else (seq, position)

    def slot(entry):
        return me if entry is None else entry

    peers = [lax.rem(me + offset + size, size) for offset, _ in offsets]
    barrier = pltpu.get_barrier_semaphore()
    for peer in peers:
        pl.semaphore_signal(barrier, inc=1, device_id=device(peer), device_id_type=mesh_id)
    pl.semaphore_wait(barrier, len(peers))

    own = offsets_own_slot(offsets, me)
    local = pltpu.make_async_copy(x_ref, out_ref.at[own], local_sem)
    local.start()
    copies = []
    for k, ((_, entry), peer) in enumerate(zip(offsets, peers)):
        copy = pltpu.make_async_remote_copy(
            src_ref=x_ref,
            dst_ref=out_ref.at[slot(entry)],
            send_sem=send_sem.at[k],
            recv_sem=recv_sem.at[k],
            device_id=device(peer),
            device_id_type=mesh_id,
        )
        copy.start()
        copies.append(copy)
    for copy in copies:
        copy.wait_send()
        copy.wait_recv()
    local.wait()


def offsets_own_slot(offsets, me):
    slots = [entry for _, entry in offsets]
    if None in slots:
        return me
    return len(offsets) // 2


def exchange(block, axis, offsets, slots, collective_id):
    count = len(offsets)
    return pl.pallas_call(
        functools.partial(exchange_kernel, axis, offsets),
        out_shape=jax.ShapeDtypeStruct((slots,) + block.shape, block.dtype),
        in_specs=[pl.BlockSpec(memory_space=pl.ANY)],
        out_specs=pl.BlockSpec(memory_space=pl.ANY),
        scratch_shapes=[
            pltpu.SemaphoreType.DMA((count,)),
            pltpu.SemaphoreType.DMA((count,)),
            pltpu.SemaphoreType.DMA(()),
        ],
        compiler_params=pltpu.CompilerParams(
            collective_id=collective_id, has_side_effects=True
        ),
    )(block)


def masked_scores(query, keys, query_seg, key_seg):
    scores = jnp.einsum(
        "qhd,khd->hqk", query, keys, preferred_element_type=jnp.float32
    ) * HEAD_DIM ** (-0.5)
    mask = (query_seg[:, None] == key_seg[None, :])[None]
    return (jnp.where(mask, scores, floor_score), mask)


def shards(tokens, norm_gain, qkv_weight, q_gain, k_gain, out_weight, layer_scale, segment_ids):
    count = tokens.shape[0]
    source = tokens.astype(jnp.float32)
    normed = (
        source * lax.rsqrt(jnp.mean(source * source, axis=-1, keepdims=True) + eps) * norm_gain
    ).astype(jnp.bfloat16)
    local_width = qkv_weight.shape[2]
    heads = local_width // HEAD_DIM
    stacked = jnp.concatenate([qkv_weight, jnp.transpose(out_weight)[:, None, :]], axis=1)
    rows, kinds, width = stacked.shape
    slab = 8
    gathered = gather_seq(stacked, lax.axis_size("seq") // slab, slab).reshape(-1, kinds, width)
    joined = jnp.einsum(
        "td,dch->tch",
        normed,
        gathered[:, :3],
        preferred_element_type=jnp.float32,
    )
    query = joined[:, 0]
    keys = joined[:, 1]
    values = joined[:, 2]
    parts = lax.axis_size("tp")
    squares = jnp.stack([jnp.sum(query * query, axis=-1), jnp.sum(keys * keys, axis=-1)])
    everyone = [(k, None) for k in range(1, parts)]
    query_sq, key_sq = jnp.sum(exchange(squares, "tp", everyone, parts, 2), axis=0)
    full_width = local_width * lax.axis_size("tp")
    query_normed = (query * lax.rsqrt(query_sq / full_width + eps)[:, None] * q_gain).astype(
        jnp.bfloat16
    )
    key_normed = (keys * lax.rsqrt(key_sq / full_width + eps)[:, None] * k_gain).astype(
        jnp.bfloat16
    )
    paired = jnp.stack([key_normed, values.astype(jnp.bfloat16)], axis=1)
    pieces = []
    for offset in (2, 1, 0, -1, -2):
        if offset == 0:
            pieces.append(paired)
        else:
            pieces.append(passed_along(paired, "seq", offset))
    widened = jnp.concatenate(pieces, axis=0)
    position = lax.axis_index("seq")
    outside = jnp.full((2 * count,), -1, jnp.int32)
    seg_pad = jnp.concatenate([outside, segment_ids, outside], axis=0)
    key_seg = lax.dynamic_slice_in_dim(seg_pad, position * count, 5 * count, 0)
    query_seg = lax.dynamic_slice_in_dim(segment_ids, position * count, count, 0)
    query_heads = query_normed.reshape(count, heads, HEAD_DIM)
    key_heads = widened[:, 0].reshape(5 * count, heads, HEAD_DIM)
    value_heads = widened[:, 1].reshape(5 * count, heads, HEAD_DIM)
    scores, mask = masked_scores(query_heads, key_heads, query_seg, key_seg)
    peak = jnp.max(scores, axis=-1, keepdims=True)
    weights = jnp.where(mask, jnp.exp(scores - peak), 0.0)
    total = jnp.sum(weights, axis=-1)
    probs = weights.astype(jnp.bfloat16)
    summed = jnp.einsum("hqk,khd->qhd", probs, value_heads, preferred_element_type=jnp.float32)
    context = (
        (summed / jnp.transpose(total)[:, :, None]).reshape(count, local_width).astype(jnp.bfloat16)
    )
    blank = jnp.zeros_like(context)
    widened_context = jnp.stack([blank, blank, blank, context], axis=1)
    chips = parts // 2
    by_owner = gathered.reshape(chips, 2, -1, *gathered.shape[1:])
    terms = jnp.einsum(
        "tkh,ycdkh->cytd", widened_context, by_owner, preferred_element_type=jnp.float32
    )
    projected = jnp.sum(
        scatter_chips(terms.astype(jnp.bfloat16)).astype(jnp.float32), axis=0
    )
    share = layer_scale.shape[0]
    residual = lax.dynamic_slice_in_dim(source, lax.axis_index("tp") * share, share, 1)
    return (residual + layer_scale * projected).astype(jnp.bfloat16)


def solution(mesh):
    return jax.shard_map(
        shards,
        mesh=mesh,
        in_specs=(
            P("seq", None),
            P(),
            P("seq", None, "tp"),
            P("tp"),
            P("tp"),
            P("tp", "seq"),
            P("tp"),
            P(),
        ),
        out_specs=P("seq", "tp"),
        check_vma=False,
    )
```

```python
import functools

import jax
import jax.numpy as jnp
from jax import lax
from jax.sharding import PartitionSpec as P
from jax.experimental import pallas as pl
from jax.experimental.pallas import tpu as pltpu

HEAD_DIM = 128


eps = 1e-06
floor_score = -1e30


def passed_along(x, axis, by):
    size = lax.axis_size(axis)
    pairs = [(i, i + by) for i in range(size) if 0 <= i + by < size]
    return lax.ppermute(x, axis, pairs)


def gather_kernel(x_ref, out_ref, pair_sems, row_sems, lane_sems, ring_sems, cross_sems, local_sem):
    rings, slab = out_ref.shape[0], out_ref.shape[1]
    pair = 2
    row = slab // pair
    rows = out_ref.shape[2]
    split = (rows * 3 + 7) // 8
    first_rows, second_rows = pl.ds(0, split), pl.ds(split, rows - split)
    me = lax.axis_index("seq")
    tp = lax.axis_index("tp")
    mesh_id = pl.DeviceIdType.MESH
    ring = me // slab
    spot = me % slab
    low = spot % pair
    across = spot // pair
    base = spot - low

    def device(r, s):
        return (r * slab + s, tp)

    ahead = (ring + 1) % rings
    behind = (ring + rings - 1) % rings
    partner = base + 1 - low
    row_spots = [((across + k) % row) * pair + low for k in range(1, row)]
    right = ((across + 1) % row) * pair + low
    left = ((across + row - 1) % row) * pair + low

    barrier = pltpu.get_barrier_semaphore()
    targets = [device(ring, partner), device(ahead, spot), device(behind, spot)]
    targets += [device(ring, s) for s in row_spots]
    for target in targets:
        pl.semaphore_signal(barrier, inc=1, device_id=target, device_id_type=mesh_id)
    pl.semaphore_wait(barrier, len(targets))

    def remote(window, target, sems, index):
        return pltpu.make_async_remote_copy(
            src_ref=window,
            dst_ref=window,
            send_sem=sems.at[(0,) + index],
            recv_sem=sems.at[(1,) + index],
            device_id=target,
            device_id_type=mesh_id,
        )

    def finish(copies):
        for copy in copies:
            copy.wait_send()
            copy.wait_recv()

    local = pltpu.make_async_copy(x_ref, out_ref.at[ring, spot], local_sem)
    local.start()
    swap = pltpu.make_async_remote_copy(
        src_ref=x_ref,
        dst_ref=out_ref.at[ring, spot],
        send_sem=pair_sems.at[0],
        recv_sem=pair_sems.at[1],
        device_id=device(ring, partner),
        device_id_type=mesh_id,
    )
    swap.start()
    local.wait()
    finish([swap])

    pair_a = out_ref.at[ring, pl.ds(base, pair), first_rows]
    rows_a = [remote(pair_a, device(ring, s), row_sems, (k,)) for k, s in enumerate(row_spots)]
    for copy in rows_a:
        copy.start()
    for t in range(rings // 2):
        last = t == rings // 2 - 1
        cw_spots = pl.ds(base, 1 if last else pair)
        ccw_spots = pl.ds(base + 1 if last else base, 1 if last else pair)
        cw = out_ref.at[(ring - t + rings) % rings, cw_spots, second_rows]
        ccw = out_ref.at[(ring + t) % rings, ccw_spots, second_rows]
        step = [
            remote(cw, device(ahead, spot), lane_sems, (0, t)),
            remote(ccw, device(behind, spot), lane_sems, (1, t)),
        ]
        for copy in step:
            copy.start()
        finish(step)
    finish(rows_a)

    half = slab // 2
    mid = rings // 2
    cross = [
        remote(out_ref.at[:, pl.ds(base, pair), second_rows], device(ring, right), cross_sems, (0, 0)),
        remote(out_ref.at[:, pl.ds(base, pair), second_rows], device(ring, left), cross_sems, (1, 0)),
    ]
    for copy in cross:
        copy.start()
    onward = None
    for t in range(rings // 2):
        last = t == rings // 2 - 1
        cw_spots = pl.ds(0, half if last else slab)
        ccw_spots = pl.ds(half if last else 0, half if last else slab)
        cw = out_ref.at[(ring - t + rings) % rings, cw_spots, first_rows]
        ccw = out_ref.at[(ring + t) % rings, ccw_spots, first_rows]
        step = [
            remote(cw, device(ahead, spot), ring_sems, (0, t)),
            remote(ccw, device(behind, spot), ring_sems, (1, t)),
        ]
        for copy in step:
            copy.start()
        finish(step)
        if t == 1:
            finish(cross)
            from_left = ((across + row - 1) % row) * pair
            from_right = ((across + 1) % row) * pair
            onward = [
                remote(
                    out_ref.at[pl.ds(0, mid), pl.ds(from_left, pair), second_rows],
                    device(ring, right),
                    cross_sems,
                    (0, 1),
                ),
                remote(
                    out_ref.at[pl.ds(mid, mid), pl.ds(from_right, pair), second_rows],
                    device(ring, left),
                    cross_sems,
                    (1, 1),
                ),
            ]
            for copy in onward:
                copy.start()
    finish(onward)


def gather_seq(block, rings, slab):
    return pl.pallas_call(
        gather_kernel,
        out_shape=jax.ShapeDtypeStruct((rings, slab) + block.shape, block.dtype),
        in_specs=[pl.BlockSpec(memory_space=pl.ANY)],
        out_specs=pl.BlockSpec(memory_space=pl.ANY),
        scratch_shapes=[
            pltpu.SemaphoreType.DMA((2,)),
            pltpu.SemaphoreType.DMA((2, slab // 2 - 1)),
            pltpu.SemaphoreType.DMA((2, 2, rings // 2)),
            pltpu.SemaphoreType.DMA((2, 2, rings // 2)),
            pltpu.SemaphoreType.DMA((2, 2, 2)),
            pltpu.SemaphoreType.DMA(()),
        ],
        compiler_params=pltpu.CompilerParams(collective_id=0, has_side_effects=True),
    )(block)


def scatter_kernel(terms_ref, out_ref, mine, incoming, sums, send_sem, recv_sem, local_sems):
    chips = out_ref.shape[0]
    seq = lax.axis_index("seq")
    tp = lax.axis_index("tp")
    mesh_id = pl.DeviceIdType.MESH
    core = tp % 2
    here = tp // 2
    owners = [(here + k) % chips for k in range(1, chips)]
    targets = [(seq, tp + 1 - 2 * core)] + [(seq, owner * 2 + core) for owner in owners]

    barrier = pltpu.get_barrier_semaphore()
    for target in targets:
        pl.semaphore_signal(barrier, inc=1, device_id=target, device_id_type=mesh_id)
    pl.semaphore_wait(barrier, len(targets))

    keep = pltpu.make_async_copy(terms_ref.at[core], mine, local_sems.at[0])
    keep.start()
    swap = pltpu.make_async_remote_copy(
        src_ref=terms_ref.at[1 - core],
        dst_ref=incoming,
        send_sem=send_sem.at[0],
        recv_sem=recv_sem.at[0],
        device_id=targets[0],
        device_id_type=mesh_id,
    )
    swap.start()
    keep.wait()
    swap.wait_send()
    swap.wait_recv()
    total = mine[...].astype(jnp.float32) + incoming[...].astype(jnp.float32)
    sums[...] = total.astype(sums.dtype)

    local = pltpu.make_async_copy(sums.at[here], out_ref.at[here], local_sems.at[1])
    local.start()
    copies = []
    for k, owner in enumerate(owners):
        copy = pltpu.make_async_remote_copy(
            src_ref=sums.at[owner],
            dst_ref=out_ref.at[here],
            send_sem=send_sem.at[k + 1],
            recv_sem=recv_sem.at[k + 1],
            device_id=targets[k + 1],
            device_id_type=mesh_id,
        )
        copy.start()
        copies.append(copy)
    for copy in copies:
        copy.wait_send()
        copy.wait_recv()
    local.wait()


def scatter_chips(terms):
    block = terms.shape[1:]
    chips = block[0]
    return pl.pallas_call(
        scatter_kernel,
        out_shape=jax.ShapeDtypeStruct(block, jnp.bfloat16),
        in_specs=[pl.BlockSpec(memory_space=pl.ANY)],
        out_specs=pl.BlockSpec(memory_space=pl.ANY),
        scratch_shapes=[
            pltpu.VMEM(block, terms.dtype),
            pltpu.VMEM(block, terms.dtype),
            pltpu.VMEM(block, jnp.bfloat16),
            pltpu.SemaphoreType.DMA((chips,)),
            pltpu.SemaphoreType.DMA((chips,)),
            pltpu.SemaphoreType.DMA((2,)),
        ],
        compiler_params=pltpu.CompilerParams(collective_id=1, has_side_effects=True),
    )(terms)


def exchange_kernel(axis, offsets, x_ref, out_ref, send_sem, recv_sem, local_sem):
    size = lax.axis_size(axis)
    me = lax.axis_index(axis)
    seq = lax.axis_index("seq")
    tp = lax.axis_index("tp")
    mesh_id = pl.DeviceIdType.MESH

    def device(position):
        return (position, tp) if axis == "seq" else (seq, position)

    def slot(entry):
        return me if entry is None else entry

    peers = [lax.rem(me + offset + size, size) for offset, _ in offsets]
    barrier = pltpu.get_barrier_semaphore()
    for peer in peers:
        pl.semaphore_signal(barrier, inc=1, device_id=device(peer), device_id_type=mesh_id)
    pl.semaphore_wait(barrier, len(peers))

    own = offsets_own_slot(offsets, me)
    local = pltpu.make_async_copy(x_ref, out_ref.at[own], local_sem)
    local.start()
    copies = []
    for k, ((_, entry), peer) in enumerate(zip(offsets, peers)):
        copy = pltpu.make_async_remote_copy(
            src_ref=x_ref,
            dst_ref=out_ref.at[slot(entry)],
            send_sem=send_sem.at[k],
            recv_sem=recv_sem.at[k],
            device_id=device(peer),
            device_id_type=mesh_id,
        )
        copy.start()
        copies.append(copy)
    for copy in copies:
        copy.wait_send()
        copy.wait_recv()
    local.wait()


def offsets_own_slot(offsets, me):
    slots = [entry for _, entry in offsets]
    if None in slots:
        return me
    return len(offsets) // 2


def exchange(block, axis, offsets, slots, collective_id):
    count = len(offsets)
    return pl.pallas_call(
        functools.partial(exchange_kernel, axis, offsets),
        out_shape=jax.ShapeDtypeStruct((slots,) + block.shape, block.dtype),
        in_specs=[pl.BlockSpec(memory_space=pl.ANY)],
        out_specs=pl.BlockSpec(memory_space=pl.ANY),
        scratch_shapes=[
            pltpu.SemaphoreType.DMA((count,)),
            pltpu.SemaphoreType.DMA((count,)),
            pltpu.SemaphoreType.DMA(()),
        ],
        compiler_params=pltpu.CompilerParams(
            collective_id=collective_id, has_side_effects=True
        ),
    )(block)


def masked_scores(query, keys, query_seg, key_seg):
    scores = jnp.einsum(
        "qhd,khd->hqk", query, keys, preferred_element_type=jnp.float32
    ) * HEAD_DIM ** (-0.5)
    mask = (query_seg[:, None] == key_seg[None, :])[None]
    return (jnp.where(mask, scores, floor_score), mask)


def shards(tokens, norm_gain, qkv_weight, q_gain, k_gain, out_weight, layer_scale, segment_ids):
    count = tokens.shape[0]
    source = tokens.astype(jnp.float32)
    normed = (
        source * lax.rsqrt(jnp.mean(source * source, axis=-1, keepdims=True) + eps) * norm_gain
    ).astype(jnp.bfloat16)
    local_width = qkv_weight.shape[2]
    heads = local_width // HEAD_DIM
    stacked = jnp.concatenate([qkv_weight, jnp.transpose(out_weight)[:, None, :]], axis=1)
    rows, kinds, width = stacked.shape
    slab = 8
    gathered = gather_seq(stacked, lax.axis_size("seq") // slab, slab).reshape(-1, kinds, width)
    joined = jnp.einsum(
        "td,dch->tch",
        normed,
        gathered[:, :3],
        preferred_element_type=jnp.float32,
    )
    query = joined[:, 0]
    keys = joined[:, 1]
    values = joined[:, 2]
    parts = lax.axis_size("tp")
    squares = jnp.stack([jnp.sum(query * query, axis=-1), jnp.sum(keys * keys, axis=-1)])
    everyone = [(k, None) for k in range(1, parts)]
    query_sq, key_sq = jnp.sum(exchange(squares, "tp", everyone, parts, 2), axis=0)
    full_width = local_width * lax.axis_size("tp")
    query_normed = (query * lax.rsqrt(query_sq / full_width + eps)[:, None] * q_gain).astype(
        jnp.bfloat16
    )
    key_normed = (keys * lax.rsqrt(key_sq / full_width + eps)[:, None] * k_gain).astype(
        jnp.bfloat16
    )
    paired = jnp.stack([key_normed, values.astype(jnp.bfloat16)], axis=1)
    pieces = []
    for offset in (2, 1, 0, -1, -2):
        if offset == 0:
            pieces.append(paired)
        else:
            pieces.append(passed_along(paired, "seq", offset))
    widened = jnp.concatenate(pieces, axis=0)
    position = lax.axis_index("seq")
    outside = jnp.full((2 * count,), -1, jnp.int32)
    seg_pad = jnp.concatenate([outside, segment_ids, outside], axis=0)
    key_seg = lax.dynamic_slice_in_dim(seg_pad, position * count, 5 * count, 0)
    query_seg = lax.dynamic_slice_in_dim(segment_ids, position * count, count, 0)
    query_heads = query_normed.reshape(count, heads, HEAD_DIM)
    key_heads = widened[:, 0].reshape(5 * count, heads, HEAD_DIM)
    value_heads = widened[:, 1].reshape(5 * count, heads, HEAD_DIM)
    scores, mask = masked_scores(query_heads, key_heads, query_seg, key_seg)
    peak = jnp.max(scores, axis=-1, keepdims=True)
    weights = jnp.where(mask, jnp.exp(scores - peak), 0.0)
    total = jnp.sum(weights, axis=-1)
    probs = weights.astype(jnp.bfloat16)
    summed = jnp.einsum("hqk,khd->qhd", probs, value_heads, preferred_element_type=jnp.float32)
    context = (
        (summed / jnp.transpose(total)[:, :, None]).reshape(count, local_width).astype(jnp.bfloat16)
    )
    blank = jnp.zeros_like(context)
    widened_context = jnp.stack([blank, blank, blank, context], axis=1)
    chips = parts // 2
    by_owner = gathered.reshape(chips, 2, -1, *gathered.shape[1:])
    terms = jnp.einsum(
        "tkh,ycdkh->cytd", widened_context, by_owner, preferred_element_type=jnp.float32
    )
    projected = jnp.sum(
        scatter_chips(terms.astype(jnp.bfloat16)).astype(jnp.float32), axis=0
    )
    share = layer_scale.shape[0]
    residual = lax.dynamic_slice_in_dim(source, lax.axis_index("tp") * share, share, 1)
    return (residual + layer_scale * projected).astype(jnp.bfloat16)


def solution(mesh):
    return jax.shard_map(
        shards,
        mesh=mesh,
        in_specs=(
            P("seq", None),
            P(),
            P("seq", None, "tp"),
            P("tp"),
            P("tp"),
            P("tp", "seq"),
            P("tp"),
            P(),
        ),
        out_specs=P("seq", "tp"),
        check_vma=False,
    )
```

```python
import functools

import jax
import jax.numpy as jnp
from jax import lax
from jax.sharding import PartitionSpec as P
from jax.experimental import pallas as pl
from jax.experimental.pallas import tpu as pltpu

HEAD_DIM = 128


eps = 1e-06
floor_score = -1e30


def passed_along(x, axis, by):
    size = lax.axis_size(axis)
    pairs = [(i, i + by) for i in range(size) if 0 <= i + by < size]
    return lax.ppermute(x, axis, pairs)


def gather_kernel(x_ref, out_ref, pair_sems, row_sems, lane_sems, ring_sems, cross_sems, local_sem):
    rings, slab = out_ref.shape[0], out_ref.shape[1]
    pair = 2
    row = slab // pair
    rows = out_ref.shape[2]
    split = (rows * 3 + 7) // 8
    first_rows, second_rows = pl.ds(0, split), pl.ds(split, rows - split)
    me = lax.axis_index("seq")
    tp = lax.axis_index("tp")
    mesh_id = pl.DeviceIdType.MESH
    ring = me // slab
    spot = me % slab
    low = spot % pair
    across = spot // pair
    base = spot - low

    def device(r, s):
        return (r * slab + s, tp)

    ahead = (ring + 1) % rings
    behind = (ring + rings - 1) % rings
    partner = base + 1 - low
    row_spots = [((across + k) % row) * pair + low for k in range(1, row)]
    right = ((across + 1) % row) * pair + low
    left = ((across + row - 1) % row) * pair + low

    barrier = pltpu.get_barrier_semaphore()
    targets = [device(ring, partner), device(ahead, spot), device(behind, spot)]
    targets += [device(ring, s) for s in row_spots]
    for target in targets:
        pl.semaphore_signal(barrier, inc=1, device_id=target, device_id_type=mesh_id)
    pl.semaphore_wait(barrier, len(targets))

    def remote(window, target, sems, index):
        return pltpu.make_async_remote_copy(
            src_ref=window,
            dst_ref=window,
            send_sem=sems.at[(0,) + index],
            recv_sem=sems.at[(1,) + index],
            device_id=target,
            device_id_type=mesh_id,
        )

    def finish(copies):
        for copy in copies:
            copy.wait_send()
            copy.wait_recv()

    local = pltpu.make_async_copy(x_ref, out_ref.at[ring, spot], local_sem)
    local.start()
    swap = pltpu.make_async_remote_copy(
        src_ref=x_ref,
        dst_ref=out_ref.at[ring, spot],
        send_sem=pair_sems.at[0],
        recv_sem=pair_sems.at[1],
        device_id=device(ring, partner),
        device_id_type=mesh_id,
    )
    swap.start()
    local.wait()
    finish([swap])

    pair_a = out_ref.at[ring, pl.ds(base, pair), first_rows]
    rows_a = [remote(pair_a, device(ring, s), row_sems, (k,)) for k, s in enumerate(row_spots)]
    for copy in rows_a:
        copy.start()
    for t in range(rings // 2):
        last = t == rings // 2 - 1
        cw_spots = pl.ds(base, 1 if last else pair)
        ccw_spots = pl.ds(base + 1 if last else base, 1 if last else pair)
        cw = out_ref.at[(ring - t + rings) % rings, cw_spots, second_rows]
        ccw = out_ref.at[(ring + t) % rings, ccw_spots, second_rows]
        step = [
            remote(cw, device(ahead, spot), lane_sems, (0, t)),
            remote(ccw, device(behind, spot), lane_sems, (1, t)),
        ]
        for copy in step:
            copy.start()
        finish(step)
    finish(rows_a)

    half = slab // 2
    mid = rings // 2
    cross = [
        remote(out_ref.at[:, pl.ds(base, pair), second_rows], device(ring, right), cross_sems, (0, 0)),
        remote(out_ref.at[:, pl.ds(base, pair), second_rows], device(ring, left), cross_sems, (1, 0)),
    ]
    for copy in cross:
        copy.start()
    onward = None
    for t in range(rings // 2):
        last = t == rings // 2 - 1
        cw_spots = pl.ds(0, half if last else slab)
        ccw_spots = pl.ds(half if last else 0, half if last else slab)
        cw = out_ref.at[(ring - t + rings) % rings, cw_spots, first_rows]
        ccw = out_ref.at[(ring + t) % rings, ccw_spots, first_rows]
        step = [
            remote(cw, device(ahead, spot), ring_sems, (0, t)),
            remote(ccw, device(behind, spot), ring_sems, (1, t)),
        ]
        for copy in step:
            copy.start()
        finish(step)
        if t == 1:
            finish(cross)
            from_left = ((across + row - 1) % row) * pair
            from_right = ((across + 1) % row) * pair
            onward = [
                remote(
                    out_ref.at[pl.ds(0, mid), pl.ds(from_left, pair), second_rows],
                    device(ring, right),
                    cross_sems,
                    (0, 1),
                ),
                remote(
                    out_ref.at[pl.ds(mid, mid), pl.ds(from_right, pair), second_rows],
                    device(ring, left),
                    cross_sems,
                    (1, 1),
                ),
            ]
            for copy in onward:
                copy.start()
    finish(onward)


def gather_seq(block, rings, slab):
    return pl.pallas_call(
        gather_kernel,
        out_shape=jax.ShapeDtypeStruct((rings, slab) + block.shape, block.dtype),
        in_specs=[pl.BlockSpec(memory_space=pl.ANY)],
        out_specs=pl.BlockSpec(memory_space=pl.ANY),
        scratch_shapes=[
            pltpu.SemaphoreType.DMA((2,)),
            pltpu.SemaphoreType.DMA((2, slab // 2 - 1)),
            pltpu.SemaphoreType.DMA((2, 2, rings // 2)),
            pltpu.SemaphoreType.DMA((2, 2, rings // 2)),
            pltpu.SemaphoreType.DMA((2, 2, 2)),
            pltpu.SemaphoreType.DMA(()),
        ],
        compiler_params=pltpu.CompilerParams(collective_id=0, has_side_effects=True),
    )(block)


def scatter_kernel(terms_ref, out_ref, mine, incoming, sums, send_sem, recv_sem, local_sems):
    chips = out_ref.shape[0]
    seq = lax.axis_index("seq")
    tp = lax.axis_index("tp")
    mesh_id = pl.DeviceIdType.MESH
    core = tp % 2
    here = tp // 2
    owners = [(here + k) % chips for k in range(1, chips)]
    targets = [(seq, tp + 1 - 2 * core)] + [(seq, owner * 2 + core) for owner in owners]

    barrier = pltpu.get_barrier_semaphore()
    for target in targets:
        pl.semaphore_signal(barrier, inc=1, device_id=target, device_id_type=mesh_id)
    pl.semaphore_wait(barrier, len(targets))

    keep = pltpu.make_async_copy(terms_ref.at[core], mine, local_sems.at[0])
    keep.start()
    swap = pltpu.make_async_remote_copy(
        src_ref=terms_ref.at[1 - core],
        dst_ref=incoming,
        send_sem=send_sem.at[0],
        recv_sem=recv_sem.at[0],
        device_id=targets[0],
        device_id_type=mesh_id,
    )
    swap.start()
    keep.wait()
    swap.wait_send()
    swap.wait_recv()
    total = mine[...].astype(jnp.float32) + incoming[...].astype(jnp.float32)
    sums[...] = total.astype(sums.dtype)

    local = pltpu.make_async_copy(sums.at[here], out_ref.at[here], local_sems.at[1])
    local.start()
    copies = []
    for k, owner in enumerate(owners):
        copy = pltpu.make_async_remote_copy(
            src_ref=sums.at[owner],
            dst_ref=out_ref.at[here],
            send_sem=send_sem.at[k + 1],
            recv_sem=recv_sem.at[k + 1],
            device_id=targets[k + 1],
            device_id_type=mesh_id,
        )
        copy.start()
        copies.append(copy)
    for copy in copies:
        copy.wait_send()
        copy.wait_recv()
    local.wait()


def scatter_chips(terms):
    block = terms.shape[1:]
    chips = block[0]
    return pl.pallas_call(
        scatter_kernel,
        out_shape=jax.ShapeDtypeStruct(block, jnp.bfloat16),
        in_specs=[pl.BlockSpec(memory_space=pl.ANY)],
        out_specs=pl.BlockSpec(memory_space=pl.ANY),
        scratch_shapes=[
            pltpu.VMEM(block, terms.dtype),
            pltpu.VMEM(block, terms.dtype),
            pltpu.VMEM(block, jnp.bfloat16),
            pltpu.SemaphoreType.DMA((chips,)),
            pltpu.SemaphoreType.DMA((chips,)),
            pltpu.SemaphoreType.DMA((2,)),
        ],
        compiler_params=pltpu.CompilerParams(collective_id=1, has_side_effects=True),
    )(terms)


def exchange_kernel(axis, offsets, x_ref, out_ref, send_sem, recv_sem, local_sem):
    size = lax.axis_size(axis)
    me = lax.axis_index(axis)
    seq = lax.axis_index("seq")
    tp = lax.axis_index("tp")
    mesh_id = pl.DeviceIdType.MESH

    def device(position):
        return (position, tp) if axis == "seq" else (seq, position)

    def slot(entry):
        return me if entry is None else entry

    peers = [lax.rem(me + offset + size, size) for offset, _ in offsets]
    barrier = pltpu.get_barrier_semaphore()
    for peer in peers:
        pl.semaphore_signal(barrier, inc=1, device_id=device(peer), device_id_type=mesh_id)
    pl.semaphore_wait(barrier, len(peers))

    own = offsets_own_slot(offsets, me)
    local = pltpu.make_async_copy(x_ref, out_ref.at[own], local_sem)
    local.start()
    copies = []
    for k, ((_, entry), peer) in enumerate(zip(offsets, peers)):
        copy = pltpu.make_async_remote_copy(
            src_ref=x_ref,
            dst_ref=out_ref.at[slot(entry)],
            send_sem=send_sem.at[k],
            recv_sem=recv_sem.at[k],
            device_id=device(peer),
            device_id_type=mesh_id,
        )
        copy.start()
        copies.append(copy)
    for copy in copies:
        copy.wait_send()
        copy.wait_recv()
    local.wait()


def offsets_own_slot(offsets, me):
    slots = [entry for _, entry in offsets]
    if None in slots:
        return me
    return len(offsets) // 2


def exchange(block, axis, offsets, slots, collective_id):
    count = len(offsets)
    return pl.pallas_call(
        functools.partial(exchange_kernel, axis, offsets),
        out_shape=jax.ShapeDtypeStruct((slots,) + block.shape, block.dtype),
        in_specs=[pl.BlockSpec(memory_space=pl.ANY)],
        out_specs=pl.BlockSpec(memory_space=pl.ANY),
        scratch_shapes=[
            pltpu.SemaphoreType.DMA((count,)),
            pltpu.SemaphoreType.DMA((count,)),
            pltpu.SemaphoreType.DMA(()),
        ],
        compiler_params=pltpu.CompilerParams(
            collective_id=collective_id, has_side_effects=True
        ),
    )(block)


def masked_scores(query, keys, query_seg, key_seg):
    scores = jnp.einsum(
        "qhd,khd->hqk", query, keys, preferred_element_type=jnp.float32
    ) * HEAD_DIM ** (-0.5)
    mask = (query_seg[:, None] == key_seg[None, :])[None]
    return (jnp.where(mask, scores, floor_score), mask)


def shards(tokens, norm_gain, qkv_weight, q_gain, k_gain, out_weight, layer_scale, segment_ids):
    count = tokens.shape[0]
    source = tokens.astype(jnp.float32)
    normed = (
        source * lax.rsqrt(jnp.mean(source * source, axis=-1, keepdims=True) + eps) * norm_gain
    ).astype(jnp.bfloat16)
    local_width = qkv_weight.shape[2]
    heads = local_width // HEAD_DIM
    stacked = jnp.concatenate([qkv_weight, jnp.transpose(out_weight)[:, None, :]], axis=1)
    rows, kinds, width = stacked.shape
    slab = 8
    gathered = gather_seq(stacked, lax.axis_size("seq") // slab, slab).reshape(-1, kinds, width)
    joined = jnp.einsum(
        "td,dch->tch",
        normed,
        gathered[:, :3],
        preferred_element_type=jnp.float32,
    )
    query = joined[:, 0]
    keys = joined[:, 1]
    values = joined[:, 2]
    values_low = values.astype(jnp.bfloat16)
    value_pieces = {
        offset: passed_along(values_low, "seq", offset) for offset in (2, 1, -1, -2)
    }
    parts = lax.axis_size("tp")
    squares = jnp.stack([jnp.sum(query * query, axis=-1), jnp.sum(keys * keys, axis=-1)])
    everyone = [(k, None) for k in range(1, parts)]
    query_sq, key_sq = jnp.sum(exchange(squares, "tp", everyone, parts, 2), axis=0)
    full_width = local_width * lax.axis_size("tp")
    query_normed = (query * lax.rsqrt(query_sq / full_width + eps)[:, None] * q_gain).astype(
        jnp.bfloat16
    )
    key_normed = (keys * lax.rsqrt(key_sq / full_width + eps)[:, None] * k_gain).astype(
        jnp.bfloat16
    )
    key_pieces = []
    value_list = []
    for offset in (2, 1, 0, -1, -2):
        if offset == 0:
            key_pieces.append(key_normed)
            value_list.append(values_low)
        else:
            key_pieces.append(passed_along(key_normed, "seq", offset))
            value_list.append(value_pieces[offset])
    wide_keys = jnp.concatenate(key_pieces, axis=0)
    wide_values = jnp.concatenate(value_list, axis=0)
    position = lax.axis_index("seq")
    outside = jnp.full((2 * count,), -1, jnp.int32)
    seg_pad = jnp.concatenate([outside, segment_ids, outside], axis=0)
    key_seg = lax.dynamic_slice_in_dim(seg_pad, position * count, 5 * count, 0)
    query_seg = lax.dynamic_slice_in_dim(segment_ids, position * count, count, 0)
    query_heads = query_normed.reshape(count, heads, HEAD_DIM)
    key_heads = wide_keys.reshape(5 * count, heads, HEAD_DIM)
    value_heads = wide_values.reshape(5 * count, heads, HEAD_DIM)
    scores, mask = masked_scores(query_heads, key_heads, query_seg, key_seg)
    peak = jnp.max(scores, axis=-1, keepdims=True)
    weights = jnp.where(mask, jnp.exp(scores - peak), 0.0)
    total = jnp.sum(weights, axis=-1)
    probs = weights.astype(jnp.bfloat16)
    summed = jnp.einsum("hqk,khd->qhd", probs, value_heads, preferred_element_type=jnp.float32)
    context = (
        (summed / jnp.transpose(total)[:, :, None]).reshape(count, local_width).astype(jnp.bfloat16)
    )
    blank = jnp.zeros_like(context)
    widened_context = jnp.stack([blank, blank, blank, context], axis=1)
    chips = parts // 2
    by_owner = gathered.reshape(chips, 2, -1, *gathered.shape[1:])
    terms = jnp.einsum(
        "tkh,ycdkh->cytd", widened_context, by_owner, preferred_element_type=jnp.float32
    )
    projected = jnp.sum(
        scatter_chips(terms.astype(jnp.bfloat16)).astype(jnp.float32), axis=0
    )
    share = layer_scale.shape[0]
    residual = lax.dynamic_slice_in_dim(source, lax.axis_index("tp") * share, share, 1)
    return (residual + layer_scale * projected).astype(jnp.bfloat16)


def solution(mesh):
    return jax.shard_map(
        shards,
        mesh=mesh,
        in_specs=(
            P("seq", None),
            P(),
            P("seq", None, "tp"),
            P("tp"),
            P("tp"),
            P("tp", "seq"),
            P("tp"),
            P(),
        ),
        out_specs=P("seq", "tp"),
        check_vma=False,
    )
```

```python
import functools

import jax
import jax.numpy as jnp
from jax import lax
from jax.sharding import PartitionSpec as P
from jax.experimental import pallas as pl
from jax.experimental.pallas import tpu as pltpu

HEAD_DIM = 128


eps = 1e-06
floor_score = -1e30


def passed_along(x, axis, by):
    size = lax.axis_size(axis)
    pairs = [(i, i + by) for i in range(size) if 0 <= i + by < size]
    return lax.ppermute(x, axis, pairs)


def gather_kernel(x_ref, out_ref, pair_sems, row_sems, lane_sems, ring_sems, cross_sems, local_sem):
    rings, slab = out_ref.shape[0], out_ref.shape[1]
    pair = 2
    row = slab // pair
    lanes = out_ref.shape[-1] // 2
    first_lanes, second_lanes = pl.ds(0, lanes), pl.ds(lanes, lanes)
    me = lax.axis_index("seq")
    tp = lax.axis_index("tp")
    mesh_id = pl.DeviceIdType.MESH
    ring = me // slab
    spot = me % slab
    low = spot % pair
    across = spot // pair
    base = spot - low

    def device(r, s):
        return (r * slab + s, tp)

    ahead = (ring + 1) % rings
    behind = (ring + rings - 1) % rings
    partner = base + 1 - low
    row_spots = [((across + k) % row) * pair + low for k in range(1, row)]
    right = ((across + 1) % row) * pair + low
    left = ((across + row - 1) % row) * pair + low

    barrier = pltpu.get_barrier_semaphore()
    targets = [device(ring, partner), device(ahead, spot), device(behind, spot)]
    targets += [device(ring, s) for s in row_spots]
    for target in targets:
        pl.semaphore_signal(barrier, inc=1, device_id=target, device_id_type=mesh_id)
    pl.semaphore_wait(barrier, len(targets))

    def remote(window, target, sems, index):
        return pltpu.make_async_remote_copy(
            src_ref=window,
            dst_ref=window,
            send_sem=sems.at[(0,) + index],
            recv_sem=sems.at[(1,) + index],
            device_id=target,
            device_id_type=mesh_id,
        )

    def finish(copies):
        for copy in copies:
            copy.wait_send()
            copy.wait_recv()

    local = pltpu.make_async_copy(x_ref, out_ref.at[ring, spot], local_sem)
    local.start()
    swap = pltpu.make_async_remote_copy(
        src_ref=x_ref,
        dst_ref=out_ref.at[ring, spot],
        send_sem=pair_sems.at[0],
        recv_sem=pair_sems.at[1],
        device_id=device(ring, partner),
        device_id_type=mesh_id,
    )
    swap.start()
    local.wait()
    finish([swap])

    pair_a = out_ref.at[ring, pl.ds(base, pair), :, :, first_lanes]
    rows_a = [remote(pair_a, device(ring, s), row_sems, (k,)) for k, s in enumerate(row_spots)]
    for copy in rows_a:
        copy.start()
    for t in range(rings // 2):
        last = t == rings // 2 - 1
        cw_spots = pl.ds(base, 1 if last else pair)
        ccw_spots = pl.ds(base + 1 if last else base, 1 if last else pair)
        cw = out_ref.at[(ring - t + rings) % rings, cw_spots, :, :, second_lanes]
        ccw = out_ref.at[(ring + t) % rings, ccw_spots, :, :, second_lanes]
        step = [
            remote(cw, device(ahead, spot), lane_sems, (0, t)),
            remote(ccw, device(behind, spot), lane_sems, (1, t)),
        ]
        for copy in step:
            copy.start()
        finish(step)
    finish(rows_a)

    half = slab // 2
    mid = rings // 2
    cross = [
        remote(out_ref.at[:, pl.ds(base, pair), :, :, second_lanes], device(ring, right), cross_sems, (0, 0)),
        remote(out_ref.at[:, pl.ds(base, pair), :, :, second_lanes], device(ring, left), cross_sems, (1, 0)),
    ]
    for copy in cross:
        copy.start()
    onward = None
    for t in range(rings // 2):
        last = t == rings // 2 - 1
        cw_spots = pl.ds(0, half if last else slab)
        ccw_spots = pl.ds(half if last else 0, half if last else slab)
        cw = out_ref.at[(ring - t + rings) % rings, cw_spots, :, :, first_lanes]
        ccw = out_ref.at[(ring + t) % rings, ccw_spots, :, :, first_lanes]
        step = [
            remote(cw, device(ahead, spot), ring_sems, (0, t)),
            remote(ccw, device(behind, spot), ring_sems, (1, t)),
        ]
        for copy in step:
            copy.start()
        finish(step)
        if t == 1:
            finish(cross)
            from_left = ((across + row - 1) % row) * pair
            from_right = ((across + 1) % row) * pair
            onward = [
                remote(
                    out_ref.at[pl.ds(0, mid), pl.ds(from_left, pair), :, :, second_lanes],
                    device(ring, right),
                    cross_sems,
                    (0, 1),
                ),
                remote(
                    out_ref.at[pl.ds(mid, mid), pl.ds(from_right, pair), :, :, second_lanes],
                    device(ring, left),
                    cross_sems,
                    (1, 1),
                ),
            ]
            for copy in onward:
                copy.start()
    finish(onward)


def gather_seq(block, rings, slab):
    return pl.pallas_call(
        gather_kernel,
        out_shape=jax.ShapeDtypeStruct((rings, slab) + block.shape, block.dtype),
        in_specs=[pl.BlockSpec(memory_space=pl.ANY)],
        out_specs=pl.BlockSpec(memory_space=pl.ANY),
        scratch_shapes=[
            pltpu.SemaphoreType.DMA((2,)),
            pltpu.SemaphoreType.DMA((2, slab // 2 - 1)),
            pltpu.SemaphoreType.DMA((2, 2, rings // 2)),
            pltpu.SemaphoreType.DMA((2, 2, rings // 2)),
            pltpu.SemaphoreType.DMA((2, 2, 2)),
            pltpu.SemaphoreType.DMA(()),
        ],
        compiler_params=pltpu.CompilerParams(collective_id=0, has_side_effects=True),
    )(block)


def scatter_kernel(terms_ref, out_ref, mine, incoming, sums, send_sem, recv_sem, local_sems):
    chips = out_ref.shape[0]
    seq = lax.axis_index("seq")
    tp = lax.axis_index("tp")
    mesh_id = pl.DeviceIdType.MESH
    core = tp % 2
    here = tp // 2
    owners = [(here + k) % chips for k in range(1, chips)]
    targets = [(seq, tp + 1 - 2 * core)] + [(seq, owner * 2 + core) for owner in owners]

    barrier = pltpu.get_barrier_semaphore()
    for target in targets:
        pl.semaphore_signal(barrier, inc=1, device_id=target, device_id_type=mesh_id)
    pl.semaphore_wait(barrier, len(targets))

    keep = pltpu.make_async_copy(terms_ref.at[core], mine, local_sems.at[0])
    keep.start()
    swap = pltpu.make_async_remote_copy(
        src_ref=terms_ref.at[1 - core],
        dst_ref=incoming,
        send_sem=send_sem.at[0],
        recv_sem=recv_sem.at[0],
        device_id=targets[0],
        device_id_type=mesh_id,
    )
    swap.start()
    keep.wait()
    swap.wait_send()
    swap.wait_recv()
    total = mine[...].astype(jnp.float32) + incoming[...].astype(jnp.float32)
    sums[...] = total.astype(sums.dtype)

    local = pltpu.make_async_copy(sums.at[here], out_ref.at[here], local_sems.at[1])
    local.start()
    copies = []
    for k, owner in enumerate(owners):
        copy = pltpu.make_async_remote_copy(
            src_ref=sums.at[owner],
            dst_ref=out_ref.at[here],
            send_sem=send_sem.at[k + 1],
            recv_sem=recv_sem.at[k + 1],
            device_id=targets[k + 1],
            device_id_type=mesh_id,
        )
        copy.start()
        copies.append(copy)
    for copy in copies:
        copy.wait_send()
        copy.wait_recv()
    local.wait()


def scatter_chips(terms):
    block = terms.shape[1:]
    chips = block[0]
    return pl.pallas_call(
        scatter_kernel,
        out_shape=jax.ShapeDtypeStruct(block, jnp.bfloat16),
        in_specs=[pl.BlockSpec(memory_space=pl.ANY)],
        out_specs=pl.BlockSpec(memory_space=pl.ANY),
        scratch_shapes=[
            pltpu.VMEM(block, terms.dtype),
            pltpu.VMEM(block, terms.dtype),
            pltpu.VMEM(block, jnp.bfloat16),
            pltpu.SemaphoreType.DMA((chips,)),
            pltpu.SemaphoreType.DMA((chips,)),
            pltpu.SemaphoreType.DMA((2,)),
        ],
        compiler_params=pltpu.CompilerParams(collective_id=1, has_side_effects=True),
    )(terms)


def exchange_kernel(axis, offsets, x_ref, out_ref, send_sem, recv_sem, local_sem):
    size = lax.axis_size(axis)
    me = lax.axis_index(axis)
    seq = lax.axis_index("seq")
    tp = lax.axis_index("tp")
    mesh_id = pl.DeviceIdType.MESH

    def device(position):
        return (position, tp) if axis == "seq" else (seq, position)

    def slot(entry):
        return me if entry is None else entry

    peers = [lax.rem(me + offset + size, size) for offset, _ in offsets]
    barrier = pltpu.get_barrier_semaphore()
    for peer in peers:
        pl.semaphore_signal(barrier, inc=1, device_id=device(peer), device_id_type=mesh_id)
    pl.semaphore_wait(barrier, len(peers))

    own = offsets_own_slot(offsets, me)
    local = pltpu.make_async_copy(x_ref, out_ref.at[own], local_sem)
    local.start()
    copies = []
    for k, ((_, entry), peer) in enumerate(zip(offsets, peers)):
        copy = pltpu.make_async_remote_copy(
            src_ref=x_ref,
            dst_ref=out_ref.at[slot(entry)],
            send_sem=send_sem.at[k],
            recv_sem=recv_sem.at[k],
            device_id=device(peer),
            device_id_type=mesh_id,
        )
        copy.start()
        copies.append(copy)
    for copy in copies:
        copy.wait_send()
        copy.wait_recv()
    local.wait()


def offsets_own_slot(offsets, me):
    slots = [entry for _, entry in offsets]
    if None in slots:
        return me
    return len(offsets) // 2


def exchange(block, axis, offsets, slots, collective_id):
    count = len(offsets)
    return pl.pallas_call(
        functools.partial(exchange_kernel, axis, offsets),
        out_shape=jax.ShapeDtypeStruct((slots,) + block.shape, block.dtype),
        in_specs=[pl.BlockSpec(memory_space=pl.ANY)],
        out_specs=pl.BlockSpec(memory_space=pl.ANY),
        scratch_shapes=[
            pltpu.SemaphoreType.DMA((count,)),
            pltpu.SemaphoreType.DMA((count,)),
            pltpu.SemaphoreType.DMA(()),
        ],
        compiler_params=pltpu.CompilerParams(
            collective_id=collective_id, has_side_effects=True
        ),
    )(block)


def masked_scores(query, keys, query_seg, key_seg):
    scores = jnp.einsum(
        "qhd,khd->hqk", query, keys, preferred_element_type=jnp.float32
    ) * HEAD_DIM ** (-0.5)
    mask = (query_seg[:, None] == key_seg[None, :])[None]
    return (jnp.where(mask, scores, floor_score), mask)


def shards(tokens, norm_gain, qkv_weight, q_gain, k_gain, out_weight, layer_scale, segment_ids):
    count = tokens.shape[0]
    source = tokens.astype(jnp.float32)
    normed = (
        source * lax.rsqrt(jnp.mean(source * source, axis=-1, keepdims=True) + eps) * norm_gain
    ).astype(jnp.bfloat16)
    local_width = qkv_weight.shape[2]
    heads = local_width // HEAD_DIM
    stacked = jnp.concatenate([qkv_weight, jnp.transpose(out_weight)[:, None, :]], axis=1)
    rows, kinds, width = stacked.shape
    slab = 8
    gathered = gather_seq(stacked, lax.axis_size("seq") // slab, slab).reshape(-1, kinds, width)
    joined = jnp.einsum(
        "td,dch->tch",
        normed,
        gathered[:, :3],
        preferred_element_type=jnp.float32,
    )
    query = joined[:, 0]
    keys = joined[:, 1]
    values = joined[:, 2]
    parts = lax.axis_size("tp")
    squares = jnp.stack([jnp.sum(query * query, axis=-1), jnp.sum(keys * keys, axis=-1)])
    everyone = [(k, None) for k in range(1, parts)]
    query_sq, key_sq = jnp.sum(exchange(squares, "tp", everyone, parts, 2), axis=0)
    full_width = local_width * lax.axis_size("tp")
    query_normed = (query * lax.rsqrt(query_sq / full_width + eps)[:, None] * q_gain).astype(
        jnp.bfloat16
    )
    key_normed = (keys * lax.rsqrt(key_sq / full_width + eps)[:, None] * k_gain).astype(
        jnp.bfloat16
    )
    paired = jnp.stack([key_normed, values.astype(jnp.bfloat16)], axis=1)
    pieces = []
    for offset in (2, 1, 0, -1, -2):
        if offset == 0:
            pieces.append(paired)
        else:
            pieces.append(passed_along(paired, "seq", offset))
    widened = jnp.concatenate(pieces, axis=0)
    position = lax.axis_index("seq")
    outside = jnp.full((2 * count,), -1, jnp.int32)
    seg_pad = jnp.concatenate([outside, segment_ids, outside], axis=0)
    key_seg = lax.dynamic_slice_in_dim(seg_pad, position * count, 5 * count, 0)
    query_seg = lax.dynamic_slice_in_dim(segment_ids, position * count, count, 0)
    query_heads = query_normed.reshape(count, heads, HEAD_DIM)
    key_heads = widened[:, 0].reshape(5 * count, heads, HEAD_DIM)
    value_heads = widened[:, 1].reshape(5 * count, heads, HEAD_DIM)
    scores, mask = masked_scores(query_heads, key_heads, query_seg, key_seg)
    peak = jnp.max(scores, axis=-1, keepdims=True)
    weights = jnp.where(mask, jnp.exp(scores - peak), 0.0)
    total = jnp.sum(weights, axis=-1)
    probs = weights.astype(jnp.bfloat16)
    summed = jnp.einsum("hqk,khd->qhd", probs, value_heads, preferred_element_type=jnp.float32)
    context = (
        (summed / jnp.transpose(total)[:, :, None]).reshape(count, local_width).astype(jnp.bfloat16)
    )
    blank = jnp.zeros_like(context)
    widened_context = jnp.stack([blank, blank, blank, context], axis=1)
    chips = parts // 2
    by_owner = gathered.reshape(chips, 2, -1, *gathered.shape[1:])
    terms = jnp.einsum(
        "tkh,ycdkh->cydt", widened_context, by_owner, preferred_element_type=jnp.float32
    )
    projected = jnp.transpose(
        jnp.sum(scatter_chips(terms.astype(jnp.bfloat16)).astype(jnp.float32), axis=0)
    )
    share = layer_scale.shape[0]
    residual = lax.dynamic_slice_in_dim(source, lax.axis_index("tp") * share, share, 1)
    return (residual + layer_scale * projected).astype(jnp.bfloat16)


def solution(mesh):
    return jax.shard_map(
        shards,
        mesh=mesh,
        in_specs=(
            P("seq", None),
            P(),
            P("seq", None, "tp"),
            P("tp"),
            P("tp"),
            P("tp", "seq"),
            P("tp"),
            P(),
        ),
        out_specs=P("seq", "tp"),
        check_vma=False,
    )
```

```python
import functools

import jax
import jax.numpy as jnp
from jax import lax
from jax.sharding import PartitionSpec as P
from jax.experimental import pallas as pl
from jax.experimental.pallas import tpu as pltpu

HEAD_DIM = 128


eps = 1e-06
floor_score = -1e30


def passed_along(x, axis, by):
    size = lax.axis_size(axis)
    pairs = [(i, (i + by) % size) for i in range(size)]
    return lax.ppermute(x, axis, pairs)


def gather_kernel(x_ref, out_ref, pair_sems, row_sems, lane_sems, ring_sems, cross_sems, local_sem):
    rings, slab = out_ref.shape[0], out_ref.shape[1]
    pair = 2
    row = slab // pair
    lanes = out_ref.shape[-1] // 2
    first_lanes, second_lanes = pl.ds(0, lanes), pl.ds(lanes, lanes)
    me = lax.axis_index("seq")
    tp = lax.axis_index("tp")
    mesh_id = pl.DeviceIdType.MESH
    ring = me // slab
    spot = me % slab
    low = spot % pair
    across = spot // pair
    base = spot - low

    def device(r, s):
        return (r * slab + s, tp)

    ahead = (ring + 1) % rings
    behind = (ring + rings - 1) % rings
    partner = base + 1 - low
    row_spots = [((across + k) % row) * pair + low for k in range(1, row)]
    right = ((across + 1) % row) * pair + low
    left = ((across + row - 1) % row) * pair + low

    barrier = pltpu.get_barrier_semaphore()
    targets = [device(ring, partner), device(ahead, spot), device(behind, spot)]
    targets += [device(ring, s) for s in row_spots]
    for target in targets:
        pl.semaphore_signal(barrier, inc=1, device_id=target, device_id_type=mesh_id)
    pl.semaphore_wait(barrier, len(targets))

    def remote(window, target, sems, index):
        return pltpu.make_async_remote_copy(
            src_ref=window,
            dst_ref=window,
            send_sem=sems.at[(0,) + index],
            recv_sem=sems.at[(1,) + index],
            device_id=target,
            device_id_type=mesh_id,
        )

    def finish(copies):
        for copy in copies:
            copy.wait_send()
            copy.wait_recv()

    local = pltpu.make_async_copy(x_ref, out_ref.at[ring, spot], local_sem)
    local.start()
    swap = pltpu.make_async_remote_copy(
        src_ref=x_ref,
        dst_ref=out_ref.at[ring, spot],
        send_sem=pair_sems.at[0],
        recv_sem=pair_sems.at[1],
        device_id=device(ring, partner),
        device_id_type=mesh_id,
    )
    swap.start()
    local.wait()
    finish([swap])

    pair_a = out_ref.at[ring, pl.ds(base, pair), :, :, first_lanes]
    rows_a = [remote(pair_a, device(ring, s), row_sems, (k,)) for k, s in enumerate(row_spots)]
    for copy in rows_a:
        copy.start()
    for t in range(rings // 2):
        last = t == rings // 2 - 1
        cw_spots = pl.ds(base, 1 if last else pair)
        ccw_spots = pl.ds(base + 1 if last else base, 1 if last else pair)
        cw = out_ref.at[(ring - t + rings) % rings, cw_spots, :, :, second_lanes]
        ccw = out_ref.at[(ring + t) % rings, ccw_spots, :, :, second_lanes]
        step = [
            remote(cw, device(ahead, spot), lane_sems, (0, t)),
            remote(ccw, device(behind, spot), lane_sems, (1, t)),
        ]
        for copy in step:
            copy.start()
        finish(step)
    finish(rows_a)

    half = slab // 2
    mid = rings // 2
    cross = [
        remote(out_ref.at[:, pl.ds(base, pair), :, :, second_lanes], device(ring, right), cross_sems, (0, 0)),
        remote(out_ref.at[:, pl.ds(base, pair), :, :, second_lanes], device(ring, left), cross_sems, (1, 0)),
    ]
    for copy in cross:
        copy.start()
    onward = None
    for t in range(rings // 2):
        last = t == rings // 2 - 1
        cw_spots = pl.ds(0, half if last else slab)
        ccw_spots = pl.ds(half if last else 0, half if last else slab)
        cw = out_ref.at[(ring - t + rings) % rings, cw_spots, :, :, first_lanes]
        ccw = out_ref.at[(ring + t) % rings, ccw_spots, :, :, first_lanes]
        step = [
            remote(cw, device(ahead, spot), ring_sems, (0, t)),
            remote(ccw, device(behind, spot), ring_sems, (1, t)),
        ]
        for copy in step:
            copy.start()
        finish(step)
        if t == 1:
            finish(cross)
            from_left = ((across + row - 1) % row) * pair
            from_right = ((across + 1) % row) * pair
            onward = [
                remote(
                    out_ref.at[pl.ds(0, mid), pl.ds(from_left, pair), :, :, second_lanes],
                    device(ring, right),
                    cross_sems,
                    (0, 1),
                ),
                remote(
                    out_ref.at[pl.ds(mid, mid), pl.ds(from_right, pair), :, :, second_lanes],
                    device(ring, left),
                    cross_sems,
                    (1, 1),
                ),
            ]
            for copy in onward:
                copy.start()
    finish(onward)


def gather_seq(block, rings, slab):
    return pl.pallas_call(
        gather_kernel,
        out_shape=jax.ShapeDtypeStruct((rings, slab) + block.shape, block.dtype),
        in_specs=[pl.BlockSpec(memory_space=pl.ANY)],
        out_specs=pl.BlockSpec(memory_space=pl.ANY),
        scratch_shapes=[
            pltpu.SemaphoreType.DMA((2,)),
            pltpu.SemaphoreType.DMA((2, slab // 2 - 1)),
            pltpu.SemaphoreType.DMA((2, 2, rings // 2)),
            pltpu.SemaphoreType.DMA((2, 2, rings // 2)),
            pltpu.SemaphoreType.DMA((2, 2, 2)),
            pltpu.SemaphoreType.DMA(()),
        ],
        compiler_params=pltpu.CompilerParams(collective_id=0, has_side_effects=True),
    )(block)


def scatter_kernel(terms_ref, out_ref, mine, incoming, sums, send_sem, recv_sem, local_sems):
    chips = out_ref.shape[0]
    seq = lax.axis_index("seq")
    tp = lax.axis_index("tp")
    mesh_id = pl.DeviceIdType.MESH
    core = tp % 2
    here = tp // 2
    owners = [(here + k) % chips for k in range(1, chips)]
    targets = [(seq, tp + 1 - 2 * core)] + [(seq, owner * 2 + core) for owner in owners]

    barrier = pltpu.get_barrier_semaphore()
    for target in targets:
        pl.semaphore_signal(barrier, inc=1, device_id=target, device_id_type=mesh_id)
    pl.semaphore_wait(barrier, len(targets))

    keep = pltpu.make_async_copy(terms_ref.at[core], mine, local_sems.at[0])
    keep.start()
    swap = pltpu.make_async_remote_copy(
        src_ref=terms_ref.at[1 - core],
        dst_ref=incoming,
        send_sem=send_sem.at[0],
        recv_sem=recv_sem.at[0],
        device_id=targets[0],
        device_id_type=mesh_id,
    )
    swap.start()
    keep.wait()
    swap.wait_send()
    swap.wait_recv()
    total = mine[...].astype(jnp.float32) + incoming[...].astype(jnp.float32)
    sums[...] = total.astype(sums.dtype)

    local = pltpu.make_async_copy(sums.at[here], out_ref.at[here], local_sems.at[1])
    local.start()
    copies = []
    for k, owner in enumerate(owners):
        copy = pltpu.make_async_remote_copy(
            src_ref=sums.at[owner],
            dst_ref=out_ref.at[here],
            send_sem=send_sem.at[k + 1],
            recv_sem=recv_sem.at[k + 1],
            device_id=targets[k + 1],
            device_id_type=mesh_id,
        )
        copy.start()
        copies.append(copy)
    for copy in copies:
        copy.wait_send()
        copy.wait_recv()
    local.wait()


def scatter_chips(terms):
    block = terms.shape[1:]
    chips = block[0]
    return pl.pallas_call(
        scatter_kernel,
        out_shape=jax.ShapeDtypeStruct(block, jnp.bfloat16),
        in_specs=[pl.BlockSpec(memory_space=pl.ANY)],
        out_specs=pl.BlockSpec(memory_space=pl.ANY),
        scratch_shapes=[
            pltpu.VMEM(block, terms.dtype),
            pltpu.VMEM(block, terms.dtype),
            pltpu.VMEM(block, jnp.bfloat16),
            pltpu.SemaphoreType.DMA((chips,)),
            pltpu.SemaphoreType.DMA((chips,)),
            pltpu.SemaphoreType.DMA((2,)),
        ],
        compiler_params=pltpu.CompilerParams(collective_id=1, has_side_effects=True),
    )(terms)


def exchange_kernel(axis, offsets, x_ref, out_ref, send_sem, recv_sem, local_sem):
    size = lax.axis_size(axis)
    me = lax.axis_index(axis)
    seq = lax.axis_index("seq")
    tp = lax.axis_index("tp")
    mesh_id = pl.DeviceIdType.MESH

    def device(position):
        return (position, tp) if axis == "seq" else (seq, position)

    def slot(entry):
        return me if entry is None else entry

    peers = [lax.rem(me + offset + size, size) for offset, _ in offsets]
    barrier = pltpu.get_barrier_semaphore()
    for peer in peers:
        pl.semaphore_signal(barrier, inc=1, device_id=device(peer), device_id_type=mesh_id)
    pl.semaphore_wait(barrier, len(peers))

    own = offsets_own_slot(offsets, me)
    local = pltpu.make_async_copy(x_ref, out_ref.at[own], local_sem)
    local.start()
    copies = []
    for k, ((_, entry), peer) in enumerate(zip(offsets, peers)):
        copy = pltpu.make_async_remote_copy(
            src_ref=x_ref,
            dst_ref=out_ref.at[slot(entry)],
            send_sem=send_sem.at[k],
            recv_sem=recv_sem.at[k],
            device_id=device(peer),
            device_id_type=mesh_id,
        )
        copy.start()
        copies.append(copy)
    for copy in copies:
        copy.wait_send()
        copy.wait_recv()
    local.wait()


def offsets_own_slot(offsets, me):
    slots = [entry for _, entry in offsets]
    if None in slots:
        return me
    return len(offsets) // 2


def exchange(block, axis, offsets, slots, collective_id):
    count = len(offsets)
    return pl.pallas_call(
        functools.partial(exchange_kernel, axis, offsets),
        out_shape=jax.ShapeDtypeStruct((slots,) + block.shape, block.dtype),
        in_specs=[pl.BlockSpec(memory_space=pl.ANY)],
        out_specs=pl.BlockSpec(memory_space=pl.ANY),
        scratch_shapes=[
            pltpu.SemaphoreType.DMA((count,)),
            pltpu.SemaphoreType.DMA((count,)),
            pltpu.SemaphoreType.DMA(()),
        ],
        compiler_params=pltpu.CompilerParams(
            collective_id=collective_id, has_side_effects=True
        ),
    )(block)


def masked_scores(query, keys, query_seg, key_seg):
    scores = jnp.einsum(
        "qhd,khd->hqk", query, keys, preferred_element_type=jnp.float32
    ) * HEAD_DIM ** (-0.5)
    mask = (query_seg[:, None] == key_seg[None, :])[None]
    return (jnp.where(mask, scores, floor_score), mask)


def shards(tokens, norm_gain, qkv_weight, q_gain, k_gain, out_weight, layer_scale, segment_ids):
    count = tokens.shape[0]
    source = tokens.astype(jnp.float32)
    normed = (
        source * lax.rsqrt(jnp.mean(source * source, axis=-1, keepdims=True) + eps) * norm_gain
    ).astype(jnp.bfloat16)
    local_width = qkv_weight.shape[2]
    heads = local_width // HEAD_DIM
    stacked = jnp.concatenate([qkv_weight, jnp.transpose(out_weight)[:, None, :]], axis=1)
    rows, kinds, width = stacked.shape
    slab = 8
    gathered = gather_seq(stacked, lax.axis_size("seq") // slab, slab).reshape(-1, kinds, width)
    joined = jnp.einsum(
        "td,dch->tch",
        normed,
        gathered[:, :3],
        preferred_element_type=jnp.float32,
    )
    query = joined[:, 0]
    keys = joined[:, 1]
    values = joined[:, 2]
    parts = lax.axis_size("tp")
    squares = jnp.stack([jnp.sum(query * query, axis=-1), jnp.sum(keys * keys, axis=-1)])
    everyone = [(k, None) for k in range(1, parts)]
    query_sq, key_sq = jnp.sum(exchange(squares, "tp", everyone, parts, 2), axis=0)
    full_width = local_width * lax.axis_size("tp")
    query_normed = (query * lax.rsqrt(query_sq / full_width + eps)[:, None] * q_gain).astype(
        jnp.bfloat16
    )
    key_normed = (keys * lax.rsqrt(key_sq / full_width + eps)[:, None] * k_gain).astype(
        jnp.bfloat16
    )
    paired = jnp.stack([key_normed, values.astype(jnp.bfloat16)], axis=1)
    pieces = []
    for offset in (2, 1, 0, -1, -2):
        if offset == 0:
            pieces.append(paired)
        else:
            pieces.append(passed_along(paired, "seq", offset))
    widened = jnp.concatenate(pieces, axis=0)
    position = lax.axis_index("seq")
    outside = jnp.full((2 * count,), -1, jnp.int32)
    seg_pad = jnp.concatenate([outside, segment_ids, outside], axis=0)
    key_seg = lax.dynamic_slice_in_dim(seg_pad, position * count, 5 * count, 0)
    query_seg = lax.dynamic_slice_in_dim(segment_ids, position * count, count, 0)
    query_heads = query_normed.reshape(count, heads, HEAD_DIM)
    key_heads = widened[:, 0].reshape(5 * count, heads, HEAD_DIM)
    value_heads = widened[:, 1].reshape(5 * count, heads, HEAD_DIM)
    scores, mask = masked_scores(query_heads, key_heads, query_seg, key_seg)
    peak = jnp.max(scores, axis=-1, keepdims=True)
    weights = jnp.where(mask, jnp.exp(scores - peak), 0.0)
    total = jnp.sum(weights, axis=-1)
    probs = weights.astype(jnp.bfloat16)
    summed = jnp.einsum("hqk,khd->qhd", probs, value_heads, preferred_element_type=jnp.float32)
    context = (
        (summed / jnp.transpose(total)[:, :, None]).reshape(count, local_width).astype(jnp.bfloat16)
    )
    blank = jnp.zeros_like(context)
    widened_context = jnp.stack([blank, blank, blank, context], axis=1)
    chips = parts // 2
    by_owner = gathered.reshape(chips, 2, -1, *gathered.shape[1:])
    terms = jnp.einsum(
        "tkh,ycdkh->cydt", widened_context, by_owner, preferred_element_type=jnp.float32
    )
    projected = jnp.transpose(
        jnp.sum(scatter_chips(terms.astype(jnp.bfloat16)).astype(jnp.float32), axis=0)
    )
    share = layer_scale.shape[0]
    residual = lax.dynamic_slice_in_dim(source, lax.axis_index("tp") * share, share, 1)
    return (residual + layer_scale * projected).astype(jnp.bfloat16)


def solution(mesh):
    return jax.shard_map(
        shards,
        mesh=mesh,
        in_specs=(
            P("seq", None),
            P(),
            P("seq", None, "tp"),
            P("tp"),
            P("tp"),
            P("tp", "seq"),
            P("tp"),
            P(),
        ),
        out_specs=P("seq", "tp"),
        check_vma=False,
    )
```

```python
import functools

import jax
import jax.numpy as jnp
from jax import lax
from jax.sharding import PartitionSpec as P
from jax.experimental import pallas as pl
from jax.experimental.pallas import tpu as pltpu

HEAD_DIM = 128


eps = 1e-06
floor_score = -1e30


def passed_along(x, axis, by):
    size = lax.axis_size(axis)
    pairs = [(i, i + by) for i in range(size) if 0 <= i + by < size]
    return lax.ppermute(x, axis, pairs)


def gather_kernel(x_ref, out_ref, pair_sems, row_sems, lane_sems, ring_sems, cross_sems, local_sem):
    rings, slab = out_ref.shape[0], out_ref.shape[1]
    pair = 2
    row = slab // pair
    lanes = out_ref.shape[-1] // 2
    first_lanes, second_lanes = pl.ds(0, lanes), pl.ds(lanes, lanes)
    me = lax.axis_index("seq")
    tp = lax.axis_index("tp")
    mesh_id = pl.DeviceIdType.MESH
    ring = me // slab
    spot = me % slab
    low = spot % pair
    across = spot // pair
    base = spot - low

    def device(r, s):
        return (r * slab + s, tp)

    ahead = (ring + 1) % rings
    behind = (ring + rings - 1) % rings
    partner = base + 1 - low
    row_spots = [((across + k) % row) * pair + low for k in range(1, row)]
    right = ((across + 1) % row) * pair + low
    left = ((across + row - 1) % row) * pair + low

    barrier = pltpu.get_barrier_semaphore()
    targets = [device(ring, partner), device(ahead, spot), device(behind, spot)]
    targets += [device(ring, s) for s in row_spots]
    for target in targets:
        pl.semaphore_signal(barrier, inc=1, device_id=target, device_id_type=mesh_id)
    pl.semaphore_wait(barrier, len(targets))

    def remote(window, target, sems, index):
        return pltpu.make_async_remote_copy(
            src_ref=window,
            dst_ref=window,
            send_sem=sems.at[(0,) + index],
            recv_sem=sems.at[(1,) + index],
            device_id=target,
            device_id_type=mesh_id,
        )

    def finish(copies):
        for copy in copies:
            copy.wait_send()
            copy.wait_recv()

    local = pltpu.make_async_copy(x_ref, out_ref.at[ring, spot], local_sem)
    local.start()
    swap = pltpu.make_async_remote_copy(
        src_ref=x_ref,
        dst_ref=out_ref.at[ring, spot],
        send_sem=pair_sems.at[0],
        recv_sem=pair_sems.at[1],
        device_id=device(ring, partner),
        device_id_type=mesh_id,
    )
    swap.start()
    local.wait()
    finish([swap])

    pair_a = out_ref.at[ring, pl.ds(base, pair), :, :, first_lanes]
    rows_a = [remote(pair_a, device(ring, s), row_sems, (k,)) for k, s in enumerate(row_spots)]
    for copy in rows_a:
        copy.start()
    for t in range(rings // 2):
        last = t == rings // 2 - 1
        cw_spots = pl.ds(base, 1 if last else pair)
        ccw_spots = pl.ds(base + 1 if last else base, 1 if last else pair)
        cw = out_ref.at[(ring - t + rings) % rings, cw_spots, :, :, second_lanes]
        ccw = out_ref.at[(ring + t) % rings, ccw_spots, :, :, second_lanes]
        step = [
            remote(cw, device(ahead, spot), lane_sems, (0, t)),
            remote(ccw, device(behind, spot), lane_sems, (1, t)),
        ]
        for copy in step:
            copy.start()
        finish(step)
    finish(rows_a)

    half = slab // 2
    mid = rings // 2
    cross = [
        remote(out_ref.at[:, pl.ds(base, pair), :, :, second_lanes], device(ring, right), cross_sems, (0, 0)),
        remote(out_ref.at[:, pl.ds(base, pair), :, :, second_lanes], device(ring, left), cross_sems, (1, 0)),
    ]
    for copy in cross:
        copy.start()
    onward = None
    for t in range(rings // 2):
        last = t == rings // 2 - 1
        cw_spots = pl.ds(0, half if last else slab)
        ccw_spots = pl.ds(half if last else 0, half if last else slab)
        cw = out_ref.at[(ring - t + rings) % rings, cw_spots, :, :, first_lanes]
        ccw = out_ref.at[(ring + t) % rings, ccw_spots, :, :, first_lanes]
        step = [
            remote(cw, device(ahead, spot), ring_sems, (0, t)),
            remote(ccw, device(behind, spot), ring_sems, (1, t)),
        ]
        for copy in step:
            copy.start()
        finish(step)
        if t == 1:
            finish(cross)
            from_left = ((across + row - 1) % row) * pair
            from_right = ((across + 1) % row) * pair
            onward = [
                remote(
                    out_ref.at[pl.ds(0, mid), pl.ds(from_left, pair), :, :, second_lanes],
                    device(ring, right),
                    cross_sems,
                    (0, 1),
                ),
                remote(
                    out_ref.at[pl.ds(mid, mid), pl.ds(from_right, pair), :, :, second_lanes],
                    device(ring, left),
                    cross_sems,
                    (1, 1),
                ),
            ]
            for copy in onward:
                copy.start()
    finish(onward)


def gather_seq(block, rings, slab):
    return pl.pallas_call(
        gather_kernel,
        out_shape=jax.ShapeDtypeStruct((rings, slab) + block.shape, block.dtype),
        in_specs=[pl.BlockSpec(memory_space=pl.ANY)],
        out_specs=pl.BlockSpec(memory_space=pl.ANY),
        scratch_shapes=[
            pltpu.SemaphoreType.DMA((2,)),
            pltpu.SemaphoreType.DMA((2, slab // 2 - 1)),
            pltpu.SemaphoreType.DMA((2, 2, rings // 2)),
            pltpu.SemaphoreType.DMA((2, 2, rings // 2)),
            pltpu.SemaphoreType.DMA((2, 2, 2)),
            pltpu.SemaphoreType.DMA(()),
        ],
        compiler_params=pltpu.CompilerParams(collective_id=0, has_side_effects=True),
    )(block)


def scatter_kernel(terms_ref, out_ref, mine, incoming, sums, send_sem, recv_sem, local_sems):
    chips = out_ref.shape[0]
    seq = lax.axis_index("seq")
    tp = lax.axis_index("tp")
    mesh_id = pl.DeviceIdType.MESH
    core = tp % 2
    here = tp // 2
    partner = (seq, tp + 1 - 2 * core)
    order = [(here + k) % chips for k in (2, 1, 3, 0)]

    def device(chip):
        return (seq, chip * 2 + core)

    barrier = pltpu.get_barrier_semaphore()
    for target in [partner] + [device(owner) for owner in order[:3]]:
        pl.semaphore_signal(barrier, inc=1, device_id=target, device_id_type=mesh_id)
    pl.semaphore_wait(barrier, 4)

    arrivals = []
    for k, owner in enumerate(order):
        keep = pltpu.make_async_copy(terms_ref.at[core, owner], mine.at[owner], local_sems.at[k])
        swap = pltpu.make_async_remote_copy(
            src_ref=terms_ref.at[1 - core, owner],
            dst_ref=incoming.at[owner],
            send_sem=send_sem.at[k],
            recv_sem=recv_sem.at[k],
            device_id=partner,
            device_id_type=mesh_id,
        )
        keep.start()
        swap.start()
        arrivals.append((keep, swap))

    outgoing = []
    for k, owner in enumerate(order):
        keep, swap = arrivals[k]
        keep.wait()
        swap.wait_send()
        swap.wait_recv()
        total = mine[owner].astype(jnp.float32) + incoming[owner].astype(jnp.float32)
        sums[owner] = total.astype(sums.dtype)
        if k < 3:
            copy = pltpu.make_async_remote_copy(
                src_ref=sums.at[owner],
                dst_ref=out_ref.at[here],
                send_sem=send_sem.at[4 + k],
                recv_sem=recv_sem.at[4 + k],
                device_id=device(owner),
                device_id_type=mesh_id,
            )
        else:
            copy = pltpu.make_async_copy(sums.at[owner], out_ref.at[here], local_sems.at[4])
        copy.start()
        outgoing.append(copy)
    for copy in outgoing[:3]:
        copy.wait_send()
        copy.wait_recv()
    outgoing[3].wait()


def scatter_chips(terms):
    block = terms.shape[1:]
    chips = block[0]
    return pl.pallas_call(
        scatter_kernel,
        out_shape=jax.ShapeDtypeStruct(block, jnp.bfloat16),
        in_specs=[pl.BlockSpec(memory_space=pl.ANY)],
        out_specs=pl.BlockSpec(memory_space=pl.ANY),
        scratch_shapes=[
            pltpu.VMEM(block, terms.dtype),
            pltpu.VMEM(block, terms.dtype),
            pltpu.VMEM(block, jnp.bfloat16),
            pltpu.SemaphoreType.DMA((7,)),
            pltpu.SemaphoreType.DMA((7,)),
            pltpu.SemaphoreType.DMA((5,)),
        ],
        compiler_params=pltpu.CompilerParams(collective_id=1, has_side_effects=True),
    )(terms)


def exchange_kernel(axis, offsets, x_ref, out_ref, send_sem, recv_sem, local_sem):
    size = lax.axis_size(axis)
    me = lax.axis_index(axis)
    seq = lax.axis_index("seq")
    tp = lax.axis_index("tp")
    mesh_id = pl.DeviceIdType.MESH

    def device(position):
        return (position, tp) if axis == "seq" else (seq, position)

    def slot(entry):
        return me if entry is None else entry

    peers = [lax.rem(me + offset + size, size) for offset, _ in offsets]
    barrier = pltpu.get_barrier_semaphore()
    for peer in peers:
        pl.semaphore_signal(barrier, inc=1, device_id=device(peer), device_id_type=mesh_id)
    pl.semaphore_wait(barrier, len(peers))

    own = offsets_own_slot(offsets, me)
    local = pltpu.make_async_copy(x_ref, out_ref.at[own], local_sem)
    local.start()
    copies = []
    for k, ((_, entry), peer) in enumerate(zip(offsets, peers)):
        copy = pltpu.make_async_remote_copy(
            src_ref=x_ref,
            dst_ref=out_ref.at[slot(entry)],
            send_sem=send_sem.at[k],
            recv_sem=recv_sem.at[k],
            device_id=device(peer),
            device_id_type=mesh_id,
        )
        copy.start()
        copies.append(copy)
    for copy in copies:
        copy.wait_send()
        copy.wait_recv()
    local.wait()


def offsets_own_slot(offsets, me):
    slots = [entry for _, entry in offsets]
    if None in slots:
        return me
    return len(offsets) // 2


def exchange(block, axis, offsets, slots, collective_id):
    count = len(offsets)
    return pl.pallas_call(
        functools.partial(exchange_kernel, axis, offsets),
        out_shape=jax.ShapeDtypeStruct((slots,) + block.shape, block.dtype),
        in_specs=[pl.BlockSpec(memory_space=pl.ANY)],
        out_specs=pl.BlockSpec(memory_space=pl.ANY),
        scratch_shapes=[
            pltpu.SemaphoreType.DMA((count,)),
            pltpu.SemaphoreType.DMA((count,)),
            pltpu.SemaphoreType.DMA(()),
        ],
        compiler_params=pltpu.CompilerParams(
            collective_id=collective_id, has_side_effects=True
        ),
    )(block)


def masked_scores(query, keys, query_seg, key_seg):
    scores = jnp.einsum(
        "qhd,khd->hqk", query, keys, preferred_element_type=jnp.float32
    ) * HEAD_DIM ** (-0.5)
    mask = (query_seg[:, None] == key_seg[None, :])[None]
    return (jnp.where(mask, scores, floor_score), mask)


def shards(tokens, norm_gain, qkv_weight, q_gain, k_gain, out_weight, layer_scale, segment_ids):
    count = tokens.shape[0]
    source = tokens.astype(jnp.float32)
    normed = (
        source * lax.rsqrt(jnp.mean(source * source, axis=-1, keepdims=True) + eps) * norm_gain
    ).astype(jnp.bfloat16)
    local_width = qkv_weight.shape[2]
    heads = local_width // HEAD_DIM
    stacked = jnp.concatenate([qkv_weight, jnp.transpose(out_weight)[:, None, :]], axis=1)
    rows, kinds, width = stacked.shape
    slab = 8
    gathered = gather_seq(stacked, lax.axis_size("seq") // slab, slab).reshape(-1, kinds, width)
    joined = jnp.einsum(
        "td,dch->tch",
        normed,
        gathered[:, :3],
        preferred_element_type=jnp.float32,
    )
    query = joined[:, 0]
    keys = joined[:, 1]
    values = joined[:, 2]
    parts = lax.axis_size("tp")
    squares = jnp.stack([jnp.sum(query * query, axis=-1), jnp.sum(keys * keys, axis=-1)])
    everyone = [(k, None) for k in range(1, parts)]
    query_sq, key_sq = jnp.sum(exchange(squares, "tp", everyone, parts, 2), axis=0)
    full_width = local_width * lax.axis_size("tp")
    query_normed = (query * lax.rsqrt(query_sq / full_width + eps)[:, None] * q_gain).astype(
        jnp.bfloat16
    )
    key_normed = (keys * lax.rsqrt(key_sq / full_width + eps)[:, None] * k_gain).astype(
        jnp.bfloat16
    )
    paired = jnp.stack([key_normed, values.astype(jnp.bfloat16)], axis=1)
    pieces = []
    for offset in (2, 1, 0, -1, -2):
        if offset == 0:
            pieces.append(paired)
        else:
            pieces.append(passed_along(paired, "seq", offset))
    widened = jnp.concatenate(pieces, axis=0)
    position = lax.axis_index("seq")
    outside = jnp.full((2 * count,), -1, jnp.int32)
    seg_pad = jnp.concatenate([outside, segment_ids, outside], axis=0)
    key_seg = lax.dynamic_slice_in_dim(seg_pad, position * count, 5 * count, 0)
    query_seg = lax.dynamic_slice_in_dim(segment_ids, position * count, count, 0)
    query_heads = query_normed.reshape(count, heads, HEAD_DIM)
    key_heads = widened[:, 0].reshape(5 * count, heads, HEAD_DIM)
    value_heads = widened[:, 1].reshape(5 * count, heads, HEAD_DIM)
    scores, mask = masked_scores(query_heads, key_heads, query_seg, key_seg)
    peak = jnp.max(scores, axis=-1, keepdims=True)
    weights = jnp.where(mask, jnp.exp(scores - peak), 0.0)
    total = jnp.sum(weights, axis=-1)
    probs = weights.astype(jnp.bfloat16)
    summed = jnp.einsum("hqk,khd->qhd", probs, value_heads, preferred_element_type=jnp.float32)
    context = (
        (summed / jnp.transpose(total)[:, :, None]).reshape(count, local_width).astype(jnp.bfloat16)
    )
    blank = jnp.zeros_like(context)
    widened_context = jnp.stack([blank, blank, blank, context], axis=1)
    chips = parts // 2
    by_owner = gathered.reshape(chips, 2, -1, *gathered.shape[1:])
    terms = jnp.einsum(
        "tkh,ycdkh->cydt", widened_context, by_owner, preferred_element_type=jnp.float32
    )
    projected = jnp.transpose(
        jnp.sum(scatter_chips(terms.astype(jnp.bfloat16)).astype(jnp.float32), axis=0)
    )
    share = layer_scale.shape[0]
    residual = lax.dynamic_slice_in_dim(source, lax.axis_index("tp") * share, share, 1)
    return (residual + layer_scale * projected).astype(jnp.bfloat16)


def solution(mesh):
    return jax.shard_map(
        shards,
        mesh=mesh,
        in_specs=(
            P("seq", None),
            P(),
            P("seq", None, "tp"),
            P("tp"),
            P("tp"),
            P("tp", "seq"),
            P("tp"),
            P(),
        ),
        out_specs=P("seq", "tp"),
        check_vma=False,
    )
```

```python
import functools

import jax
import jax.numpy as jnp
from jax import lax
from jax.sharding import PartitionSpec as P
from jax.experimental import pallas as pl
from jax.experimental.pallas import tpu as pltpu

HEAD_DIM = 128


eps = 1e-06
floor_score = -1e30


def passed_along(x, axis, by):
    size = lax.axis_size(axis)
    pairs = [(i, i + by) for i in range(size) if 0 <= i + by < size]
    return lax.ppermute(x, axis, pairs)


def gather_kernel(
    x_ref, tokens_ref, gain_ref, out_ref, normed_ref,
    pair_sems, row_sems, lane_sems, ring_sems, cross_sems, local_sem,
):
    rings, slab = out_ref.shape[0], out_ref.shape[1]
    pair = 2
    row = slab // pair
    lanes = out_ref.shape[-1] // 2
    first_lanes, second_lanes = pl.ds(0, lanes), pl.ds(lanes, lanes)
    me = lax.axis_index("seq")
    tp = lax.axis_index("tp")
    mesh_id = pl.DeviceIdType.MESH
    ring = me // slab
    spot = me % slab
    low = spot % pair
    across = spot // pair
    base = spot - low

    def device(r, s):
        return (r * slab + s, tp)

    ahead = (ring + 1) % rings
    behind = (ring + rings - 1) % rings
    partner = base + 1 - low
    row_spots = [((across + k) % row) * pair + low for k in range(1, row)]
    right = ((across + 1) % row) * pair + low
    left = ((across + row - 1) % row) * pair + low

    barrier = pltpu.get_barrier_semaphore()
    targets = [device(ring, partner), device(ahead, spot), device(behind, spot)]
    targets += [device(ring, s) for s in row_spots]
    for target in targets:
        pl.semaphore_signal(barrier, inc=1, device_id=target, device_id_type=mesh_id)
    pl.semaphore_wait(barrier, len(targets))

    def remote(window, target, sems, index):
        return pltpu.make_async_remote_copy(
            src_ref=window,
            dst_ref=window,
            send_sem=sems.at[(0,) + index],
            recv_sem=sems.at[(1,) + index],
            device_id=target,
            device_id_type=mesh_id,
        )

    def finish(copies):
        for copy in copies:
            copy.wait_send()
            copy.wait_recv()

    local = pltpu.make_async_copy(x_ref, out_ref.at[ring, spot], local_sem)
    local.start()
    swap = pltpu.make_async_remote_copy(
        src_ref=x_ref,
        dst_ref=out_ref.at[ring, spot],
        send_sem=pair_sems.at[0],
        recv_sem=pair_sems.at[1],
        device_id=device(ring, partner),
        device_id_type=mesh_id,
    )
    swap.start()
    local.wait()
    finish([swap])

    pair_a = out_ref.at[ring, pl.ds(base, pair), :, :, first_lanes]
    rows_a = [remote(pair_a, device(ring, s), row_sems, (k,)) for k, s in enumerate(row_spots)]
    for copy in rows_a:
        copy.start()
    for t in range(rings // 2):
        last = t == rings // 2 - 1
        cw_spots = pl.ds(base, 1 if last else pair)
        ccw_spots = pl.ds(base + 1 if last else base, 1 if last else pair)
        cw = out_ref.at[(ring - t + rings) % rings, cw_spots, :, :, second_lanes]
        ccw = out_ref.at[(ring + t) % rings, ccw_spots, :, :, second_lanes]
        step = [
            remote(cw, device(ahead, spot), lane_sems, (0, t)),
            remote(ccw, device(behind, spot), lane_sems, (1, t)),
        ]
        for copy in step:
            copy.start()
        finish(step)
    finish(rows_a)

    half = slab // 2
    mid = rings // 2
    cross = [
        remote(out_ref.at[:, pl.ds(base, pair), :, :, second_lanes], device(ring, right), cross_sems, (0, 0)),
        remote(out_ref.at[:, pl.ds(base, pair), :, :, second_lanes], device(ring, left), cross_sems, (1, 0)),
    ]
    for copy in cross:
        copy.start()
    source = tokens_ref[...].astype(jnp.float32)
    power = jnp.mean(source * source, axis=-1, keepdims=True)
    scaled = source * lax.rsqrt(power + eps) * gain_ref[...]
    normed_ref[...] = jnp.transpose(scaled.astype(jnp.bfloat16).astype(jnp.float32)).astype(
        normed_ref.dtype
    )
    onward = None
    for t in range(rings // 2):
        last = t == rings // 2 - 1
        cw_spots = pl.ds(0, half if last else slab)
        ccw_spots = pl.ds(half if last else 0, half if last else slab)
        cw = out_ref.at[(ring - t + rings) % rings, cw_spots, :, :, first_lanes]
        ccw = out_ref.at[(ring + t) % rings, ccw_spots, :, :, first_lanes]
        step = [
            remote(cw, device(ahead, spot), ring_sems, (0, t)),
            remote(ccw, device(behind, spot), ring_sems, (1, t)),
        ]
        for copy in step:
            copy.start()
        finish(step)
        if t == 1:
            finish(cross)
            from_left = ((across + row - 1) % row) * pair
            from_right = ((across + 1) % row) * pair
            onward = [
                remote(
                    out_ref.at[pl.ds(0, mid), pl.ds(from_left, pair), :, :, second_lanes],
                    device(ring, right),
                    cross_sems,
                    (0, 1),
                ),
                remote(
                    out_ref.at[pl.ds(mid, mid), pl.ds(from_right, pair), :, :, second_lanes],
                    device(ring, left),
                    cross_sems,
                    (1, 1),
                ),
            ]
            for copy in onward:
                copy.start()
    finish(onward)


def gather_seq(block, tokens, gain, rings, slab):
    return pl.pallas_call(
        gather_kernel,
        out_shape=(
            jax.ShapeDtypeStruct((rings, slab) + block.shape, block.dtype),
            jax.ShapeDtypeStruct(tokens.shape[::-1], jnp.bfloat16),
        ),
        in_specs=[
            pl.BlockSpec(memory_space=pl.ANY),
            pl.BlockSpec(memory_space=pltpu.VMEM),
            pl.BlockSpec(memory_space=pltpu.VMEM),
        ],
        out_specs=(
            pl.BlockSpec(memory_space=pl.ANY),
            pl.BlockSpec(memory_space=pltpu.VMEM),
        ),
        scratch_shapes=[
            pltpu.SemaphoreType.DMA((2,)),
            pltpu.SemaphoreType.DMA((2, slab // 2 - 1)),
            pltpu.SemaphoreType.DMA((2, 2, rings // 2)),
            pltpu.SemaphoreType.DMA((2, 2, rings // 2)),
            pltpu.SemaphoreType.DMA((2, 2, 2)),
            pltpu.SemaphoreType.DMA(()),
        ],
        compiler_params=pltpu.CompilerParams(collective_id=0, has_side_effects=True),
    )(block, tokens, gain.reshape(1, -1))


def scatter_kernel(terms_ref, out_ref, mine, incoming, sums, send_sem, recv_sem, local_sems):
    chips = out_ref.shape[0]
    seq = lax.axis_index("seq")
    tp = lax.axis_index("tp")
    mesh_id = pl.DeviceIdType.MESH
    core = tp % 2
    here = tp // 2
    partner = (seq, tp + 1 - 2 * core)
    order = [(here + k) % chips for k in (2, 1, 3, 0)]

    def device(chip):
        return (seq, chip * 2 + core)

    barrier = pltpu.get_barrier_semaphore()
    for target in [partner] + [device(owner) for owner in order[:3]]:
        pl.semaphore_signal(barrier, inc=1, device_id=target, device_id_type=mesh_id)
    pl.semaphore_wait(barrier, 4)

    arrivals = []
    for k, owner in enumerate(order):
        keep = pltpu.make_async_copy(terms_ref.at[core, owner], mine.at[owner], local_sems.at[k])
        swap = pltpu.make_async_remote_copy(
            src_ref=terms_ref.at[1 - core, owner],
            dst_ref=incoming.at[owner],
            send_sem=send_sem.at[k],
            recv_sem=recv_sem.at[k],
            device_id=partner,
            device_id_type=mesh_id,
        )
        keep.start()
        swap.start()
        arrivals.append((keep, swap))

    outgoing = []
    for k, owner in enumerate(order):
        keep, swap = arrivals[k]
        keep.wait()
        swap.wait_send()
        swap.wait_recv()
        total = mine[owner].astype(jnp.float32) + incoming[owner].astype(jnp.float32)
        sums[owner] = total.astype(sums.dtype)
        if k < 3:
            copy = pltpu.make_async_remote_copy(
                src_ref=sums.at[owner],
                dst_ref=out_ref.at[here],
                send_sem=send_sem.at[4 + k],
                recv_sem=recv_sem.at[4 + k],
                device_id=device(owner),
                device_id_type=mesh_id,
            )
        else:
            copy = pltpu.make_async_copy(sums.at[owner], out_ref.at[here], local_sems.at[4])
        copy.start()
        outgoing.append(copy)
    for copy in outgoing[:3]:
        copy.wait_send()
        copy.wait_recv()
    outgoing[3].wait()


def scatter_chips(terms):
    block = terms.shape[1:]
    chips = block[0]
    return pl.pallas_call(
        scatter_kernel,
        out_shape=jax.ShapeDtypeStruct(block, jnp.bfloat16),
        in_specs=[pl.BlockSpec(memory_space=pl.ANY)],
        out_specs=pl.BlockSpec(memory_space=pl.ANY),
        scratch_shapes=[
            pltpu.VMEM(block, terms.dtype),
            pltpu.VMEM(block, terms.dtype),
            pltpu.VMEM(block, jnp.bfloat16),
            pltpu.SemaphoreType.DMA((7,)),
            pltpu.SemaphoreType.DMA((7,)),
            pltpu.SemaphoreType.DMA((5,)),
        ],
        compiler_params=pltpu.CompilerParams(collective_id=1, has_side_effects=True),
    )(terms)


def exchange_kernel(axis, offsets, x_ref, out_ref, send_sem, recv_sem, local_sem):
    size = lax.axis_size(axis)
    me = lax.axis_index(axis)
    seq = lax.axis_index("seq")
    tp = lax.axis_index("tp")
    mesh_id = pl.DeviceIdType.MESH

    def device(position):
        return (position, tp) if axis == "seq" else (seq, position)

    def slot(entry):
        return me if entry is None else entry

    peers = [lax.rem(me + offset + size, size) for offset, _ in offsets]
    barrier = pltpu.get_barrier_semaphore()
    for peer in peers:
        pl.semaphore_signal(barrier, inc=1, device_id=device(peer), device_id_type=mesh_id)
    pl.semaphore_wait(barrier, len(peers))

    own = offsets_own_slot(offsets, me)
    local = pltpu.make_async_copy(x_ref, out_ref.at[own], local_sem)
    local.start()
    copies = []
    for k, ((_, entry), peer) in enumerate(zip(offsets, peers)):
        copy = pltpu.make_async_remote_copy(
            src_ref=x_ref,
            dst_ref=out_ref.at[slot(entry)],
            send_sem=send_sem.at[k],
            recv_sem=recv_sem.at[k],
            device_id=device(peer),
            device_id_type=mesh_id,
        )
        copy.start()
        copies.append(copy)
    for copy in copies:
        copy.wait_send()
        copy.wait_recv()
    local.wait()


def offsets_own_slot(offsets, me):
    slots = [entry for _, entry in offsets]
    if None in slots:
        return me
    return len(offsets) // 2


def exchange(block, axis, offsets, slots, collective_id):
    count = len(offsets)
    return pl.pallas_call(
        functools.partial(exchange_kernel, axis, offsets),
        out_shape=jax.ShapeDtypeStruct((slots,) + block.shape, block.dtype),
        in_specs=[pl.BlockSpec(memory_space=pl.ANY)],
        out_specs=pl.BlockSpec(memory_space=pl.ANY),
        scratch_shapes=[
            pltpu.SemaphoreType.DMA((count,)),
            pltpu.SemaphoreType.DMA((count,)),
            pltpu.SemaphoreType.DMA(()),
        ],
        compiler_params=pltpu.CompilerParams(
            collective_id=collective_id, has_side_effects=True
        ),
    )(block)


def masked_scores(query, keys, query_seg, key_seg):
    scores = jnp.einsum(
        "qhd,khd->hqk", query, keys, preferred_element_type=jnp.float32
    ) * HEAD_DIM ** (-0.5)
    mask = (query_seg[:, None] == key_seg[None, :])[None]
    return (jnp.where(mask, scores, floor_score), mask)


def shards(tokens, norm_gain, qkv_weight, q_gain, k_gain, out_weight, layer_scale, segment_ids):
    count = tokens.shape[0]
    source = tokens.astype(jnp.float32)
    local_width = qkv_weight.shape[2]
    heads = local_width // HEAD_DIM
    stacked = jnp.concatenate([qkv_weight, jnp.transpose(out_weight)[:, None, :]], axis=1)
    rows, kinds, width = stacked.shape
    slab = 8
    gathered, normed_t = gather_seq(
        stacked, tokens, norm_gain, lax.axis_size("seq") // slab, slab
    )
    gathered = gathered.reshape(-1, kinds, width)
    joined = jnp.einsum(
        "dt,dch->tch",
        normed_t,
        gathered[:, :3],
        preferred_element_type=jnp.float32,
    )
    query = joined[:, 0]
    keys = joined[:, 1]
    values = joined[:, 2]
    parts = lax.axis_size("tp")
    squares = jnp.stack([jnp.sum(query * query, axis=-1), jnp.sum(keys * keys, axis=-1)])
    everyone = [(k, None) for k in range(1, parts)]
    query_sq, key_sq = jnp.sum(exchange(squares, "tp", everyone, parts, 2), axis=0)
    full_width = local_width * lax.axis_size("tp")
    query_normed = (query * lax.rsqrt(query_sq / full_width + eps)[:, None] * q_gain).astype(
        jnp.bfloat16
    )
    key_normed = (keys * lax.rsqrt(key_sq / full_width + eps)[:, None] * k_gain).astype(
        jnp.bfloat16
    )
    paired = jnp.stack([key_normed, values.astype(jnp.bfloat16)], axis=1)
    pieces = []
    for offset in (2, 1, 0, -1, -2):
        if offset == 0:
            pieces.append(paired)
        else:
            pieces.append(passed_along(paired, "seq", offset))
    widened = jnp.concatenate(pieces, axis=0)
    position = lax.axis_index("seq")
    outside = jnp.full((2 * count,), -1, jnp.int32)
    seg_pad = jnp.concatenate([outside, segment_ids, outside], axis=0)
    key_seg = lax.dynamic_slice_in_dim(seg_pad, position * count, 5 * count, 0)
    query_seg = lax.dynamic_slice_in_dim(segment_ids, position * count, count, 0)
    query_heads = query_normed.reshape(count, heads, HEAD_DIM)
    key_heads = widened[:, 0].reshape(5 * count, heads, HEAD_DIM)
    value_heads = widened[:, 1].reshape(5 * count, heads, HEAD_DIM)
    scores, mask = masked_scores(query_heads, key_heads, query_seg, key_seg)
    peak = jnp.max(scores, axis=-1, keepdims=True)
    weights = jnp.where(mask, jnp.exp(scores - peak), 0.0)
    total = jnp.sum(weights, axis=-1)
    probs = weights.astype(jnp.bfloat16)
    summed = jnp.einsum("hqk,khd->qhd", probs, value_heads, preferred_element_type=jnp.float32)
    context = (
        (summed / jnp.transpose(total)[:, :, None]).reshape(count, local_width).astype(jnp.bfloat16)
    )
    blank = jnp.zeros_like(context)
    widened_context = jnp.stack([blank, blank, blank, context], axis=1)
    chips = parts // 2
    by_owner = gathered.reshape(chips, 2, -1, *gathered.shape[1:])
    terms = jnp.einsum(
        "tkh,ycdkh->cydt", widened_context, by_owner, preferred_element_type=jnp.float32
    )
    projected = jnp.transpose(
        jnp.sum(scatter_chips(terms.astype(jnp.bfloat16)).astype(jnp.float32), axis=0)
    )
    share = layer_scale.shape[0]
    residual = lax.dynamic_slice_in_dim(source, lax.axis_index("tp") * share, share, 1)
    return (residual + layer_scale * projected).astype(jnp.bfloat16)


def solution(mesh):
    return jax.shard_map(
        shards,
        mesh=mesh,
        in_specs=(
            P("seq", None),
            P(),
            P("seq", None, "tp"),
            P("tp"),
            P("tp"),
            P("tp", "seq"),
            P("tp"),
            P(),
        ),
        out_specs=P("seq", "tp"),
        check_vma=False,
    )
```

```python
import functools

import jax
import jax.numpy as jnp
from jax import lax
from jax.sharding import PartitionSpec as P
from jax.experimental import pallas as pl
from jax.experimental.pallas import tpu as pltpu

HEAD_DIM = 128


eps = 1e-06
floor_score = -1e30


def passed_along(x, axis, by):
    size = lax.axis_size(axis)
    pairs = [(i, i + by) for i in range(size) if 0 <= i + by < size]
    return lax.ppermute(x, axis, pairs)


def gather_kernel(
    x_ref, tokens_ref, gain_ref, out_ref, normed_ref,
    pair_sems, row_sems, lane_sems, ring_sems, cross_sems, local_sem,
):
    rings, slab = out_ref.shape[0], out_ref.shape[1]
    pair = 2
    row = slab // pair
    lanes = out_ref.shape[-1] // 2
    first_lanes, second_lanes = pl.ds(0, lanes), pl.ds(lanes, lanes)
    me = lax.axis_index("seq")
    tp = lax.axis_index("tp")
    mesh_id = pl.DeviceIdType.MESH
    ring = me // slab
    spot = me % slab
    low = spot % pair
    across = spot // pair
    base = spot - low

    def device(r, s):
        return (r * slab + s, tp)

    ahead = (ring + 1) % rings
    behind = (ring + rings - 1) % rings
    partner = base + 1 - low
    row_spots = [((across + k) % row) * pair + low for k in range(1, row)]
    right = ((across + 1) % row) * pair + low
    left = ((across + row - 1) % row) * pair + low

    barrier = pltpu.get_barrier_semaphore()
    targets = [device(ring, partner), device(ahead, spot), device(behind, spot)]
    targets += [device(ring, s) for s in row_spots]
    for target in targets:
        pl.semaphore_signal(barrier, inc=1, device_id=target, device_id_type=mesh_id)
    pl.semaphore_wait(barrier, len(targets))

    def remote(window, target, sems, index):
        return pltpu.make_async_remote_copy(
            src_ref=window,
            dst_ref=window,
            send_sem=sems.at[(0,) + index],
            recv_sem=sems.at[(1,) + index],
            device_id=target,
            device_id_type=mesh_id,
        )

    def finish(copies):
        for copy in copies:
            copy.wait_send()
            copy.wait_recv()

    local = pltpu.make_async_copy(x_ref, out_ref.at[ring, spot], local_sem)
    local.start()
    swap = pltpu.make_async_remote_copy(
        src_ref=x_ref,
        dst_ref=out_ref.at[ring, spot],
        send_sem=pair_sems.at[0],
        recv_sem=pair_sems.at[1],
        device_id=device(ring, partner),
        device_id_type=mesh_id,
    )
    swap.start()
    local.wait()
    finish([swap])

    pair_a = out_ref.at[ring, pl.ds(base, pair), :, :, first_lanes]
    rows_a = [remote(pair_a, device(ring, s), row_sems, (k,)) for k, s in enumerate(row_spots)]
    for copy in rows_a:
        copy.start()
    for t in range(rings // 2):
        last = t == rings // 2 - 1
        cw_spots = pl.ds(base, 1 if last else pair)
        ccw_spots = pl.ds(base + 1 if last else base, 1 if last else pair)
        cw = out_ref.at[(ring - t + rings) % rings, cw_spots, :, :, second_lanes]
        ccw = out_ref.at[(ring + t) % rings, ccw_spots, :, :, second_lanes]
        step = [
            remote(cw, device(ahead, spot), lane_sems, (0, t)),
            remote(ccw, device(behind, spot), lane_sems, (1, t)),
        ]
        for copy in step:
            copy.start()
        finish(step)
    finish(rows_a)

    half = slab // 2
    mid = rings // 2
    cross = [
        remote(out_ref.at[:, pl.ds(base, pair), :, :, second_lanes], device(ring, right), cross_sems, (0, 0)),
        remote(out_ref.at[:, pl.ds(base, pair), :, :, second_lanes], device(ring, left), cross_sems, (1, 0)),
    ]
    for copy in cross:
        copy.start()
    onward = None
    for t in range(rings // 2):
        last = t == rings // 2 - 1
        cw_spots = pl.ds(0, half if last else slab)
        ccw_spots = pl.ds(half if last else 0, half if last else slab)
        cw = out_ref.at[(ring - t + rings) % rings, cw_spots, :, :, first_lanes]
        ccw = out_ref.at[(ring + t) % rings, ccw_spots, :, :, first_lanes]
        step = [
            remote(cw, device(ahead, spot), ring_sems, (0, t)),
            remote(ccw, device(behind, spot), ring_sems, (1, t)),
        ]
        for copy in step:
            copy.start()
        if t == 0:
            source = tokens_ref[...].astype(jnp.float32)
            power = jnp.mean(source * source, axis=-1, keepdims=True)
            scaled = source * lax.rsqrt(power + eps) * gain_ref[...]
            normed_ref[...] = jnp.transpose(scaled.astype(jnp.bfloat16).astype(jnp.float32)).astype(
                normed_ref.dtype
            )
        finish(step)
        if t == 1:
            finish(cross)
            from_left = ((across + row - 1) % row) * pair
            from_right = ((across + 1) % row) * pair
            onward = [
                remote(
                    out_ref.at[pl.ds(0, mid), pl.ds(from_left, pair), :, :, second_lanes],
                    device(ring, right),
                    cross_sems,
                    (0, 1),
                ),
                remote(
                    out_ref.at[pl.ds(mid, mid), pl.ds(from_right, pair), :, :, second_lanes],
                    device(ring, left),
                    cross_sems,
                    (1, 1),
                ),
            ]
            for copy in onward:
                copy.start()
    finish(onward)


def gather_seq(block, tokens, gain, rings, slab):
    return pl.pallas_call(
        gather_kernel,
        out_shape=(
            jax.ShapeDtypeStruct((rings, slab) + block.shape, block.dtype),
            jax.ShapeDtypeStruct(tokens.shape[::-1], jnp.bfloat16),
        ),
        in_specs=[
            pl.BlockSpec(memory_space=pl.ANY),
            pl.BlockSpec(memory_space=pltpu.VMEM),
            pl.BlockSpec(memory_space=pltpu.VMEM),
        ],
        out_specs=(
            pl.BlockSpec(memory_space=pl.ANY),
            pl.BlockSpec(memory_space=pltpu.VMEM),
        ),
        scratch_shapes=[
            pltpu.SemaphoreType.DMA((2,)),
            pltpu.SemaphoreType.DMA((2, slab // 2 - 1)),
            pltpu.SemaphoreType.DMA((2, 2, rings // 2)),
            pltpu.SemaphoreType.DMA((2, 2, rings // 2)),
            pltpu.SemaphoreType.DMA((2, 2, 2)),
            pltpu.SemaphoreType.DMA(()),
        ],
        compiler_params=pltpu.CompilerParams(collective_id=0, has_side_effects=True),
    )(block, tokens, gain.reshape(1, -1))


def scatter_kernel(terms_ref, out_ref, mine, incoming, sums, send_sem, recv_sem, local_sems):
    chips = out_ref.shape[0]
    seq = lax.axis_index("seq")
    tp = lax.axis_index("tp")
    mesh_id = pl.DeviceIdType.MESH
    core = tp % 2
    here = tp // 2
    partner = (seq, tp + 1 - 2 * core)
    order = [(here + k) % chips for k in (2, 1, 3, 0)]

    def device(chip):
        return (seq, chip * 2 + core)

    barrier = pltpu.get_barrier_semaphore()
    for target in [partner] + [device(owner) for owner in order[:3]]:
        pl.semaphore_signal(barrier, inc=1, device_id=target, device_id_type=mesh_id)
    pl.semaphore_wait(barrier, 4)

    arrivals = []
    for k, owner in enumerate(order):
        keep = pltpu.make_async_copy(terms_ref.at[core, owner], mine.at[owner], local_sems.at[k])
        swap = pltpu.make_async_remote_copy(
            src_ref=terms_ref.at[1 - core, owner],
            dst_ref=incoming.at[owner],
            send_sem=send_sem.at[k],
            recv_sem=recv_sem.at[k],
            device_id=partner,
            device_id_type=mesh_id,
        )
        keep.start()
        swap.start()
        arrivals.append((keep, swap))

    outgoing = []
    for k, owner in enumerate(order):
        keep, swap = arrivals[k]
        keep.wait()
        swap.wait_send()
        swap.wait_recv()
        total = mine[owner].astype(jnp.float32) + incoming[owner].astype(jnp.float32)
        sums[owner] = total.astype(sums.dtype)
        if k < 3:
            copy = pltpu.make_async_remote_copy(
                src_ref=sums.at[owner],
                dst_ref=out_ref.at[here],
                send_sem=send_sem.at[4 + k],
                recv_sem=recv_sem.at[4 + k],
                device_id=device(owner),
                device_id_type=mesh_id,
            )
        else:
            copy = pltpu.make_async_copy(sums.at[owner], out_ref.at[here], local_sems.at[4])
        copy.start()
        outgoing.append(copy)
    for copy in outgoing[:3]:
        copy.wait_send()
        copy.wait_recv()
    outgoing[3].wait()


def scatter_chips(terms):
    block = terms.shape[1:]
    chips = block[0]
    return pl.pallas_call(
        scatter_kernel,
        out_shape=jax.ShapeDtypeStruct(block, jnp.bfloat16),
        in_specs=[pl.BlockSpec(memory_space=pl.ANY)],
        out_specs=pl.BlockSpec(memory_space=pl.ANY),
        scratch_shapes=[
            pltpu.VMEM(block, terms.dtype),
            pltpu.VMEM(block, terms.dtype),
            pltpu.VMEM(block, jnp.bfloat16),
            pltpu.SemaphoreType.DMA((7,)),
            pltpu.SemaphoreType.DMA((7,)),
            pltpu.SemaphoreType.DMA((5,)),
        ],
        compiler_params=pltpu.CompilerParams(collective_id=1, has_side_effects=True),
    )(terms)


def exchange_kernel(axis, offsets, x_ref, out_ref, send_sem, recv_sem, local_sem):
    size = lax.axis_size(axis)
    me = lax.axis_index(axis)
    seq = lax.axis_index("seq")
    tp = lax.axis_index("tp")
    mesh_id = pl.DeviceIdType.MESH

    def device(position):
        return (position, tp) if axis == "seq" else (seq, position)

    def slot(entry):
        return me if entry is None else entry

    peers = [lax.rem(me + offset + size, size) for offset, _ in offsets]
    barrier = pltpu.get_barrier_semaphore()
    for peer in peers:
        pl.semaphore_signal(barrier, inc=1, device_id=device(peer), device_id_type=mesh_id)
    pl.semaphore_wait(barrier, len(peers))

    own = offsets_own_slot(offsets, me)
    local = pltpu.make_async_copy(x_ref, out_ref.at[own], local_sem)
    local.start()
    copies = []
    for k, ((_, entry), peer) in enumerate(zip(offsets, peers)):
        copy = pltpu.make_async_remote_copy(
            src_ref=x_ref,
            dst_ref=out_ref.at[slot(entry)],
            send_sem=send_sem.at[k],
            recv_sem=recv_sem.at[k],
            device_id=device(peer),
            device_id_type=mesh_id,
        )
        copy.start()
        copies.append(copy)
    for copy in copies:
        copy.wait_send()
        copy.wait_recv()
    local.wait()


def offsets_own_slot(offsets, me):
    slots = [entry for _, entry in offsets]
    if None in slots:
        return me
    return len(offsets) // 2


def exchange(block, axis, offsets, slots, collective_id):
    count = len(offsets)
    return pl.pallas_call(
        functools.partial(exchange_kernel, axis, offsets),
        out_shape=jax.ShapeDtypeStruct((slots,) + block.shape, block.dtype),
        in_specs=[pl.BlockSpec(memory_space=pl.ANY)],
        out_specs=pl.BlockSpec(memory_space=pl.ANY),
        scratch_shapes=[
            pltpu.SemaphoreType.DMA((count,)),
            pltpu.SemaphoreType.DMA((count,)),
            pltpu.SemaphoreType.DMA(()),
        ],
        compiler_params=pltpu.CompilerParams(
            collective_id=collective_id, has_side_effects=True
        ),
    )(block)


def masked_scores(query, keys, query_seg, key_seg):
    scores = jnp.einsum(
        "qhd,khd->hqk", query, keys, preferred_element_type=jnp.float32
    ) * HEAD_DIM ** (-0.5)
    mask = (query_seg[:, None] == key_seg[None, :])[None]
    return (jnp.where(mask, scores, floor_score), mask)


def shards(tokens, norm_gain, qkv_weight, q_gain, k_gain, out_weight, layer_scale, segment_ids):
    count = tokens.shape[0]
    source = tokens.astype(jnp.float32)
    local_width = qkv_weight.shape[2]
    heads = local_width // HEAD_DIM
    stacked = jnp.concatenate([qkv_weight, jnp.transpose(out_weight)[:, None, :]], axis=1)
    rows, kinds, width = stacked.shape
    slab = 8
    gathered, normed_t = gather_seq(
        stacked, tokens, norm_gain, lax.axis_size("seq") // slab, slab
    )
    gathered = gathered.reshape(-1, kinds, width)
    joined = jnp.einsum(
        "dt,dch->tch",
        normed_t,
        gathered[:, :3],
        preferred_element_type=jnp.float32,
    )
    query = joined[:, 0]
    keys = joined[:, 1]
    values = joined[:, 2]
    parts = lax.axis_size("tp")
    squares = jnp.stack([jnp.sum(query * query, axis=-1), jnp.sum(keys * keys, axis=-1)])
    everyone = [(k, None) for k in range(1, parts)]
    query_sq, key_sq = jnp.sum(exchange(squares, "tp", everyone, parts, 2), axis=0)
    full_width = local_width * lax.axis_size("tp")
    query_normed = (query * lax.rsqrt(query_sq / full_width + eps)[:, None] * q_gain).astype(
        jnp.bfloat16
    )
    key_normed = (keys * lax.rsqrt(key_sq / full_width + eps)[:, None] * k_gain).astype(
        jnp.bfloat16
    )
    paired = jnp.stack([key_normed, values.astype(jnp.bfloat16)], axis=1)
    pieces = []
    for offset in (2, 1, 0, -1, -2):
        if offset == 0:
            pieces.append(paired)
        else:
            pieces.append(passed_along(paired, "seq", offset))
    widened = jnp.concatenate(pieces, axis=0)
    position = lax.axis_index("seq")
    outside = jnp.full((2 * count,), -1, jnp.int32)
    seg_pad = jnp.concatenate([outside, segment_ids, outside], axis=0)
    key_seg = lax.dynamic_slice_in_dim(seg_pad, position * count, 5 * count, 0)
    query_seg = lax.dynamic_slice_in_dim(segment_ids, position * count, count, 0)
    query_heads = query_normed.reshape(count, heads, HEAD_DIM)
    key_heads = widened[:, 0].reshape(5 * count, heads, HEAD_DIM)
    value_heads = widened[:, 1].reshape(5 * count, heads, HEAD_DIM)
    scores, mask = masked_scores(query_heads, key_heads, query_seg, key_seg)
    peak = jnp.max(scores, axis=-1, keepdims=True)
    weights = jnp.where(mask, jnp.exp(scores - peak), 0.0)
    total = jnp.sum(weights, axis=-1)
    probs = weights.astype(jnp.bfloat16)
    summed = jnp.einsum("hqk,khd->qhd", probs, value_heads, preferred_element_type=jnp.float32)
    context = (
        (summed / jnp.transpose(total)[:, :, None]).reshape(count, local_width).astype(jnp.bfloat16)
    )
    blank = jnp.zeros_like(context)
    widened_context = jnp.stack([blank, blank, blank, context], axis=1)
    chips = parts // 2
    by_owner = gathered.reshape(chips, 2, -1, *gathered.shape[1:])
    terms = jnp.einsum(
        "tkh,ycdkh->cydt", widened_context, by_owner, preferred_element_type=jnp.float32
    )
    projected = jnp.transpose(
        jnp.sum(scatter_chips(terms.astype(jnp.bfloat16)).astype(jnp.float32), axis=0)
    )
    share = layer_scale.shape[0]
    residual = lax.dynamic_slice_in_dim(source, lax.axis_index("tp") * share, share, 1)
    return (residual + layer_scale * projected).astype(jnp.bfloat16)


def solution(mesh):
    return jax.shard_map(
        shards,
        mesh=mesh,
        in_specs=(
            P("seq", None),
            P(),
            P("seq", None, "tp"),
            P("tp"),
            P("tp"),
            P("tp", "seq"),
            P("tp"),
            P(),
        ),
        out_specs=P("seq", "tp"),
        check_vma=False,
    )
```

```python
import functools

import jax
import jax.numpy as jnp
from jax import lax
from jax.sharding import PartitionSpec as P
from jax.experimental import pallas as pl
from jax.experimental.pallas import tpu as pltpu

HEAD_DIM = 128


eps = 1e-06
floor_score = -1e30


def passed_along(x, axis, by):
    size = lax.axis_size(axis)
    pairs = [(i, i + by) for i in range(size) if 0 <= i + by < size]
    return lax.ppermute(x, axis, pairs)


def gather_kernel(x_ref, out_ref, pair_sems, row_sems, lane_sems, ring_sems, cross_sems, local_sem):
    rings, slab = out_ref.shape[0], out_ref.shape[1]
    pair = 2
    row = slab // pair
    lanes = out_ref.shape[-1] // 2
    first_lanes, second_lanes = pl.ds(0, lanes), pl.ds(lanes, lanes)
    me = lax.axis_index("seq")
    tp = lax.axis_index("tp")
    mesh_id = pl.DeviceIdType.MESH
    ring = me // slab
    spot = me % slab
    low = spot % pair
    across = spot // pair
    base = spot - low

    def device(r, s):
        return (r * slab + s, tp)

    ahead = (ring + 1) % rings
    behind = (ring + rings - 1) % rings
    partner = base + 1 - low
    row_spots = [((across + k) % row) * pair + low for k in range(1, row)]
    right = ((across + 1) % row) * pair + low
    left = ((across + row - 1) % row) * pair + low

    barrier = pltpu.get_barrier_semaphore()
    targets = [device(ring, partner), device(ahead, spot), device(behind, spot)]
    targets += [device(ring, s) for s in row_spots]
    for target in targets:
        pl.semaphore_signal(barrier, inc=1, device_id=target, device_id_type=mesh_id)
    pl.semaphore_wait(barrier, len(targets))

    def remote(window, target, sems, index):
        return pltpu.make_async_remote_copy(
            src_ref=window,
            dst_ref=window,
            send_sem=sems.at[(0,) + index],
            recv_sem=sems.at[(1,) + index],
            device_id=target,
            device_id_type=mesh_id,
        )

    def finish(copies):
        for copy in copies:
            copy.wait_send()
            copy.wait_recv()

    local = pltpu.make_async_copy(x_ref, out_ref.at[ring, spot], local_sem)
    local.start()
    swap = pltpu.make_async_remote_copy(
        src_ref=x_ref,
        dst_ref=out_ref.at[ring, spot],
        send_sem=pair_sems.at[0],
        recv_sem=pair_sems.at[1],
        device_id=device(ring, partner),
        device_id_type=mesh_id,
    )
    swap.start()
    local.wait()
    finish([swap])

    pair_a = out_ref.at[ring, pl.ds(base, pair), :, :, first_lanes]
    rows_a = [remote(pair_a, device(ring, s), row_sems, (k,)) for k, s in enumerate(row_spots)]
    for copy in rows_a:
        copy.start()
    for t in range(rings // 2):
        last = t == rings // 2 - 1
        cw_spots = pl.ds(base, 1 if last else pair)
        ccw_spots = pl.ds(base + 1 if last else base, 1 if last else pair)
        cw = out_ref.at[(ring - t + rings) % rings, cw_spots, :, :, second_lanes]
        ccw = out_ref.at[(ring + t) % rings, ccw_spots, :, :, second_lanes]
        step = [
            remote(cw, device(ahead, spot), lane_sems, (0, t)),
            remote(ccw, device(behind, spot), lane_sems, (1, t)),
        ]
        for copy in step:
            copy.start()
        finish(step)
    finish(rows_a)

    half = slab // 2
    mid = rings // 2
    cross = [
        remote(out_ref.at[:, pl.ds(base, pair), :, :, second_lanes], device(ring, right), cross_sems, (0, 0)),
        remote(out_ref.at[:, pl.ds(base, pair), :, :, second_lanes], device(ring, left), cross_sems, (1, 0)),
    ]
    for copy in cross:
        copy.start()
    onward = None
    for t in range(rings // 2):
        last = t == rings // 2 - 1
        cw_spots = pl.ds(0, half if last else slab)
        ccw_spots = pl.ds(half if last else 0, half if last else slab)
        cw = out_ref.at[(ring - t + rings) % rings, cw_spots, :, :, first_lanes]
        ccw = out_ref.at[(ring + t) % rings, ccw_spots, :, :, first_lanes]
        step = [
            remote(cw, device(ahead, spot), ring_sems, (0, t)),
            remote(ccw, device(behind, spot), ring_sems, (1, t)),
        ]
        for copy in step:
            copy.start()
        finish(step)
        if t == 1:
            finish(cross)
            from_left = ((across + row - 1) % row) * pair
            from_right = ((across + 1) % row) * pair
            onward = [
                remote(
                    out_ref.at[pl.ds(0, mid), pl.ds(from_left, pair), :, :, second_lanes],
                    device(ring, right),
                    cross_sems,
                    (0, 1),
                ),
                remote(
                    out_ref.at[pl.ds(mid, mid), pl.ds(from_right, pair), :, :, second_lanes],
                    device(ring, left),
                    cross_sems,
                    (1, 1),
                ),
            ]
            for copy in onward:
                copy.start()
    finish(onward)


def gather_seq(block, rings, slab):
    return pl.pallas_call(
        gather_kernel,
        out_shape=jax.ShapeDtypeStruct((rings, slab) + block.shape, block.dtype),
        in_specs=[pl.BlockSpec(memory_space=pltpu.VMEM)],
        out_specs=pl.BlockSpec(memory_space=pl.ANY),
        scratch_shapes=[
            pltpu.SemaphoreType.DMA((2,)),
            pltpu.SemaphoreType.DMA((2, slab // 2 - 1)),
            pltpu.SemaphoreType.DMA((2, 2, rings // 2)),
            pltpu.SemaphoreType.DMA((2, 2, rings // 2)),
            pltpu.SemaphoreType.DMA((2, 2, 2)),
            pltpu.SemaphoreType.DMA(()),
        ],
        compiler_params=pltpu.CompilerParams(collective_id=0, has_side_effects=True),
    )(block)


def scatter_kernel(terms_ref, out_ref, mine, incoming, sums, send_sem, recv_sem, local_sems):
    chips = out_ref.shape[0]
    seq = lax.axis_index("seq")
    tp = lax.axis_index("tp")
    mesh_id = pl.DeviceIdType.MESH
    core = tp % 2
    here = tp // 2
    partner = (seq, tp + 1 - 2 * core)
    order = [(here + k) % chips for k in (2, 1, 3, 0)]

    def device(chip):
        return (seq, chip * 2 + core)

    barrier = pltpu.get_barrier_semaphore()
    for target in [partner] + [device(owner) for owner in order[:3]]:
        pl.semaphore_signal(barrier, inc=1, device_id=target, device_id_type=mesh_id)
    pl.semaphore_wait(barrier, 4)

    arrivals = []
    for k, owner in enumerate(order):
        keep = pltpu.make_async_copy(terms_ref.at[core, owner], mine.at[owner], local_sems.at[k])
        swap = pltpu.make_async_remote_copy(
            src_ref=terms_ref.at[1 - core, owner],
            dst_ref=incoming.at[owner],
            send_sem=send_sem.at[k],
            recv_sem=recv_sem.at[k],
            device_id=partner,
            device_id_type=mesh_id,
        )
        keep.start()
        swap.start()
        arrivals.append((keep, swap))

    outgoing = []
    for k, owner in enumerate(order):
        keep, swap = arrivals[k]
        keep.wait()
        swap.wait_send()
        swap.wait_recv()
        total = mine[owner].astype(jnp.float32) + incoming[owner].astype(jnp.float32)
        sums[owner] = total.astype(sums.dtype)
        if k < 3:
            copy = pltpu.make_async_remote_copy(
                src_ref=sums.at[owner],
                dst_ref=out_ref.at[here],
                send_sem=send_sem.at[4 + k],
                recv_sem=recv_sem.at[4 + k],
                device_id=device(owner),
                device_id_type=mesh_id,
            )
        else:
            copy = pltpu.make_async_copy(sums.at[owner], out_ref.at[here], local_sems.at[4])
        copy.start()
        outgoing.append(copy)
    for copy in outgoing[:3]:
        copy.wait_send()
        copy.wait_recv()
    outgoing[3].wait()


def scatter_chips(terms):
    block = terms.shape[1:]
    chips = block[0]
    return pl.pallas_call(
        scatter_kernel,
        out_shape=jax.ShapeDtypeStruct(block, jnp.bfloat16),
        in_specs=[pl.BlockSpec(memory_space=pl.ANY)],
        out_specs=pl.BlockSpec(memory_space=pl.ANY),
        scratch_shapes=[
            pltpu.VMEM(block, terms.dtype),
            pltpu.VMEM(block, terms.dtype),
            pltpu.VMEM(block, jnp.bfloat16),
            pltpu.SemaphoreType.DMA((7,)),
            pltpu.SemaphoreType.DMA((7,)),
            pltpu.SemaphoreType.DMA((5,)),
        ],
        compiler_params=pltpu.CompilerParams(collective_id=1, has_side_effects=True),
    )(terms)


def exchange_kernel(axis, offsets, x_ref, out_ref, send_sem, recv_sem, local_sem):
    size = lax.axis_size(axis)
    me = lax.axis_index(axis)
    seq = lax.axis_index("seq")
    tp = lax.axis_index("tp")
    mesh_id = pl.DeviceIdType.MESH

    def device(position):
        return (position, tp) if axis == "seq" else (seq, position)

    def slot(entry):
        return me if entry is None else entry

    peers = [lax.rem(me + offset + size, size) for offset, _ in offsets]
    barrier = pltpu.get_barrier_semaphore()
    for peer in peers:
        pl.semaphore_signal(barrier, inc=1, device_id=device(peer), device_id_type=mesh_id)
    pl.semaphore_wait(barrier, len(peers))

    own = offsets_own_slot(offsets, me)
    local = pltpu.make_async_copy(x_ref, out_ref.at[own], local_sem)
    local.start()
    copies = []
    for k, ((_, entry), peer) in enumerate(zip(offsets, peers)):
        copy = pltpu.make_async_remote_copy(
            src_ref=x_ref,
            dst_ref=out_ref.at[slot(entry)],
            send_sem=send_sem.at[k],
            recv_sem=recv_sem.at[k],
            device_id=device(peer),
            device_id_type=mesh_id,
        )
        copy.start()
        copies.append(copy)
    for copy in copies:
        copy.wait_send()
        copy.wait_recv()
    local.wait()


def offsets_own_slot(offsets, me):
    slots = [entry for _, entry in offsets]
    if None in slots:
        return me
    return len(offsets) // 2


def exchange(block, axis, offsets, slots, collective_id):
    count = len(offsets)
    return pl.pallas_call(
        functools.partial(exchange_kernel, axis, offsets),
        out_shape=jax.ShapeDtypeStruct((slots,) + block.shape, block.dtype),
        in_specs=[pl.BlockSpec(memory_space=pl.ANY)],
        out_specs=pl.BlockSpec(memory_space=pl.ANY),
        scratch_shapes=[
            pltpu.SemaphoreType.DMA((count,)),
            pltpu.SemaphoreType.DMA((count,)),
            pltpu.SemaphoreType.DMA(()),
        ],
        compiler_params=pltpu.CompilerParams(
            collective_id=collective_id, has_side_effects=True
        ),
    )(block)


def masked_scores(query, keys, query_seg, key_seg):
    scores = jnp.einsum(
        "qhd,khd->hqk", query, keys, preferred_element_type=jnp.float32
    ) * HEAD_DIM ** (-0.5)
    mask = (query_seg[:, None] == key_seg[None, :])[None]
    return (jnp.where(mask, scores, floor_score), mask)


def shards(tokens, norm_gain, qkv_weight, q_gain, k_gain, out_weight, layer_scale, segment_ids):
    count = tokens.shape[0]
    source = tokens.astype(jnp.float32)
    normed = (
        source * lax.rsqrt(jnp.mean(source * source, axis=-1, keepdims=True) + eps) * norm_gain
    ).astype(jnp.bfloat16)
    local_width = qkv_weight.shape[2]
    heads = local_width // HEAD_DIM
    stacked = jnp.concatenate([qkv_weight, jnp.transpose(out_weight)[:, None, :]], axis=1)
    rows, kinds, width = stacked.shape
    slab = 8
    gathered = gather_seq(stacked, lax.axis_size("seq") // slab, slab).reshape(-1, kinds, width)
    joined = jnp.einsum(
        "td,dch->tch",
        normed,
        gathered[:, :3],
        preferred_element_type=jnp.float32,
    )
    query = joined[:, 0]
    keys = joined[:, 1]
    values = joined[:, 2]
    parts = lax.axis_size("tp")
    squares = jnp.stack([jnp.sum(query * query, axis=-1), jnp.sum(keys * keys, axis=-1)])
    everyone = [(k, None) for k in range(1, parts)]
    query_sq, key_sq = jnp.sum(exchange(squares, "tp", everyone, parts, 2), axis=0)
    full_width = local_width * lax.axis_size("tp")
    query_normed = (query * lax.rsqrt(query_sq / full_width + eps)[:, None] * q_gain).astype(
        jnp.bfloat16
    )
    key_normed = (keys * lax.rsqrt(key_sq / full_width + eps)[:, None] * k_gain).astype(
        jnp.bfloat16
    )
    paired = jnp.stack([key_normed, values.astype(jnp.bfloat16)], axis=1)
    pieces = []
    for offset in (2, 1, 0, -1, -2):
        if offset == 0:
            pieces.append(paired)
        else:
            pieces.append(passed_along(paired, "seq", offset))
    widened = jnp.concatenate(pieces, axis=0)
    position = lax.axis_index("seq")
    outside = jnp.full((2 * count,), -1, jnp.int32)
    seg_pad = jnp.concatenate([outside, segment_ids, outside], axis=0)
    key_seg = lax.dynamic_slice_in_dim(seg_pad, position * count, 5 * count, 0)
    query_seg = lax.dynamic_slice_in_dim(segment_ids, position * count, count, 0)
    query_heads = query_normed.reshape(count, heads, HEAD_DIM)
    key_heads = widened[:, 0].reshape(5 * count, heads, HEAD_DIM)
    value_heads = widened[:, 1].reshape(5 * count, heads, HEAD_DIM)
    scores, mask = masked_scores(query_heads, key_heads, query_seg, key_seg)
    peak = jnp.max(scores, axis=-1, keepdims=True)
    weights = jnp.where(mask, jnp.exp(scores - peak), 0.0)
    total = jnp.sum(weights, axis=-1)
    probs = weights.astype(jnp.bfloat16)
    summed = jnp.einsum("hqk,khd->qhd", probs, value_heads, preferred_element_type=jnp.float32)
    context = (
        (summed / jnp.transpose(total)[:, :, None]).reshape(count, local_width).astype(jnp.bfloat16)
    )
    blank = jnp.zeros_like(context)
    widened_context = jnp.stack([blank, blank, blank, context], axis=1)
    chips = parts // 2
    by_owner = gathered.reshape(chips, 2, -1, *gathered.shape[1:])
    terms = jnp.einsum(
        "tkh,ycdkh->cydt", widened_context, by_owner, preferred_element_type=jnp.float32
    )
    projected = jnp.transpose(
        jnp.sum(scatter_chips(terms.astype(jnp.bfloat16)).astype(jnp.float32), axis=0)
    )
    share = layer_scale.shape[0]
    residual = lax.dynamic_slice_in_dim(source, lax.axis_index("tp") * share, share, 1)
    return (residual + layer_scale * projected).astype(jnp.bfloat16)


def solution(mesh):
    return jax.shard_map(
        shards,
        mesh=mesh,
        in_specs=(
            P("seq", None),
            P(),
            P("seq", None, "tp"),
            P("tp"),
            P("tp"),
            P("tp", "seq"),
            P("tp"),
            P(),
        ),
        out_specs=P("seq", "tp"),
        check_vma=False,
    )
```

```python
import functools

import jax
import jax.numpy as jnp
from jax import lax
from jax.sharding import PartitionSpec as P
from jax.experimental import pallas as pl
from jax.experimental.pallas import tpu as pltpu

HEAD_DIM = 128


eps = 1e-06
floor_score = -1e30


def passed_along(x, axis, by):
    size = lax.axis_size(axis)
    pairs = [(i, i + by) for i in range(size) if 0 <= i + by < size]
    return lax.ppermute(x, axis, pairs)


def gather_kernel(x_ref, out_ref, pair_sems, row_sems, lane_sems, ring_sems, cross_sems, local_sem):
    rings, slab = out_ref.shape[0], out_ref.shape[1]
    pair = 2
    row = slab // pair
    lanes = out_ref.shape[-1] // 2
    first_lanes, second_lanes = pl.ds(0, lanes), pl.ds(lanes, lanes)
    me = lax.axis_index("seq")
    tp = lax.axis_index("tp")
    mesh_id = pl.DeviceIdType.MESH
    ring = me // slab
    spot = me % slab
    low = spot % pair
    across = spot // pair
    base = spot - low

    def device(r, s):
        return (r * slab + s, tp)

    ahead = (ring + 1) % rings
    behind = (ring + rings - 1) % rings
    partner = base + 1 - low
    row_spots = [((across + k) % row) * pair + low for k in range(1, row)]
    right = ((across + 1) % row) * pair + low
    left = ((across + row - 1) % row) * pair + low

    barrier = pltpu.get_barrier_semaphore()
    targets = [device(ring, partner), device(ahead, spot), device(behind, spot)]
    targets += [device(ring, s) for s in row_spots]
    for target in targets:
        pl.semaphore_signal(barrier, inc=1, device_id=target, device_id_type=mesh_id)
    pl.semaphore_wait(barrier, len(targets))

    def remote(window, target, sems, index):
        return pltpu.make_async_remote_copy(
            src_ref=window,
            dst_ref=window,
            send_sem=sems.at[(0,) + index],
            recv_sem=sems.at[(1,) + index],
            device_id=target,
            device_id_type=mesh_id,
        )

    def finish(copies):
        for copy in copies:
            copy.wait_send()
            copy.wait_recv()

    local = pltpu.make_async_copy(x_ref, out_ref.at[ring, spot], local_sem)
    local.start()
    swap = pltpu.make_async_remote_copy(
        src_ref=x_ref,
        dst_ref=out_ref.at[ring, spot],
        send_sem=pair_sems.at[0],
        recv_sem=pair_sems.at[1],
        device_id=device(ring, partner),
        device_id_type=mesh_id,
    )
    swap.start()
    local.wait()
    finish([swap])

    pair_a = out_ref.at[ring, pl.ds(base, pair), :, :, first_lanes]
    rows_a = [remote(pair_a, device(ring, s), row_sems, (k,)) for k, s in enumerate(row_spots)]
    for copy in rows_a:
        copy.start()
    for t in range(rings // 2):
        last = t == rings // 2 - 1
        cw_spots = pl.ds(base, 1 if last else pair)
        ccw_spots = pl.ds(base + 1 if last else base, 1 if last else pair)
        cw = out_ref.at[(ring - t + rings) % rings, cw_spots, :, :, second_lanes]
        ccw = out_ref.at[(ring + t) % rings, ccw_spots, :, :, second_lanes]
        step = [
            remote(cw, device(ahead, spot), lane_sems, (0, t)),
            remote(ccw, device(behind, spot), lane_sems, (1, t)),
        ]
        for copy in step:
            copy.start()
        finish(step)
    finish(rows_a)

    half = slab // 2
    mid = rings // 2
    cross = [
        remote(out_ref.at[:, pl.ds(base, pair), :, :, second_lanes], device(ring, right), cross_sems, (0, 0)),
        remote(out_ref.at[:, pl.ds(base, pair), :, :, second_lanes], device(ring, left), cross_sems, (1, 0)),
    ]
    for copy in cross:
        copy.start()
    onward = None
    for t in range(rings // 2):
        last = t == rings // 2 - 1
        cw_spots = pl.ds(0, half if last else slab)
        ccw_spots = pl.ds(half if last else 0, half if last else slab)
        cw = out_ref.at[(ring - t + rings) % rings, cw_spots, :, :, first_lanes]
        ccw = out_ref.at[(ring + t) % rings, ccw_spots, :, :, first_lanes]
        step = [
            remote(cw, device(ahead, spot), ring_sems, (0, t)),
            remote(ccw, device(behind, spot), ring_sems, (1, t)),
        ]
        for copy in step:
            copy.start()
        finish(step)
        if t == 1:
            finish(cross)
            from_left = ((across + row - 1) % row) * pair
            from_right = ((across + 1) % row) * pair
            onward = [
                remote(
                    out_ref.at[pl.ds(0, mid), pl.ds(from_left, pair), :, :, second_lanes],
                    device(ring, right),
                    cross_sems,
                    (0, 1),
                ),
                remote(
                    out_ref.at[pl.ds(mid, mid), pl.ds(from_right, pair), :, :, second_lanes],
                    device(ring, left),
                    cross_sems,
                    (1, 1),
                ),
            ]
            for copy in onward:
                copy.start()
    finish(onward)


def gather_seq(block, rings, slab):
    return pl.pallas_call(
        gather_kernel,
        out_shape=jax.ShapeDtypeStruct((rings, slab) + block.shape, block.dtype),
        in_specs=[pl.BlockSpec(memory_space=pl.ANY)],
        out_specs=pl.BlockSpec(memory_space=pl.ANY),
        scratch_shapes=[
            pltpu.SemaphoreType.DMA((2,)),
            pltpu.SemaphoreType.DMA((2, slab // 2 - 1)),
            pltpu.SemaphoreType.DMA((2, 2, rings // 2)),
            pltpu.SemaphoreType.DMA((2, 2, rings // 2)),
            pltpu.SemaphoreType.DMA((2, 2, 2)),
            pltpu.SemaphoreType.DMA(()),
        ],
        compiler_params=pltpu.CompilerParams(collective_id=0, has_side_effects=True),
    )(block)


def scatter_kernel(terms_ref, out_ref, mine, incoming, sums, landed, send_sem, recv_sem, local_sems):
    chips = landed.shape[0]
    seq = lax.axis_index("seq")
    tp = lax.axis_index("tp")
    mesh_id = pl.DeviceIdType.MESH
    core = tp % 2
    here = tp // 2
    partner = (seq, tp + 1 - 2 * core)
    order = [(here + k) % chips for k in (2, 1, 3, 0)]

    def device(chip):
        return (seq, chip * 2 + core)

    barrier = pltpu.get_barrier_semaphore()
    for target in [partner] + [device(owner) for owner in order[:3]]:
        pl.semaphore_signal(barrier, inc=1, device_id=target, device_id_type=mesh_id)
    pl.semaphore_wait(barrier, 4)

    arrivals = []
    for k, owner in enumerate(order):
        keep = pltpu.make_async_copy(terms_ref.at[core, owner], mine.at[owner], local_sems.at[k])
        swap = pltpu.make_async_remote_copy(
            src_ref=terms_ref.at[1 - core, owner],
            dst_ref=incoming.at[owner],
            send_sem=send_sem.at[k],
            recv_sem=recv_sem.at[k],
            device_id=partner,
            device_id_type=mesh_id,
        )
        keep.start()
        swap.start()
        arrivals.append((keep, swap))

    outgoing = []
    for k, owner in enumerate(order):
        keep, swap = arrivals[k]
        keep.wait()
        swap.wait_send()
        swap.wait_recv()
        total = mine[owner].astype(jnp.float32) + incoming[owner].astype(jnp.float32)
        sums[owner] = total.astype(sums.dtype)
        if k < 3:
            copy = pltpu.make_async_remote_copy(
                src_ref=sums.at[owner],
                dst_ref=landed.at[here],
                send_sem=send_sem.at[4 + k],
                recv_sem=recv_sem.at[4 + k],
                device_id=device(owner),
                device_id_type=mesh_id,
            )
        else:
            copy = pltpu.make_async_copy(sums.at[owner], landed.at[here], local_sems.at[4])
        copy.start()
        outgoing.append(copy)
    for copy in outgoing[:3]:
        copy.wait_send()
        copy.wait_recv()
    outgoing[3].wait()
    total = landed[0].astype(jnp.float32)
    for chip in range(1, chips):
        total = total + landed[chip].astype(jnp.float32)
    out_ref[...] = total


def scatter_chips(terms):
    block = terms.shape[1:]
    chips = block[0]
    return pl.pallas_call(
        scatter_kernel,
        out_shape=jax.ShapeDtypeStruct(block[1:], jnp.float32),
        in_specs=[pl.BlockSpec(memory_space=pl.ANY)],
        out_specs=pl.BlockSpec(memory_space=pltpu.VMEM),
        scratch_shapes=[
            pltpu.VMEM(block, terms.dtype),
            pltpu.VMEM(block, terms.dtype),
            pltpu.VMEM(block, jnp.bfloat16),
            pltpu.VMEM(block, jnp.bfloat16),
            pltpu.SemaphoreType.DMA((7,)),
            pltpu.SemaphoreType.DMA((7,)),
            pltpu.SemaphoreType.DMA((5,)),
        ],
        compiler_params=pltpu.CompilerParams(collective_id=1, has_side_effects=True),
    )(terms)


def exchange_kernel(axis, offsets, x_ref, out_ref, send_sem, recv_sem, local_sem):
    size = lax.axis_size(axis)
    me = lax.axis_index(axis)
    seq = lax.axis_index("seq")
    tp = lax.axis_index("tp")
    mesh_id = pl.DeviceIdType.MESH

    def device(position):
        return (position, tp) if axis == "seq" else (seq, position)

    def slot(entry):
        return me if entry is None else entry

    peers = [lax.rem(me + offset + size, size) for offset, _ in offsets]
    barrier = pltpu.get_barrier_semaphore()
    for peer in peers:
        pl.semaphore_signal(barrier, inc=1, device_id=device(peer), device_id_type=mesh_id)
    pl.semaphore_wait(barrier, len(peers))

    own = offsets_own_slot(offsets, me)
    local = pltpu.make_async_copy(x_ref, out_ref.at[own], local_sem)
    local.start()
    copies = []
    for k, ((_, entry), peer) in enumerate(zip(offsets, peers)):
        copy = pltpu.make_async_remote_copy(
            src_ref=x_ref,
            dst_ref=out_ref.at[slot(entry)],
            send_sem=send_sem.at[k],
            recv_sem=recv_sem.at[k],
            device_id=device(peer),
            device_id_type=mesh_id,
        )
        copy.start()
        copies.append(copy)
    for copy in copies:
        copy.wait_send()
        copy.wait_recv()
    local.wait()


def offsets_own_slot(offsets, me):
    slots = [entry for _, entry in offsets]
    if None in slots:
        return me
    return len(offsets) // 2


def exchange(block, axis, offsets, slots, collective_id):
    count = len(offsets)
    return pl.pallas_call(
        functools.partial(exchange_kernel, axis, offsets),
        out_shape=jax.ShapeDtypeStruct((slots,) + block.shape, block.dtype),
        in_specs=[pl.BlockSpec(memory_space=pl.ANY)],
        out_specs=pl.BlockSpec(memory_space=pl.ANY),
        scratch_shapes=[
            pltpu.SemaphoreType.DMA((count,)),
            pltpu.SemaphoreType.DMA((count,)),
            pltpu.SemaphoreType.DMA(()),
        ],
        compiler_params=pltpu.CompilerParams(
            collective_id=collective_id, has_side_effects=True
        ),
    )(block)


def masked_scores(query, keys, query_seg, key_seg):
    scores = jnp.einsum(
        "qhd,khd->hqk", query, keys, preferred_element_type=jnp.float32
    ) * HEAD_DIM ** (-0.5)
    mask = (query_seg[:, None] == key_seg[None, :])[None]
    return (jnp.where(mask, scores, floor_score), mask)


def shards(tokens, norm_gain, qkv_weight, q_gain, k_gain, out_weight, layer_scale, segment_ids):
    count = tokens.shape[0]
    source = tokens.astype(jnp.float32)
    normed = (
        source * lax.rsqrt(jnp.mean(source * source, axis=-1, keepdims=True) + eps) * norm_gain
    ).astype(jnp.bfloat16)
    local_width = qkv_weight.shape[2]
    heads = local_width // HEAD_DIM
    stacked = jnp.concatenate([qkv_weight, jnp.transpose(out_weight)[:, None, :]], axis=1)
    rows, kinds, width = stacked.shape
    slab = 8
    gathered = gather_seq(stacked, lax.axis_size("seq") // slab, slab).reshape(-1, kinds, width)
    joined = jnp.einsum(
        "td,dch->tch",
        normed,
        gathered[:, :3],
        preferred_element_type=jnp.float32,
    )
    query = joined[:, 0]
    keys = joined[:, 1]
    values = joined[:, 2]
    parts = lax.axis_size("tp")
    squares = jnp.stack([jnp.sum(query * query, axis=-1), jnp.sum(keys * keys, axis=-1)])
    everyone = [(k, None) for k in range(1, parts)]
    query_sq, key_sq = jnp.sum(exchange(squares, "tp", everyone, parts, 2), axis=0)
    full_width = local_width * lax.axis_size("tp")
    query_normed = (query * lax.rsqrt(query_sq / full_width + eps)[:, None] * q_gain).astype(
        jnp.bfloat16
    )
    key_normed = (keys * lax.rsqrt(key_sq / full_width + eps)[:, None] * k_gain).astype(
        jnp.bfloat16
    )
    paired = jnp.stack([key_normed, values.astype(jnp.bfloat16)], axis=1)
    pieces = []
    for offset in (2, 1, 0, -1, -2):
        if offset == 0:
            pieces.append(paired)
        else:
            pieces.append(passed_along(paired, "seq", offset))
    widened = jnp.concatenate(pieces, axis=0)
    position = lax.axis_index("seq")
    outside = jnp.full((2 * count,), -1, jnp.int32)
    seg_pad = jnp.concatenate([outside, segment_ids, outside], axis=0)
    key_seg = lax.dynamic_slice_in_dim(seg_pad, position * count, 5 * count, 0)
    query_seg = lax.dynamic_slice_in_dim(segment_ids, position * count, count, 0)
    query_heads = query_normed.reshape(count, heads, HEAD_DIM)
    key_heads = widened[:, 0].reshape(5 * count, heads, HEAD_DIM)
    value_heads = widened[:, 1].reshape(5 * count, heads, HEAD_DIM)
    scores, mask = masked_scores(query_heads, key_heads, query_seg, key_seg)
    peak = jnp.max(scores, axis=-1, keepdims=True)
    weights = jnp.where(mask, jnp.exp(scores - peak), 0.0)
    total = jnp.sum(weights, axis=-1)
    probs = weights.astype(jnp.bfloat16)
    summed = jnp.einsum("hqk,khd->qhd", probs, value_heads, preferred_element_type=jnp.float32)
    context = (
        (summed / jnp.transpose(total)[:, :, None]).reshape(count, local_width).astype(jnp.bfloat16)
    )
    blank = jnp.zeros_like(context)
    widened_context = jnp.stack([blank, blank, blank, context], axis=1)
    chips = parts // 2
    by_owner = gathered.reshape(chips, 2, -1, *gathered.shape[1:])
    terms = jnp.einsum(
        "tkh,ycdkh->cydt", widened_context, by_owner, preferred_element_type=jnp.float32
    )
    projected = jnp.transpose(scatter_chips(terms.astype(jnp.bfloat16)))
    share = layer_scale.shape[0]
    residual = lax.dynamic_slice_in_dim(source, lax.axis_index("tp") * share, share, 1)
    return (residual + layer_scale * projected).astype(jnp.bfloat16)


def solution(mesh):
    return jax.shard_map(
        shards,
        mesh=mesh,
        in_specs=(
            P("seq", None),
            P(),
            P("seq", None, "tp"),
            P("tp"),
            P("tp"),
            P("tp", "seq"),
            P("tp"),
            P(),
        ),
        out_specs=P("seq", "tp"),
        check_vma=False,
    )
```

```python
import functools

import jax
import jax.numpy as jnp
from jax import lax
from jax.sharding import PartitionSpec as P
from jax.experimental import pallas as pl
from jax.experimental.pallas import tpu as pltpu

HEAD_DIM = 128


eps = 1e-06
floor_score = -1e30


def passed_along(x, axis, by):
    size = lax.axis_size(axis)
    pairs = [(i, i + by) for i in range(size) if 0 <= i + by < size]
    return lax.ppermute(x, axis, pairs)


def gather_kernel(x_ref, out_ref, pair_sems, row_sems, lane_sems, ring_sems, cross_sems, local_sem):
    rings, slab = out_ref.shape[0], out_ref.shape[1]
    pair = 2
    row = slab // pair
    lanes = out_ref.shape[-1] // 2
    first_lanes, second_lanes = pl.ds(0, lanes), pl.ds(lanes, lanes)
    me = lax.axis_index("seq")
    tp = lax.axis_index("tp")
    mesh_id = pl.DeviceIdType.MESH
    ring = me // slab
    spot = me % slab
    low = spot % pair
    across = spot // pair
    base = spot - low

    def device(r, s):
        return (r * slab + s, tp)

    ahead = (ring + 1) % rings
    behind = (ring + rings - 1) % rings
    partner = base + 1 - low
    row_spots = [((across + k) % row) * pair + low for k in range(1, row)]
    right = ((across + 1) % row) * pair + low
    left = ((across + row - 1) % row) * pair + low

    barrier = pltpu.get_barrier_semaphore()
    targets = [device(ring, partner), device(ahead, spot), device(behind, spot)]
    targets += [device(ring, s) for s in row_spots]
    for target in targets:
        pl.semaphore_signal(barrier, inc=1, device_id=target, device_id_type=mesh_id)
    pl.semaphore_wait(barrier, len(targets))

    def remote(window, target, sems, index):
        return pltpu.make_async_remote_copy(
            src_ref=window,
            dst_ref=window,
            send_sem=sems.at[(0,) + index],
            recv_sem=sems.at[(1,) + index],
            device_id=target,
            device_id_type=mesh_id,
        )

    def finish(copies):
        for copy in copies:
            copy.wait_send()
            copy.wait_recv()

    local = pltpu.make_async_copy(x_ref, out_ref.at[ring, spot], local_sem)
    local.start()
    swap = pltpu.make_async_remote_copy(
        src_ref=x_ref,
        dst_ref=out_ref.at[ring, spot],
        send_sem=pair_sems.at[0],
        recv_sem=pair_sems.at[1],
        device_id=device(ring, partner),
        device_id_type=mesh_id,
    )
    swap.start()
    local.wait()
    finish([swap])

    pair_a = out_ref.at[ring, pl.ds(base, pair), :, :, first_lanes]
    rows_a = [remote(pair_a, device(ring, s), row_sems, (k,)) for k, s in enumerate(row_spots)]
    for copy in rows_a:
        copy.start()
    for t in range(rings // 2):
        last = t == rings // 2 - 1
        cw_spots = pl.ds(base, 1 if last else pair)
        ccw_spots = pl.ds(base + 1 if last else base, 1 if last else pair)
        cw = out_ref.at[(ring - t + rings) % rings, cw_spots, :, :, second_lanes]
        ccw = out_ref.at[(ring + t) % rings, ccw_spots, :, :, second_lanes]
        step = [
            remote(cw, device(ahead, spot), lane_sems, (0, t)),
            remote(ccw, device(behind, spot), lane_sems, (1, t)),
        ]
        for copy in step:
            copy.start()
        finish(step)
    finish(rows_a)

    half = slab // 2
    mid = rings // 2
    cross = [
        remote(out_ref.at[:, pl.ds(base, pair), :, :, second_lanes], device(ring, right), cross_sems, (0, 0)),
        remote(out_ref.at[:, pl.ds(base, pair), :, :, second_lanes], device(ring, left), cross_sems, (1, 0)),
    ]
    for copy in cross:
        copy.start()
    onward = None
    for t in range(rings // 2):
        last = t == rings // 2 - 1
        cw_spots = pl.ds(0, half if last else slab)
        ccw_spots = pl.ds(half if last else 0, half if last else slab)
        cw = out_ref.at[(ring - t + rings) % rings, cw_spots, :, :, first_lanes]
        ccw = out_ref.at[(ring + t) % rings, ccw_spots, :, :, first_lanes]
        step = [
            remote(cw, device(ahead, spot), ring_sems, (0, t)),
            remote(ccw, device(behind, spot), ring_sems, (1, t)),
        ]
        for copy in step:
            copy.start()
        finish(step)
        if t == 1:
            finish(cross)
            from_left = ((across + row - 1) % row) * pair
            from_right = ((across + 1) % row) * pair
            onward = [
                remote(
                    out_ref.at[pl.ds(0, mid), pl.ds(from_left, pair), :, :, second_lanes],
                    device(ring, right),
                    cross_sems,
                    (0, 1),
                ),
                remote(
                    out_ref.at[pl.ds(mid, mid), pl.ds(from_right, pair), :, :, second_lanes],
                    device(ring, left),
                    cross_sems,
                    (1, 1),
                ),
            ]
            for copy in onward:
                copy.start()
    finish(onward)


def gather_seq(block, rings, slab):
    return pl.pallas_call(
        gather_kernel,
        out_shape=jax.ShapeDtypeStruct((rings, slab) + block.shape, block.dtype),
        in_specs=[pl.BlockSpec(memory_space=pl.ANY)],
        out_specs=pl.BlockSpec(memory_space=pl.ANY),
        scratch_shapes=[
            pltpu.SemaphoreType.DMA((2,)),
            pltpu.SemaphoreType.DMA((2, slab // 2 - 1)),
            pltpu.SemaphoreType.DMA((2, 2, rings // 2)),
            pltpu.SemaphoreType.DMA((2, 2, rings // 2)),
            pltpu.SemaphoreType.DMA((2, 2, 2)),
            pltpu.SemaphoreType.DMA(()),
        ],
        compiler_params=pltpu.CompilerParams(collective_id=0, has_side_effects=True),
    )(block)


def scatter_kernel(terms_ref, out_ref, mine, incoming, sums, landed, send_sem, recv_sem, local_sems):
    chips = landed.shape[0]
    seq = lax.axis_index("seq")
    tp = lax.axis_index("tp")
    mesh_id = pl.DeviceIdType.MESH
    core = tp % 2
    here = tp // 2
    partner = (seq, tp + 1 - 2 * core)
    order = [(here + k) % chips for k in (2, 1, 3, 0)]

    def device(chip):
        return (seq, chip * 2 + core)

    barrier = pltpu.get_barrier_semaphore()
    for target in [partner] + [device(owner) for owner in order[:3]]:
        pl.semaphore_signal(barrier, inc=1, device_id=target, device_id_type=mesh_id)
    pl.semaphore_wait(barrier, 4)

    arrivals = []
    for k, owner in enumerate(order):
        keep = pltpu.make_async_copy(terms_ref.at[core, owner], mine.at[owner], local_sems.at[k])
        swap = pltpu.make_async_remote_copy(
            src_ref=terms_ref.at[1 - core, owner],
            dst_ref=incoming.at[owner],
            send_sem=send_sem.at[k],
            recv_sem=recv_sem.at[k],
            device_id=partner,
            device_id_type=mesh_id,
        )
        keep.start()
        swap.start()
        arrivals.append((keep, swap))

    outgoing = []
    for k, owner in enumerate(order):
        keep, swap = arrivals[k]
        keep.wait()
        swap.wait_send()
        swap.wait_recv()
        total = mine[owner].astype(jnp.float32) + incoming[owner].astype(jnp.float32)
        sums[owner] = total.astype(sums.dtype)
        if k < 3:
            copy = pltpu.make_async_remote_copy(
                src_ref=sums.at[owner],
                dst_ref=landed.at[here],
                send_sem=send_sem.at[4 + k],
                recv_sem=recv_sem.at[4 + k],
                device_id=device(owner),
                device_id_type=mesh_id,
            )
        else:
            copy = pltpu.make_async_copy(sums.at[owner], landed.at[here], local_sems.at[4])
        copy.start()
        outgoing.append(copy)
    for copy in outgoing[:3]:
        copy.wait_send()
        copy.wait_recv()
    outgoing[3].wait()
    total = landed[0].astype(jnp.float32)
    for chip in range(1, chips):
        total = total + landed[chip].astype(jnp.float32)
    out_ref[...] = total


def scatter_chips(terms):
    block = terms.shape[1:]
    chips = block[0]
    return pl.pallas_call(
        scatter_kernel,
        out_shape=jax.ShapeDtypeStruct(block[1:], jnp.float32),
        in_specs=[pl.BlockSpec(memory_space=pl.ANY)],
        out_specs=pl.BlockSpec(memory_space=pltpu.VMEM),
        scratch_shapes=[
            pltpu.VMEM(block, terms.dtype),
            pltpu.VMEM(block, terms.dtype),
            pltpu.VMEM(block, jnp.bfloat16),
            pltpu.VMEM(block, jnp.bfloat16),
            pltpu.SemaphoreType.DMA((7,)),
            pltpu.SemaphoreType.DMA((7,)),
            pltpu.SemaphoreType.DMA((5,)),
        ],
        compiler_params=pltpu.CompilerParams(collective_id=1, has_side_effects=True),
    )(terms)


def exchange_kernel(axis, offsets, x_ref, total_ref, out_ref, send_sem, recv_sem, local_sem):
    size = lax.axis_size(axis)
    me = lax.axis_index(axis)
    seq = lax.axis_index("seq")
    tp = lax.axis_index("tp")
    mesh_id = pl.DeviceIdType.MESH

    def device(position):
        return (position, tp) if axis == "seq" else (seq, position)

    def slot(entry):
        return me if entry is None else entry

    peers = [lax.rem(me + offset + size, size) for offset, _ in offsets]
    barrier = pltpu.get_barrier_semaphore()
    for peer in peers:
        pl.semaphore_signal(barrier, inc=1, device_id=device(peer), device_id_type=mesh_id)
    pl.semaphore_wait(barrier, len(peers))

    own = offsets_own_slot(offsets, me)
    local = pltpu.make_async_copy(x_ref, out_ref.at[own], local_sem)
    local.start()
    copies = []
    for k, ((_, entry), peer) in enumerate(zip(offsets, peers)):
        copy = pltpu.make_async_remote_copy(
            src_ref=x_ref,
            dst_ref=out_ref.at[slot(entry)],
            send_sem=send_sem.at[k],
            recv_sem=recv_sem.at[k],
            device_id=device(peer),
            device_id_type=mesh_id,
        )
        copy.start()
        copies.append(copy)
    for copy in copies:
        copy.wait_send()
        copy.wait_recv()
    local.wait()
    total = out_ref[0]
    for slot in range(1, out_ref.shape[0]):
        total = total + out_ref[slot]
    total_ref[...] = total


def offsets_own_slot(offsets, me):
    slots = [entry for _, entry in offsets]
    if None in slots:
        return me
    return len(offsets) // 2


def exchange(block, axis, offsets, slots, collective_id):
    count = len(offsets)
    return pl.pallas_call(
        functools.partial(exchange_kernel, axis, offsets),
        out_shape=jax.ShapeDtypeStruct(block.shape, block.dtype),
        in_specs=[pl.BlockSpec(memory_space=pl.ANY)],
        out_specs=pl.BlockSpec(memory_space=pltpu.VMEM),
        scratch_shapes=[
            pltpu.VMEM((slots,) + block.shape, block.dtype),
            pltpu.SemaphoreType.DMA((count,)),
            pltpu.SemaphoreType.DMA((count,)),
            pltpu.SemaphoreType.DMA(()),
        ],
        compiler_params=pltpu.CompilerParams(
            collective_id=collective_id, has_side_effects=True
        ),
    )(block)


def masked_scores(query, keys, query_seg, key_seg):
    scores = jnp.einsum(
        "qhd,khd->hqk", query, keys, preferred_element_type=jnp.float32
    ) * HEAD_DIM ** (-0.5)
    mask = (query_seg[:, None] == key_seg[None, :])[None]
    return (jnp.where(mask, scores, floor_score), mask)


def shards(tokens, norm_gain, qkv_weight, q_gain, k_gain, out_weight, layer_scale, segment_ids):
    count = tokens.shape[0]
    source = tokens.astype(jnp.float32)
    normed = (
        source * lax.rsqrt(jnp.mean(source * source, axis=-1, keepdims=True) + eps) * norm_gain
    ).astype(jnp.bfloat16)
    local_width = qkv_weight.shape[2]
    heads = local_width // HEAD_DIM
    stacked = jnp.concatenate([qkv_weight, jnp.transpose(out_weight)[:, None, :]], axis=1)
    rows, kinds, width = stacked.shape
    slab = 8
    gathered = gather_seq(stacked, lax.axis_size("seq") // slab, slab).reshape(-1, kinds, width)
    joined = jnp.einsum(
        "td,dch->tch",
        normed,
        gathered[:, :3],
        preferred_element_type=jnp.float32,
    )
    query = joined[:, 0]
    keys = joined[:, 1]
    values = joined[:, 2]
    parts = lax.axis_size("tp")
    squares = jnp.stack([jnp.sum(query * query, axis=-1), jnp.sum(keys * keys, axis=-1)])
    everyone = [(k, None) for k in range(1, parts)]
    query_sq, key_sq = exchange(squares, "tp", everyone, parts, 2)
    full_width = local_width * lax.axis_size("tp")
    query_normed = (query * lax.rsqrt(query_sq / full_width + eps)[:, None] * q_gain).astype(
        jnp.bfloat16
    )
    key_normed = (keys * lax.rsqrt(key_sq / full_width + eps)[:, None] * k_gain).astype(
        jnp.bfloat16
    )
    paired = jnp.stack([key_normed, values.astype(jnp.bfloat16)], axis=1)
    pieces = []
    for offset in (2, 1, 0, -1, -2):
        if offset == 0:
            pieces.append(paired)
        else:
            pieces.append(passed_along(paired, "seq", offset))
    widened = jnp.concatenate(pieces, axis=0)
    position = lax.axis_index("seq")
    outside = jnp.full((2 * count,), -1, jnp.int32)
    seg_pad = jnp.concatenate([outside, segment_ids, outside], axis=0)
    key_seg = lax.dynamic_slice_in_dim(seg_pad, position * count, 5 * count, 0)
    query_seg = lax.dynamic_slice_in_dim(segment_ids, position * count, count, 0)
    query_heads = query_normed.reshape(count, heads, HEAD_DIM)
    key_heads = widened[:, 0].reshape(5 * count, heads, HEAD_DIM)
    value_heads = widened[:, 1].reshape(5 * count, heads, HEAD_DIM)
    scores, mask = masked_scores(query_heads, key_heads, query_seg, key_seg)
    peak = jnp.max(scores, axis=-1, keepdims=True)
    weights = jnp.where(mask, jnp.exp(scores - peak), 0.0)
    total = jnp.sum(weights, axis=-1)
    probs = weights.astype(jnp.bfloat16)
    summed = jnp.einsum("hqk,khd->qhd", probs, value_heads, preferred_element_type=jnp.float32)
    context = (
        (summed / jnp.transpose(total)[:, :, None]).reshape(count, local_width).astype(jnp.bfloat16)
    )
    blank = jnp.zeros_like(context)
    widened_context = jnp.stack([blank, blank, blank, context], axis=1)
    chips = parts // 2
    by_owner = gathered.reshape(chips, 2, -1, *gathered.shape[1:])
    terms = jnp.einsum(
        "tkh,ycdkh->cydt", widened_context, by_owner, preferred_element_type=jnp.float32
    )
    projected = jnp.transpose(scatter_chips(terms.astype(jnp.bfloat16)))
    share = layer_scale.shape[0]
    residual = lax.dynamic_slice_in_dim(source, lax.axis_index("tp") * share, share, 1)
    return (residual + layer_scale * projected).astype(jnp.bfloat16)


def solution(mesh):
    return jax.shard_map(
        shards,
        mesh=mesh,
        in_specs=(
            P("seq", None),
            P(),
            P("seq", None, "tp"),
            P("tp"),
            P("tp"),
            P("tp", "seq"),
            P("tp"),
            P(),
        ),
        out_specs=P("seq", "tp"),
        check_vma=False,
    )
```

```python
import functools

import jax
import jax.numpy as jnp
from jax import lax
from jax.sharding import PartitionSpec as P
from jax.experimental import pallas as pl
from jax.experimental.pallas import tpu as pltpu

HEAD_DIM = 128


eps = 1e-06
floor_score = -1e30


def passed_along(x, axis, by):
    size = lax.axis_size(axis)
    pairs = [(i, i + by) for i in range(size) if 0 <= i + by < size]
    return lax.ppermute(x, axis, pairs)


def gather_kernel(x_ref, out_ref, pair_sems, row_sems, lane_sems, ring_sems, cross_sems, local_sem):
    rings, slab = out_ref.shape[0], out_ref.shape[1]
    pair = 2
    row = slab // pair
    lanes = out_ref.shape[-1] // 2
    first_lanes, second_lanes = pl.ds(0, lanes), pl.ds(lanes, lanes)
    me = lax.axis_index("seq")
    tp = lax.axis_index("tp")
    mesh_id = pl.DeviceIdType.MESH
    ring = me // slab
    spot = me % slab
    low = spot % pair
    across = spot // pair
    base = spot - low

    def device(r, s):
        return (r * slab + s, tp)

    ahead = (ring + 1) % rings
    behind = (ring + rings - 1) % rings
    partner = base + 1 - low
    row_spots = [((across + k) % row) * pair + low for k in range(1, row)]
    right = ((across + 1) % row) * pair + low
    left = ((across + row - 1) % row) * pair + low

    barrier = pltpu.get_barrier_semaphore()
    targets = [device(ring, partner), device(ahead, spot), device(behind, spot)]
    targets += [device(ring, s) for s in row_spots]
    for target in targets:
        pl.semaphore_signal(barrier, inc=1, device_id=target, device_id_type=mesh_id)
    pl.semaphore_wait(barrier, len(targets))

    def remote(window, target, sems, index):
        return pltpu.make_async_remote_copy(
            src_ref=window,
            dst_ref=window,
            send_sem=sems.at[(0,) + index],
            recv_sem=sems.at[(1,) + index],
            device_id=target,
            device_id_type=mesh_id,
        )

    def finish(copies):
        for copy in copies:
            copy.wait_send()
            copy.wait_recv()

    local = pltpu.make_async_copy(x_ref, out_ref.at[ring, spot], local_sem)
    local.start()
    swap = pltpu.make_async_remote_copy(
        src_ref=x_ref,
        dst_ref=out_ref.at[ring, spot],
        send_sem=pair_sems.at[0],
        recv_sem=pair_sems.at[1],
        device_id=device(ring, partner),
        device_id_type=mesh_id,
    )
    swap.start()
    local.wait()
    finish([swap])

    pair_a = out_ref.at[ring, pl.ds(base, pair), :, :, first_lanes]
    rows_a = [remote(pair_a, device(ring, s), row_sems, (k,)) for k, s in enumerate(row_spots)]
    for copy in rows_a:
        copy.start()
    for t in range(rings // 2):
        last = t == rings // 2 - 1
        cw_spots = pl.ds(base, 1 if last else pair)
        ccw_spots = pl.ds(base + 1 if last else base, 1 if last else pair)
        cw = out_ref.at[(ring - t + rings) % rings, cw_spots, :, :, second_lanes]
        ccw = out_ref.at[(ring + t) % rings, ccw_spots, :, :, second_lanes]
        step = [
            remote(cw, device(ahead, spot), lane_sems, (0, t)),
            remote(ccw, device(behind, spot), lane_sems, (1, t)),
        ]
        for copy in step:
            copy.start()
        finish(step)
    finish(rows_a)

    half = slab // 2
    mid = rings // 2
    cross = [
        remote(out_ref.at[:, pl.ds(base, pair), :, :, second_lanes], device(ring, right), cross_sems, (0, 0)),
        remote(out_ref.at[:, pl.ds(base, pair), :, :, second_lanes], device(ring, left), cross_sems, (1, 0)),
    ]
    for copy in cross:
        copy.start()
    onward = None
    for t in range(rings // 2):
        last = t == rings // 2 - 1
        cw_spots = pl.ds(0, half if last else slab)
        ccw_spots = pl.ds(half if last else 0, half if last else slab)
        cw = out_ref.at[(ring - t + rings) % rings, cw_spots, :, :, first_lanes]
        ccw = out_ref.at[(ring + t) % rings, ccw_spots, :, :, first_lanes]
        step = [
            remote(cw, device(ahead, spot), ring_sems, (0, t)),
            remote(ccw, device(behind, spot), ring_sems, (1, t)),
        ]
        for copy in step:
            copy.start()
        finish(step)
        if t == 1:
            finish(cross)
            from_left = ((across + row - 1) % row) * pair
            from_right = ((across + 1) % row) * pair
            onward = [
                remote(
                    out_ref.at[pl.ds(0, mid), pl.ds(from_left, pair), :, :, second_lanes],
                    device(ring, right),
                    cross_sems,
                    (0, 1),
                ),
                remote(
                    out_ref.at[pl.ds(mid, mid), pl.ds(from_right, pair), :, :, second_lanes],
                    device(ring, left),
                    cross_sems,
                    (1, 1),
                ),
            ]
            for copy in onward:
                copy.start()
    finish(onward)


def gather_seq(block, rings, slab):
    return pl.pallas_call(
        gather_kernel,
        out_shape=jax.ShapeDtypeStruct((rings, slab) + block.shape, block.dtype),
        in_specs=[pl.BlockSpec(memory_space=pl.ANY)],
        out_specs=pl.BlockSpec(memory_space=pl.ANY),
        scratch_shapes=[
            pltpu.SemaphoreType.DMA((2,)),
            pltpu.SemaphoreType.DMA((2, slab // 2 - 1)),
            pltpu.SemaphoreType.DMA((2, 2, rings // 2)),
            pltpu.SemaphoreType.DMA((2, 2, rings // 2)),
            pltpu.SemaphoreType.DMA((2, 2, 2)),
            pltpu.SemaphoreType.DMA(()),
        ],
        compiler_params=pltpu.CompilerParams(collective_id=0, has_side_effects=True),
    )(block)


def scatter_kernel(terms_ref, out_ref, mine, incoming, sums, landed, send_sem, recv_sem, local_sems):
    chips = landed.shape[0]
    seq = lax.axis_index("seq")
    tp = lax.axis_index("tp")
    mesh_id = pl.DeviceIdType.MESH
    core = tp % 2
    here = tp // 2
    partner = (seq, tp + 1 - 2 * core)
    order = [(here + k) % chips for k in (2, 1, 3, 0)]

    def device(chip):
        return (seq, chip * 2 + core)

    barrier = pltpu.get_barrier_semaphore()
    for target in [partner] + [device(owner) for owner in order[:3]]:
        pl.semaphore_signal(barrier, inc=1, device_id=target, device_id_type=mesh_id)
    pl.semaphore_wait(barrier, 4)

    arrivals = []
    for k, owner in enumerate(order):
        keep = pltpu.make_async_copy(terms_ref.at[core, owner], mine.at[owner], local_sems.at[k])
        swap = pltpu.make_async_remote_copy(
            src_ref=terms_ref.at[1 - core, owner],
            dst_ref=incoming.at[owner],
            send_sem=send_sem.at[k],
            recv_sem=recv_sem.at[k],
            device_id=partner,
            device_id_type=mesh_id,
        )
        keep.start()
        swap.start()
        arrivals.append((keep, swap))

    outgoing = []
    for k, owner in enumerate(order):
        keep, swap = arrivals[k]
        keep.wait()
        swap.wait_send()
        swap.wait_recv()
        total = mine[owner].astype(jnp.float32) + incoming[owner].astype(jnp.float32)
        sums[owner] = total.astype(sums.dtype)
        if k < 3:
            copy = pltpu.make_async_remote_copy(
                src_ref=sums.at[owner],
                dst_ref=landed.at[here],
                send_sem=send_sem.at[4 + k],
                recv_sem=recv_sem.at[4 + k],
                device_id=device(owner),
                device_id_type=mesh_id,
            )
        else:
            continue
        copy.start()
        outgoing.append(copy)
    for copy in outgoing:
        copy.wait_send()
        copy.wait_recv()
    total = sums[here].astype(jnp.float32)
    for chip in range(1, chips):
        total = total + landed[(here + chip) % chips].astype(jnp.float32)
    out_ref[...] = total


def scatter_chips(terms):
    block = terms.shape[1:]
    chips = block[0]
    return pl.pallas_call(
        scatter_kernel,
        out_shape=jax.ShapeDtypeStruct(block[1:], jnp.float32),
        in_specs=[pl.BlockSpec(memory_space=pl.ANY)],
        out_specs=pl.BlockSpec(memory_space=pltpu.VMEM),
        scratch_shapes=[
            pltpu.VMEM(block, terms.dtype),
            pltpu.VMEM(block, terms.dtype),
            pltpu.VMEM(block, jnp.bfloat16),
            pltpu.VMEM(block, jnp.bfloat16),
            pltpu.SemaphoreType.DMA((7,)),
            pltpu.SemaphoreType.DMA((7,)),
            pltpu.SemaphoreType.DMA((4,)),
        ],
        compiler_params=pltpu.CompilerParams(collective_id=1, has_side_effects=True),
    )(terms)


def exchange_kernel(axis, offsets, x_ref, out_ref, send_sem, recv_sem, local_sem):
    size = lax.axis_size(axis)
    me = lax.axis_index(axis)
    seq = lax.axis_index("seq")
    tp = lax.axis_index("tp")
    mesh_id = pl.DeviceIdType.MESH

    def device(position):
        return (position, tp) if axis == "seq" else (seq, position)

    def slot(entry):
        return me if entry is None else entry

    peers = [lax.rem(me + offset + size, size) for offset, _ in offsets]
    barrier = pltpu.get_barrier_semaphore()
    for peer in peers:
        pl.semaphore_signal(barrier, inc=1, device_id=device(peer), device_id_type=mesh_id)
    pl.semaphore_wait(barrier, len(peers))

    own = offsets_own_slot(offsets, me)
    local = pltpu.make_async_copy(x_ref, out_ref.at[own], local_sem)
    local.start()
    copies = []
    for k, ((_, entry), peer) in enumerate(zip(offsets, peers)):
        copy = pltpu.make_async_remote_copy(
            src_ref=x_ref,
            dst_ref=out_ref.at[slot(entry)],
            send_sem=send_sem.at[k],
            recv_sem=recv_sem.at[k],
            device_id=device(peer),
            device_id_type=mesh_id,
        )
        copy.start()
        copies.append(copy)
    for copy in copies:
        copy.wait_send()
        copy.wait_recv()
    local.wait()


def offsets_own_slot(offsets, me):
    slots = [entry for _, entry in offsets]
    if None in slots:
        return me
    return len(offsets) // 2


def exchange(block, axis, offsets, slots, collective_id):
    count = len(offsets)
    return pl.pallas_call(
        functools.partial(exchange_kernel, axis, offsets),
        out_shape=jax.ShapeDtypeStruct((slots,) + block.shape, block.dtype),
        in_specs=[pl.BlockSpec(memory_space=pl.ANY)],
        out_specs=pl.BlockSpec(memory_space=pl.ANY),
        scratch_shapes=[
            pltpu.SemaphoreType.DMA((count,)),
            pltpu.SemaphoreType.DMA((count,)),
            pltpu.SemaphoreType.DMA(()),
        ],
        compiler_params=pltpu.CompilerParams(
            collective_id=collective_id, has_side_effects=True
        ),
    )(block)


def masked_scores(query, keys, query_seg, key_seg):
    scores = jnp.einsum(
        "qhd,khd->hqk", query, keys, preferred_element_type=jnp.float32
    ) * HEAD_DIM ** (-0.5)
    mask = (query_seg[:, None] == key_seg[None, :])[None]
    return (jnp.where(mask, scores, floor_score), mask)


def shards(tokens, norm_gain, qkv_weight, q_gain, k_gain, out_weight, layer_scale, segment_ids):
    count = tokens.shape[0]
    source = tokens.astype(jnp.float32)
    normed = (
        source * lax.rsqrt(jnp.mean(source * source, axis=-1, keepdims=True) + eps) * norm_gain
    ).astype(jnp.bfloat16)
    local_width = qkv_weight.shape[2]
    heads = local_width // HEAD_DIM
    stacked = jnp.concatenate([qkv_weight, jnp.transpose(out_weight)[:, None, :]], axis=1)
    rows, kinds, width = stacked.shape
    slab = 8
    gathered = gather_seq(stacked, lax.axis_size("seq") // slab, slab).reshape(-1, kinds, width)
    joined = jnp.einsum(
        "td,dch->tch",
        normed,
        gathered[:, :3],
        preferred_element_type=jnp.float32,
    )
    query = joined[:, 0]
    keys = joined[:, 1]
    values = joined[:, 2]
    parts = lax.axis_size("tp")
    squares = jnp.stack([jnp.sum(query * query, axis=-1), jnp.sum(keys * keys, axis=-1)])
    everyone = [(k, None) for k in range(1, parts)]
    query_sq, key_sq = jnp.sum(exchange(squares, "tp", everyone, parts, 2), axis=0)
    full_width = local_width * lax.axis_size("tp")
    query_normed = (query * lax.rsqrt(query_sq / full_width + eps)[:, None] * q_gain).astype(
        jnp.bfloat16
    )
    key_normed = (keys * lax.rsqrt(key_sq / full_width + eps)[:, None] * k_gain).astype(
        jnp.bfloat16
    )
    paired = jnp.stack([key_normed, values.astype(jnp.bfloat16)], axis=1)
    pieces = []
    for offset in (2, 1, 0, -1, -2):
        if offset == 0:
            pieces.append(paired)
        else:
            pieces.append(passed_along(paired, "seq", offset))
    widened = jnp.concatenate(pieces, axis=0)
    position = lax.axis_index("seq")
    outside = jnp.full((2 * count,), -1, jnp.int32)
    seg_pad = jnp.concatenate([outside, segment_ids, outside], axis=0)
    key_seg = lax.dynamic_slice_in_dim(seg_pad, position * count, 5 * count, 0)
    query_seg = lax.dynamic_slice_in_dim(segment_ids, position * count, count, 0)
    query_heads = query_normed.reshape(count, heads, HEAD_DIM)
    key_heads = widened[:, 0].reshape(5 * count, heads, HEAD_DIM)
    value_heads = widened[:, 1].reshape(5 * count, heads, HEAD_DIM)
    scores, mask = masked_scores(query_heads, key_heads, query_seg, key_seg)
    peak = jnp.max(scores, axis=-1, keepdims=True)
    weights = jnp.where(mask, jnp.exp(scores - peak), 0.0)
    total = jnp.sum(weights, axis=-1)
    probs = weights.astype(jnp.bfloat16)
    summed = jnp.einsum("hqk,khd->qhd", probs, value_heads, preferred_element_type=jnp.float32)
    context = (
        (summed / jnp.transpose(total)[:, :, None]).reshape(count, local_width).astype(jnp.bfloat16)
    )
    blank = jnp.zeros_like(context)
    widened_context = jnp.stack([blank, blank, blank, context], axis=1)
    chips = parts // 2
    by_owner = gathered.reshape(chips, 2, -1, *gathered.shape[1:])
    terms = jnp.einsum(
        "tkh,ycdkh->cydt", widened_context, by_owner, preferred_element_type=jnp.float32
    )
    projected = jnp.transpose(scatter_chips(terms.astype(jnp.bfloat16)))
    share = layer_scale.shape[0]
    residual = lax.dynamic_slice_in_dim(source, lax.axis_index("tp") * share, share, 1)
    return (residual + layer_scale * projected).astype(jnp.bfloat16)


def solution(mesh):
    return jax.shard_map(
        shards,
        mesh=mesh,
        in_specs=(
            P("seq", None),
            P(),
            P("seq", None, "tp"),
            P("tp"),
            P("tp"),
            P("tp", "seq"),
            P("tp"),
            P(),
        ),
        out_specs=P("seq", "tp"),
        check_vma=False,
    )
```

```python
import functools

import jax
import jax.numpy as jnp
from jax import lax
from jax.sharding import PartitionSpec as P
from jax.experimental import pallas as pl
from jax.experimental.pallas import tpu as pltpu

HEAD_DIM = 128


eps = 1e-06
floor_score = -1e30


def passed_along(x, axis, by):
    size = lax.axis_size(axis)
    pairs = [(i, i + by) for i in range(size) if 0 <= i + by < size]
    return lax.ppermute(x, axis, pairs)


def gather_kernel(x_ref, out_ref, pair_sems, row_sems, lane_sems, ring_sems, cross_sems, local_sem):
    rings, slab = out_ref.shape[0], out_ref.shape[1]
    pair = 2
    row = slab // pair
    lanes = out_ref.shape[-1] // 2
    first_lanes, second_lanes = pl.ds(0, lanes), pl.ds(lanes, lanes)
    me = lax.axis_index("seq")
    tp = lax.axis_index("tp")
    mesh_id = pl.DeviceIdType.MESH
    ring = me // slab
    spot = me % slab
    low = spot % pair
    across = spot // pair
    base = spot - low

    def device(r, s):
        return (r * slab + s, tp)

    ahead = (ring + 1) % rings
    behind = (ring + rings - 1) % rings
    partner = base + 1 - low
    row_spots = [((across + k) % row) * pair + low for k in range(1, row)]
    right = ((across + 1) % row) * pair + low
    left = ((across + row - 1) % row) * pair + low

    barrier = pltpu.get_barrier_semaphore()
    targets = [device(ring, partner), device(ahead, spot), device(behind, spot)]
    targets += [device(ring, s) for s in row_spots]
    for target in targets:
        pl.semaphore_signal(barrier, inc=1, device_id=target, device_id_type=mesh_id)
    pl.semaphore_wait(barrier, len(targets))

    def remote(window, target, sems, index):
        return pltpu.make_async_remote_copy(
            src_ref=window,
            dst_ref=window,
            send_sem=sems.at[(0,) + index],
            recv_sem=sems.at[(1,) + index],
            device_id=target,
            device_id_type=mesh_id,
        )

    def finish(copies):
        for copy in copies:
            copy.wait_send()
            copy.wait_recv()

    local = pltpu.make_async_copy(x_ref, out_ref.at[ring, spot], local_sem)
    local.start()
    swap = pltpu.make_async_remote_copy(
        src_ref=x_ref,
        dst_ref=out_ref.at[ring, spot],
        send_sem=pair_sems.at[0],
        recv_sem=pair_sems.at[1],
        device_id=device(ring, partner),
        device_id_type=mesh_id,
    )
    swap.start()
    local.wait()
    finish([swap])

    pair_a = out_ref.at[ring, pl.ds(base, pair), :, :, first_lanes]
    rows_a = [remote(pair_a, device(ring, s), row_sems, (k,)) for k, s in enumerate(row_spots)]
    for copy in rows_a:
        copy.start()
    for t in range(rings // 2):
        last = t == rings // 2 - 1
        cw_spots = pl.ds(base, 1 if last else pair)
        ccw_spots = pl.ds(base + 1 if last else base, 1 if last else pair)
        cw = out_ref.at[(ring - t + rings) % rings, cw_spots, :, :, second_lanes]
        ccw = out_ref.at[(ring + t) % rings, ccw_spots, :, :, second_lanes]
        step = [
            remote(cw, device(ahead, spot), lane_sems, (0, t)),
            remote(ccw, device(behind, spot), lane_sems, (1, t)),
        ]
        for copy in step:
            copy.start()
        finish(step)
    finish(rows_a)

    half = slab // 2
    mid = rings // 2
    cross = [
        remote(out_ref.at[:, pl.ds(base, pair), :, :, second_lanes], device(ring, right), cross_sems, (0, 0)),
        remote(out_ref.at[:, pl.ds(base, pair), :, :, second_lanes], device(ring, left), cross_sems, (1, 0)),
    ]
    for copy in cross:
        copy.start()
    onward = None
    for t in range(rings // 2):
        last = t == rings // 2 - 1
        cw_spots = pl.ds(0, half if last else slab)
        ccw_spots = pl.ds(half if last else 0, half if last else slab)
        cw = out_ref.at[(ring - t + rings) % rings, cw_spots, :, :, first_lanes]
        ccw = out_ref.at[(ring + t) % rings, ccw_spots, :, :, first_lanes]
        step = [
            remote(cw, device(ahead, spot), ring_sems, (0, t)),
            remote(ccw, device(behind, spot), ring_sems, (1, t)),
        ]
        for copy in step:
            copy.start()
        finish(step)
        if t == 1:
            finish(cross)
            from_left = ((across + row - 1) % row) * pair
            from_right = ((across + 1) % row) * pair
            onward = [
                remote(
                    out_ref.at[pl.ds(0, mid), pl.ds(from_left, pair), :, :, second_lanes],
                    device(ring, right),
                    cross_sems,
                    (0, 1),
                ),
                remote(
                    out_ref.at[pl.ds(mid, mid), pl.ds(from_right, pair), :, :, second_lanes],
                    device(ring, left),
                    cross_sems,
                    (1, 1),
                ),
            ]
            for copy in onward:
                copy.start()
    finish(onward)


def gather_seq(block, rings, slab):
    return pl.pallas_call(
        gather_kernel,
        out_shape=jax.ShapeDtypeStruct((rings, slab) + block.shape, block.dtype),
        in_specs=[pl.BlockSpec(memory_space=pl.ANY)],
        out_specs=pl.BlockSpec(memory_space=pl.ANY),
        scratch_shapes=[
            pltpu.SemaphoreType.DMA((2,)),
            pltpu.SemaphoreType.DMA((2, slab // 2 - 1)),
            pltpu.SemaphoreType.DMA((2, 2, rings // 2)),
            pltpu.SemaphoreType.DMA((2, 2, rings // 2)),
            pltpu.SemaphoreType.DMA((2, 2, 2)),
            pltpu.SemaphoreType.DMA(()),
        ],
        compiler_params=pltpu.CompilerParams(collective_id=0, has_side_effects=True),
    )(block)


def scatter_kernel(terms_ref, out_ref, mine, incoming, sums, landed, send_sem, recv_sem, local_sems):
    chips = landed.shape[0]
    seq = lax.axis_index("seq")
    tp = lax.axis_index("tp")
    mesh_id = pl.DeviceIdType.MESH
    core = tp % 2
    here = tp // 2
    partner = (seq, tp + 1 - 2 * core)
    order = [(here + k) % chips for k in (2, 1, 3, 0)]

    def device(chip):
        return (seq, chip * 2 + core)

    barrier = pltpu.get_barrier_semaphore()
    for target in [partner] + [device(owner) for owner in order[:3]]:
        pl.semaphore_signal(barrier, inc=1, device_id=target, device_id_type=mesh_id)
    pl.semaphore_wait(barrier, 4)

    arrivals = []
    for k, owner in enumerate(order):
        keep = pltpu.make_async_copy(terms_ref.at[core, owner], mine.at[owner], local_sems.at[k])
        swap = pltpu.make_async_remote_copy(
            src_ref=terms_ref.at[1 - core, owner],
            dst_ref=incoming.at[owner],
            send_sem=send_sem.at[k],
            recv_sem=recv_sem.at[k],
            device_id=partner,
            device_id_type=mesh_id,
        )
        keep.start()
        swap.start()
        arrivals.append((keep, swap))

    outgoing = []
    for k, owner in enumerate(order):
        keep, swap = arrivals[k]
        keep.wait()
        swap.wait_send()
        swap.wait_recv()
        total = mine[owner].astype(jnp.float32) + incoming[owner].astype(jnp.float32)
        sums[owner] = total.astype(sums.dtype)
        if k < 3:
            copy = pltpu.make_async_remote_copy(
                src_ref=sums.at[owner],
                dst_ref=landed.at[here],
                send_sem=send_sem.at[4 + k],
                recv_sem=recv_sem.at[4 + k],
                device_id=device(owner),
                device_id_type=mesh_id,
            )
        else:
            continue
        copy.start()
        outgoing.append(copy)
    for copy in outgoing:
        copy.wait_send()
        copy.wait_recv()
    total = sums[here].astype(jnp.float32)
    for chip in range(1, chips):
        total = total + landed[(here + chip) % chips].astype(jnp.float32)
    out_ref[...] = total


def scatter_chips(terms):
    block = terms.shape[1:]
    chips = block[0]
    return pl.pallas_call(
        scatter_kernel,
        out_shape=jax.ShapeDtypeStruct(block[1:], jnp.float32),
        in_specs=[pl.BlockSpec(memory_space=pl.ANY)],
        out_specs=pl.BlockSpec(memory_space=pltpu.VMEM),
        scratch_shapes=[
            pltpu.VMEM(block, terms.dtype),
            pltpu.VMEM(block, terms.dtype),
            pltpu.VMEM(block, jnp.bfloat16),
            pltpu.VMEM(block, jnp.bfloat16),
            pltpu.SemaphoreType.DMA((7,)),
            pltpu.SemaphoreType.DMA((7,)),
            pltpu.SemaphoreType.DMA((4,)),
        ],
        compiler_params=pltpu.CompilerParams(collective_id=1, has_side_effects=True),
    )(terms)


def exchange_kernel(axis, offsets, x_ref, out_ref, send_sem, recv_sem, local_sem):
    size = lax.axis_size(axis)
    me = lax.axis_index(axis)
    seq = lax.axis_index("seq")
    tp = lax.axis_index("tp")
    mesh_id = pl.DeviceIdType.MESH

    def device(position):
        return (position, tp) if axis == "seq" else (seq, position)

    def slot(entry):
        return me if entry is None else entry

    peers = [lax.rem(me + offset + size, size) for offset, _ in offsets]
    barrier = pltpu.get_barrier_semaphore()
    for peer in peers:
        pl.semaphore_signal(barrier, inc=1, device_id=device(peer), device_id_type=mesh_id)
    pl.semaphore_wait(barrier, len(peers))

    own = offsets_own_slot(offsets, me)
    local = pltpu.make_async_copy(x_ref, out_ref.at[own], local_sem)
    local.start()
    copies = []
    for k, ((_, entry), peer) in enumerate(zip(offsets, peers)):
        copy = pltpu.make_async_remote_copy(
            src_ref=x_ref,
            dst_ref=out_ref.at[slot(entry)],
            send_sem=send_sem.at[k],
            recv_sem=recv_sem.at[k],
            device_id=device(peer),
            device_id_type=mesh_id,
        )
        copy.start()
        copies.append(copy)
    for copy in copies:
        copy.wait_send()
        copy.wait_recv()
    local.wait()


def offsets_own_slot(offsets, me):
    slots = [entry for _, entry in offsets]
    if None in slots:
        return me
    return len(offsets) // 2


def exchange(block, axis, offsets, slots, collective_id):
    count = len(offsets)
    return pl.pallas_call(
        functools.partial(exchange_kernel, axis, offsets),
        out_shape=jax.ShapeDtypeStruct((slots,) + block.shape, block.dtype),
        in_specs=[pl.BlockSpec(memory_space=pltpu.VMEM)],
        out_specs=pl.BlockSpec(memory_space=pl.ANY),
        scratch_shapes=[
            pltpu.SemaphoreType.DMA((count,)),
            pltpu.SemaphoreType.DMA((count,)),
            pltpu.SemaphoreType.DMA(()),
        ],
        compiler_params=pltpu.CompilerParams(
            collective_id=collective_id, has_side_effects=True
        ),
    )(block)


def masked_scores(query, keys, query_seg, key_seg):
    scores = jnp.einsum(
        "qhd,khd->hqk", query, keys, preferred_element_type=jnp.float32
    ) * HEAD_DIM ** (-0.5)
    mask = (query_seg[:, None] == key_seg[None, :])[None]
    return (jnp.where(mask, scores, floor_score), mask)


def shards(tokens, norm_gain, qkv_weight, q_gain, k_gain, out_weight, layer_scale, segment_ids):
    count = tokens.shape[0]
    source = tokens.astype(jnp.float32)
    normed = (
        source * lax.rsqrt(jnp.mean(source * source, axis=-1, keepdims=True) + eps) * norm_gain
    ).astype(jnp.bfloat16)
    local_width = qkv_weight.shape[2]
    heads = local_width // HEAD_DIM
    stacked = jnp.concatenate([qkv_weight, jnp.transpose(out_weight)[:, None, :]], axis=1)
    rows, kinds, width = stacked.shape
    slab = 8
    gathered = gather_seq(stacked, lax.axis_size("seq") // slab, slab).reshape(-1, kinds, width)
    joined = jnp.einsum(
        "td,dch->tch",
        normed,
        gathered[:, :3],
        preferred_element_type=jnp.float32,
    )
    query = joined[:, 0]
    keys = joined[:, 1]
    values = joined[:, 2]
    parts = lax.axis_size("tp")
    squares = jnp.stack([jnp.sum(query * query, axis=-1), jnp.sum(keys * keys, axis=-1)])
    everyone = [(k, None) for k in range(1, parts)]
    query_sq, key_sq = jnp.sum(exchange(squares, "tp", everyone, parts, 2), axis=0)
    full_width = local_width * lax.axis_size("tp")
    query_normed = (query * lax.rsqrt(query_sq / full_width + eps)[:, None] * q_gain).astype(
        jnp.bfloat16
    )
    key_normed = (keys * lax.rsqrt(key_sq / full_width + eps)[:, None] * k_gain).astype(
        jnp.bfloat16
    )
    paired = jnp.stack([key_normed, values.astype(jnp.bfloat16)], axis=1)
    pieces = []
    for offset in (2, 1, 0, -1, -2):
        if offset == 0:
            pieces.append(paired)
        else:
            pieces.append(passed_along(paired, "seq", offset))
    widened = jnp.concatenate(pieces, axis=0)
    position = lax.axis_index("seq")
    outside = jnp.full((2 * count,), -1, jnp.int32)
    seg_pad = jnp.concatenate([outside, segment_ids, outside], axis=0)
    key_seg = lax.dynamic_slice_in_dim(seg_pad, position * count, 5 * count, 0)
    query_seg = lax.dynamic_slice_in_dim(segment_ids, position * count, count, 0)
    query_heads = query_normed.reshape(count, heads, HEAD_DIM)
    key_heads = widened[:, 0].reshape(5 * count, heads, HEAD_DIM)
    value_heads = widened[:, 1].reshape(5 * count, heads, HEAD_DIM)
    scores, mask = masked_scores(query_heads, key_heads, query_seg, key_seg)
    peak = jnp.max(scores, axis=-1, keepdims=True)
    weights = jnp.where(mask, jnp.exp(scores - peak), 0.0)
    total = jnp.sum(weights, axis=-1)
    probs = weights.astype(jnp.bfloat16)
    summed = jnp.einsum("hqk,khd->qhd", probs, value_heads, preferred_element_type=jnp.float32)
    context = (
        (summed / jnp.transpose(total)[:, :, None]).reshape(count, local_width).astype(jnp.bfloat16)
    )
    blank = jnp.zeros_like(context)
    widened_context = jnp.stack([blank, blank, blank, context], axis=1)
    chips = parts // 2
    by_owner = gathered.reshape(chips, 2, -1, *gathered.shape[1:])
    terms = jnp.einsum(
        "tkh,ycdkh->cydt", widened_context, by_owner, preferred_element_type=jnp.float32
    )
    projected = jnp.transpose(scatter_chips(terms.astype(jnp.bfloat16)))
    share = layer_scale.shape[0]
    residual = lax.dynamic_slice_in_dim(source, lax.axis_index("tp") * share, share, 1)
    return (residual + layer_scale * projected).astype(jnp.bfloat16)


def solution(mesh):
    return jax.shard_map(
        shards,
        mesh=mesh,
        in_specs=(
            P("seq", None),
            P(),
            P("seq", None, "tp"),
            P("tp"),
            P("tp"),
            P("tp", "seq"),
            P("tp"),
            P(),
        ),
        out_specs=P("seq", "tp"),
        check_vma=False,
    )
```
